256 devices in a mesh: ctx: 32 (over z_lo, x, y), tp: 8 (over z_hi, core).
Axes of the slice: x: 4, y: 4, z: 8 (z_hi: 4, z_lo: 2; z = z_hi * 2 + z_lo), core: 2. Of those that a mesh axis runs over, the one named last changes fastest.
Arguments:
- queries: bfloat16 [4096, 8192], P('ctx', 'tp'), may hold values from -8 to 8
- span_kv: bfloat16 [4096, 8, 2, 128], P('ctx', 'tp'), may hold values from -8 to 8
- cache_kv: bfloat16 [16384, 8, 2, 128], P('ctx', 'tp'), may hold values from -4 to 4
- out_weight: bfloat16 [8192, 8192], P('tp', 'ctx'), may hold values from -2.390625 to 2.390625
- offset: int32 [1], replicated, may hold values from 16384 to 24575
- lengths: int32 [64], replicated, may hold values from 64 to 256, as said below
Outputs:
- mixed: bfloat16 [4096, 8192], P('tp', 'ctx')
The draws below stay inside these ranges and needn't reach their ends.
Inputs may be any that keep to these rules, and one draw needn't show every extreme that they name: `lengths`: each at most 256; in every draw some match has all 256 of its positions valid.
All inputs are finite; a program needn't handle non-finite values.
Results may differ from the reference program's by a relative error of at most 0.025.
Values may be sent and summed in bfloat16 or wider, within the bound.
A program may use at most 64 MiB of HBM per device.

```python
import math
import jax
import jax.numpy as jnp
from jax import lax

D = 8192
HEADS = 64
KV_HEADS = 8
HEAD_DIM = 128
TOKENS = 4096
SLOT = 256
CACHE = 16384
MATCHES = 64


def draw_queries(key, part):
    base_key = jax.random.fold_in(key, 11)
    shape = (TOKENS, HEADS, HEAD_DIM)
    entries = jnp.clip(2.0 * jax.random.normal(base_key, shape, jnp.float32), -8.0, 8.0)
    return entries.reshape(TOKENS, HEADS * HEAD_DIM).astype(jnp.bfloat16)


def draw_span_kv(key, part):
    base_key = jax.random.fold_in(key, 12)
    shape = (TOKENS, KV_HEADS, 2, HEAD_DIM)
    entries = jnp.clip(jax.random.normal(base_key, shape, jnp.float32), -4.0, 4.0)
    return entries.astype(jnp.bfloat16)


def draw_lengths(key, part):
    counts = jax.random.randint(jax.random.fold_in(key, 21), (MATCHES,), SLOT // 4, SLOT + 1)
    filled = jax.random.randint(jax.random.fold_in(key, 22), (), 0, MATCHES)
    return jnp.where(jnp.arange(MATCHES) == filled, SLOT, counts).astype(jnp.int32)


def block_levels(rng, dims, split, least, high):
    def one(dim, shards_of):
        heights = jax.random.uniform(jax.random.fold_in(jax.random.fold_in(rng, 6), dim), (shards_of,), jnp.float32, least / len(split), high / len(split))
        return jnp.repeat(jnp.exp(heights), dims[dim] // shards_of).reshape((-1,) + (1,) * (len(dims) - dim - 1))

    level = one(*split[0])
    for cut in split[1:]:
        level = level * one(*cut)
    return level


def bell_draw(key, extent, spread, most, cuts=(), held_as=jnp.bfloat16):
    result = jax.random.normal(key, extent, jnp.float32) * spread
    if len(cuts) > 0:
        result = block_levels(key, extent, cuts, -0.22, 0.18) * result
    return jnp.clip(result, min=-most, max=most).astype(held_as)


def setup_inputs(seed: int = 0) -> dict:
    seeds = jax.random.split(jax.random.key(seed), 7)
    return {
        "queries": draw_queries(jax.random.fold_in(seeds[6], 71), 0),
        "span_kv": draw_span_kv(jax.random.fold_in(seeds[6], 71), 0),
        "cache_kv": bell_draw(seeds[2], (CACHE, KV_HEADS, 2, HEAD_DIM), 1.0, 4.0, ((0, 32), (1, 8))),
        "out_weight": bell_draw(seeds[3], (HEADS * HEAD_DIM, D), 0.4, 2.390625, ((0, 8), (1, 32))),
        "offset": jax.random.randint(seeds[4], (1,), CACHE, CACHE + 8192).astype(jnp.int32),
        "lengths": draw_lengths(jax.random.fold_in(seeds[6], 71), 0),
    }


lowest_score = -1e+30
rope_base = 500000.0

def rotate(values, positions):
    head_size = values.shape[-1]
    half_dim = head_size // 2
    frequency = jnp.exp(jnp.arange(half_dim, dtype=jnp.float32) * (-2.0 * math.log(rope_base) / head_size))
    angles = positions.astype(jnp.float32)[:, None] * frequency[None, :]
    cosine = jnp.cos(angles)[:, None, :]
    sine_part = jnp.sin(angles)[:, None, :]
    first_half = values[..., :half_dim]
    second_half = values[..., half_dim:]
    return jnp.concatenate([first_half * cosine - second_half * sine_part, second_half * cosine + first_half * sine_part], axis=-1)

def reference(queries, span_kv, cache_kv, out_weight, offset, lengths):
    group = HEADS // KV_HEADS
    scale = 1.0 / math.sqrt(HEAD_DIM)
    positions = offset[0] + jnp.arange(TOKENS, dtype=jnp.int32)
    rotated = rotate(queries.reshape(TOKENS, HEADS, HEAD_DIM).astype(jnp.float32), positions).astype(jnp.bfloat16)
    rotated = rotated.reshape(TOKENS, KV_HEADS, group, HEAD_DIM)
    span_keys = rotate(span_kv[:, :, 0, :].astype(jnp.float32), positions).astype(jnp.bfloat16)
    every_key = jnp.concatenate([cache_kv[:, :, 0, :], span_keys], axis=0).astype(jnp.float32)
    every_value = jnp.concatenate([cache_kv[:, :, 1, :], span_kv[:, :, 1, :]], axis=0).astype(jnp.float32)
    cache_index = jnp.arange(CACHE, dtype=jnp.int32)
    cache_valid = cache_index % SLOT < lengths[cache_index // SLOT]
    span_index = jnp.arange(TOKENS, dtype=jnp.int32)
    block = min(TOKENS, 256)
    block_count = TOKENS // block

    def one_block(index):
        row_block = index // KV_HEADS
        head = index % KV_HEADS
        query_part = lax.dynamic_slice_in_dim(rotated, (row_block * block).astype(jnp.int32), block, 0)
        query_part = lax.dynamic_index_in_dim(query_part, head, axis=1, keepdims=False).astype(jnp.float32)
        key_rows = lax.dynamic_index_in_dim(every_key, head, axis=1, keepdims=False)
        value_rows = lax.dynamic_index_in_dim(every_value, head, axis=1, keepdims=False)
        scores = jnp.einsum('tgd,nd->tgn', query_part, key_rows) * scale
        query_token = row_block * block + jnp.arange(block, dtype=jnp.int32)
        span_valid = span_index[None, :] <= query_token[:, None]
        valid = jnp.concatenate([jnp.broadcast_to(cache_valid[None, :], (block, CACHE)), span_valid], axis=1)[:, None, :]
        scores = jnp.where(valid, scores, lowest_score)
        row_max = lax.optimization_barrier(jnp.max(scores, axis=-1, keepdims=True))
        weights = jnp.where(valid, jnp.exp(scores - row_max), 0.0)
        denominators = lax.optimization_barrier(jnp.sum(weights, axis=-1))
        rounded = lax.optimization_barrier(weights.astype(jnp.bfloat16)).astype(jnp.float32)
        numerator = jnp.einsum('tgn,nd->tgd', rounded, value_rows)
        return (numerator / denominators[..., None]).astype(jnp.bfloat16)
    blocks = lax.map(one_block, jnp.arange(block_count * KV_HEADS, dtype=jnp.int32))
    attention = blocks.reshape(block_count, KV_HEADS, block, group, HEAD_DIM).transpose(0, 2, 1, 3, 4)
    attention = attention.reshape(TOKENS, HEADS * HEAD_DIM)
    return jnp.dot(attention, out_weight, preferred_element_type=jnp.float32).astype(jnp.bfloat16)
```

```python
import math

import jax
import jax.numpy as jnp
from jax import lax
from jax.experimental import pallas as pl
from jax.experimental.pallas import tpu as pltpu
from jax.sharding import PartitionSpec as P

SLOT = 256
HD = 128
TOK = 128
HEADS = 8
KV_ROWS = 640
CACHE_ROWS = 512
CH = 512
NCH = 10
A_ROWS = 256
lowest_score = -1e30
rope_base = 500000.0
MESH = pl.DeviceIdType.MESH
SCALE2 = math.log2(math.e) / math.sqrt(HD)


def rotate(values, positions):
    head_size = values.shape[-1]
    half_dim = head_size // 2
    frequency = jnp.exp(
        jnp.arange(half_dim, dtype=jnp.float32) * (-2.0 * math.log(rope_base) / head_size)
    )
    angles = positions.astype(jnp.float32)[:, None] * frequency[None, :]
    cosine = jnp.cos(angles)[:, None, :]
    sine_part = jnp.sin(angles)[:, None, :]
    first_half = values[..., :half_dim]
    second_half = values[..., half_dim:]
    return jnp.concatenate(
        [
            first_half * cosine - second_half * sine_part,
            second_half * cosine + first_half * sine_part,
        ],
        axis=-1,
    )


def coords():
    c = lax.axis_index("ctx")
    z = c // 16
    x = (c // 4) % 4
    y = c % 4
    return z, x, y


def ctx_of(z, x, y):
    return z * 16 + x * 4 + y


def entry_barrier(devices):
    barrier = pltpu.get_barrier_semaphore()
    for d in devices:
        pl.semaphore_signal(barrier, inc=1, device_id=d, device_id_type=MESH)
    pl.semaphore_wait(barrier, len(devices))


class Sender:
    def __init__(self, ssem, rsem):
        self.ssem, self.rsem, self.count, self.sent = ssem, rsem, 0, []

    def __call__(self, src, dst, device):
        n = self.count
        self.count += 1
        copy = pltpu.make_async_remote_copy(
            src_ref=src,
            dst_ref=dst,
            send_sem=self.ssem.at[n],
            recv_sem=self.rsem.at[n],
            device_id=device,
            device_id_type=MESH,
        )
        copy.start()
        self.sent.append(copy)
        return copy

    def finish(self):
        for copy in self.sent:
            copy.wait_send()


GATHER_COPIES = 22


def gather_kernel(q_ref, kv_ref, q4_ref, kvg_ref, ssem, rsem, lsem):
    z, x, y = coords()
    xp, xm, x2 = (x + 1) % 4, (x + 3) % 4, (x + 2) % 4
    yp, ym = (y + 1) % 4, (y + 3) % 4
    zo = 1 - z
    dz = {"ctx": ctx_of(zo, x, y)}
    dxp = {"ctx": ctx_of(z, xp, y)}
    dxm = {"ctx": ctx_of(z, xm, y)}
    dyp = {"ctx": ctx_of(z, x, yp)}
    dym = {"ctx": ctx_of(z, x, ym)}
    a = pl.ds(0, A_ROWS)
    a0 = pl.ds(0, A_ROWS // 2)
    a1 = pl.ds(A_ROWS // 2, A_ROWS // 2)
    nb = KV_ROWS - A_ROWS
    b = pl.ds(A_ROWS, nb)
    b0 = pl.ds(A_ROWS, nb // 2)
    b1 = pl.ds(A_ROWS + nb // 2, nb // 2)
    t0 = pl.ds(0, TOK // 2)
    t1 = pl.ds(TOK // 2, TOK // 2)

    own = z * 4 + x
    lq = pltpu.make_async_copy(q_ref, q4_ref.at[y], lsem.at[0])
    lkv = pltpu.make_async_copy(kv_ref, kvg_ref.at[own], lsem.at[1])
    entry_barrier([dz, dxp, dxm, dyp, dym])
    lq.start()
    lkv.start()
    send = Sender(ssem, rsem)

    def kv(j, rows):
        return kvg_ref.at[j, rows]

    def pass_on(j, rows, device):
        return send(kv(j, rows), kv(j, rows), device)

    b_z = send(kv_ref.at[b], kv(own, b), dz)
    b_xp = send(kv_ref.at[b], kv(own, b), dxp)
    b_xm = send(kv_ref.at[b], kv(own, b), dxm)
    q_yp = send(q_ref, q4_ref.at[y], dyp)
    q_ym = send(q_ref, q4_ref.at[y], dym)
    a_xp = send(kv_ref.at[a], kv(own, a), dxp)
    a_xm = send(kv_ref.at[a], kv(own, a), dxm)
    a_z = send(kv_ref.at[a], kv(own, a), dz)
    b_z.wait_recv()
    oz = zo * 4 + x
    bz_xp = pass_on(oz, b, dxp)
    bz_xm = pass_on(oz, b, dxm)
    b_xp.wait_recv()
    bf_xp = pass_on(z * 4 + xm, b0, dxp)
    b_xm.wait_recv()
    bf_xm = pass_on(z * 4 + xp, b1, dxm)
    q_yp.wait_recv()
    qf_yp = send(q4_ref.at[ym, t0], q4_ref.at[ym, t0], dyp)
    q_ym.wait_recv()
    qf_ym = send(q4_ref.at[yp, t1], q4_ref.at[yp, t1], dym)
    a_xp.wait_recv()
    af_xp = pass_on(z * 4 + xm, a0, dxp)
    az_m = pass_on(z * 4 + xm, a, dz)
    a_xm.wait_recv()
    af_xm = pass_on(z * 4 + xp, a1, dxm)
    az_p = pass_on(z * 4 + xp, a, dz)
    bz_xp.wait_recv()
    bzf_xp = pass_on(zo * 4 + xm, b0, dxp)
    bz_xm.wait_recv()
    bzf_xm = pass_on(zo * 4 + xp, b1, dxm)
    af_xp.wait_recv()
    az_2a = pass_on(z * 4 + x2, a0, dz)
    af_xm.wait_recv()
    az_2b = pass_on(z * 4 + x2, a1, dz)
    for copy in (a_z, bf_xp, bf_xm, qf_yp, qf_ym, az_m, az_p, bzf_xp, bzf_xm, az_2a, az_2b):
        copy.wait_recv()
    send.finish()
    lq.wait()
    lkv.wait()


def gather(q, kv):
    return pl.pallas_call(
        gather_kernel,
        name="gather_qkv",
        out_shape=(
            jax.ShapeDtypeStruct((4, TOK, HEADS * HD), jnp.bfloat16),
            jax.ShapeDtypeStruct((8, KV_ROWS, 2 * HD), jnp.bfloat16),
        ),
        in_specs=[pl.BlockSpec(memory_space=pltpu.VMEM)] * 2,
        out_specs=[pl.BlockSpec(memory_space=pltpu.VMEM)] * 2,
        scratch_shapes=[
            pltpu.SemaphoreType.DMA((GATHER_COPIES,)),
            pltpu.SemaphoreType.DMA((GATHER_COPIES,)),
            pltpu.SemaphoreType.DMA((2,)),
        ],
        compiler_params=pltpu.CompilerParams(
            collective_id=0, has_side_effects=True, vmem_limit_bytes=16 << 20
        ),
    )(q, kv)


ROWS = HEADS * TOK


def attention_kernel(
    lens_ref, q4_ref, kvg_ref, o4_ref, st_ref, qh, kbuf, vbuf, bias, sbuf, sown, mx, mc, lsum, acc
):
    z, x, y = coords()
    j0 = z * 4 + x
    for yy in range(4):
        for h in range(HEADS):
            qh[yy, h * TOK : (h + 1) * TOK, :] = q4_ref[yy, :, h * HD : (h + 1) * HD]

    pos = lax.broadcasted_iota(jnp.int32, bias.shape, 0) * CH + lax.broadcasted_iota(
        jnp.int32, bias.shape, 1
    )
    mask = jnp.full(bias.shape, lowest_score, jnp.float32)
    off = jnp.int32(0)
    for j in range(8):
        for s in range(2):
            n = lens_ref[2 * (4 * j + y) + s]
            o = pl.multiple_of(off, 16)
            rows = pl.ds(s * SLOT, SLOT)
            kbuf[pl.ds(o, SLOT), :] = kvg_ref[j, rows, 0:HD]
            vbuf[pl.ds(o, SLOT), :] = kvg_ref[j, rows, HD : 2 * HD]
            mask = jnp.where((pos >= off) & (pos < off + n), 0.0, mask)
            off = off + ((n + 15) // 16) * 16
    for j in range(7):
        o = pl.multiple_of(off + j * TOK, 16)
        rows = pl.ds(CACHE_ROWS, TOK)
        kbuf[pl.ds(o, TOK), :] = kvg_ref[j, rows, 0:HD]
        vbuf[pl.ds(o, TOK), :] = kvg_ref[j, rows, HD : 2 * HD]
    total = off + j0 * TOK
    mask = jnp.where((pos >= off) & (pos < total), 0.0, mask)
    bias[...] = mask
    o = pl.multiple_of(total, 16)
    kbuf[pl.ds(o, CH), :] = jnp.zeros((CH, HD), jnp.bfloat16)
    vbuf[pl.ds(o, CH), :] = jnp.zeros((CH, HD), jnp.bfloat16)
    chunks = (total + CH - 1) // CH

    row_tok = lax.broadcasted_iota(jnp.int32, (TOK, TOK), 0)
    key_tok = lax.broadcasted_iota(jnp.int32, (TOK, TOK), 1)

    def scores(rows, keys):
        return lax.dot_general(
            rows, keys, (((1,), (1,)), ((), ())), preferred_element_type=jnp.float32
        )

    def fold(op, values):
        out = values[:, 0:HD]
        for n in range(1, values.shape[1] // HD):
            out = op(out, values[:, n * HD : (n + 1) * HD])
        return out

    def first_own(i, slot):
        own_keys = kvg_ref[j0, CACHE_ROWS:KV_ROWS, 0:HD]
        s = scores(qh[i], own_keys)
        ok = (key_tok + (y - i) * TOK) <= row_tok
        own_bias = jnp.where(ok, 0.0, lowest_score)
        s = s + jnp.concatenate([own_bias] * HEADS, axis=0)
        sown[slot] = s
        mx[...] = s

    def first_step(kc, i, slot):
        k0 = pl.multiple_of(kc * CH, CH)
        s = scores(qh[i], kbuf[pl.ds(k0, CH), :]) + bias[pl.ds(kc, 1), :]
        sbuf[slot, kc] = s
        mx[...] = jnp.maximum(mx[...], fold(jnp.maximum, s))

    def first_end():
        m = jnp.max(mx[...], axis=1, keepdims=True)
        mc[...] = jnp.broadcast_to(m * SCALE2, (ROWS, HD))

    def second_own(slot):
        own_values = kvg_ref[j0, CACHE_ROWS:KV_ROWS, HD : 2 * HD]
        p = jnp.exp2(sown[slot] * SCALE2 - mc[...])
        lsum[...] = p
        acc[...] = jnp.dot(p.astype(jnp.bfloat16), own_values, preferred_element_type=jnp.float32)

    def second_step(kc, slot):
        k0 = pl.multiple_of(kc * CH, CH)
        m = mc[...]
        p = jnp.exp2(sbuf[slot, kc] * SCALE2 - jnp.concatenate([m] * (CH // HD), axis=1))
        lsum[...] += fold(jnp.add, p)
        acc[...] += jnp.dot(
            p.astype(jnp.bfloat16), vbuf[pl.ds(k0, CH), :], preferred_element_type=jnp.float32
        )

    def second_end(i):
        l = jnp.broadcast_to(jnp.sum(lsum[...], axis=1, keepdims=True), (ROWS, HD))
        o = acc[...] / l
        lse = mc[...] + jnp.log2(l)
        lane = lax.broadcasted_iota(jnp.int32, (TOK, HD), 1)
        packed = jnp.zeros((TOK, HD), jnp.float32)
        for h in range(HEADS):
            rows = slice(h * TOK, (h + 1) * TOK)
            o4_ref[i, :, h * HD : (h + 1) * HD] = o[rows].astype(jnp.bfloat16)
            packed = jnp.where(lane == h, lse[rows], packed)
        st_ref[i] = packed.T[0:HEADS]

    first_own(0, 0)

    @pl.loop(0, chunks)
    def _(kc):
        first_step(kc, 0, 0)

    first_end()

    for i in range(4):
        slot = i % 2
        second_own(slot)
        if i < 3:
            first_own(i + 1, 1 - slot)

        @pl.loop(0, chunks)
        def _(kc, i=i, slot=slot):
            if i < 3:
                first_step(kc, i + 1, 1 - slot)
            second_step(kc, slot)

        second_end(i)
        if i < 3:
            first_end()


def attention(lengths, q4, kvg):
    rows = NCH * CH + CH
    return pl.pallas_call(
        attention_kernel,
        name="attention",
        out_shape=(
            jax.ShapeDtypeStruct((4, TOK, HEADS * HD), jnp.bfloat16),
            jax.ShapeDtypeStruct((4, HEADS, TOK), jnp.float32),
        ),
        in_specs=[
            pl.BlockSpec(memory_space=pltpu.SMEM),
            pl.BlockSpec(memory_space=pltpu.VMEM),
            pl.BlockSpec(memory_space=pltpu.VMEM),
        ],
        out_specs=[pl.BlockSpec(memory_space=pltpu.VMEM)] * 2,
        scratch_shapes=[
            pltpu.VMEM((4, ROWS, HD), jnp.bfloat16),
            pltpu.VMEM((rows, HD), jnp.bfloat16),
            pltpu.VMEM((rows, HD), jnp.bfloat16),
            pltpu.VMEM((16, CH), jnp.float32),
            pltpu.VMEM((2, NCH, ROWS, CH), jnp.float32),
            pltpu.VMEM((2, ROWS, HD), jnp.float32),
            pltpu.VMEM((ROWS, HD), jnp.float32),
            pltpu.VMEM((ROWS, HD), jnp.float32),
            pltpu.VMEM((ROWS, HD), jnp.float32),
            pltpu.VMEM((ROWS, HD), jnp.float32),
        ],
        compiler_params=pltpu.CompilerParams(vmem_limit_bytes=62 << 20),
    )(lengths, q4, kvg)


COMBINE_COPIES = 8
PLANE_COPIES = 40


def combine_kernel(
    o4_ref, st_ref, w_ref, att_ref, wz_ref, part, stat, fwd, mine, ssem, rsem, ssem2, rsem2, lsem
):
    z, x, y = coords()
    xp, xm, x2 = (x + 1) % 4, (x + 3) % 4, (x + 2) % 4
    yp, ym, y2 = (y + 1) % 4, (y + 3) % 4, (y + 2) % 4
    dz = {"ctx": ctx_of(1 - z, x, y)}
    dxp = {"ctx": ctx_of(z, xp, y)}
    dxm = {"ctx": ctx_of(z, xm, y)}
    dyp = {"ctx": ctx_of(z, x, yp)}
    dym = {"ctx": ctx_of(z, x, ym)}
    dy2 = {"ctx": ctx_of(z, x, y2)}
    half = TOK // 2
    t0 = pl.ds(0, half)
    t1 = pl.ds(half, half)
    entry_barrier([dz, dxp, dxm, dyp, dym, dy2])
    send = Sender(ssem, rsem)
    far_p = send(o4_ref.at[y2, t0], fwd.at[0], dyp)
    far_m = send(o4_ref.at[y2, t1], fwd.at[1], dym)
    to_p = send(o4_ref.at[yp], part.at[2], dyp)
    to_m = send(o4_ref.at[ym], part.at[0], dym)
    st_p = send(st_ref.at[yp], stat.at[2], dyp)
    st_m = send(st_ref.at[ym], stat.at[0], dym)
    st_2 = send(st_ref.at[y2], stat.at[1], dy2)
    swap = send(w_ref, wz_ref, dz)
    send2 = Sender(ssem2, rsem2)
    far_p.wait_recv()
    fw_p = send2(fwd.at[0], part.at[1, t0], dyp)
    far_m.wait_recv()
    fw_m = send2(fwd.at[1], part.at[1, t1], dym)
    for copy in (st_p, st_m, st_2):
        copy.wait_recv()
    s_own = st_ref[y]
    s_p, s_m, s_2 = stat[0], stat[2], stat[1]
    top = jnp.maximum(jnp.maximum(s_own, s_p), jnp.maximum(s_m, s_2))
    e_own = jnp.exp2(s_own - top)
    e_p = jnp.exp2(s_p - top)
    e_m = jnp.exp2(s_m - top)
    e_2 = jnp.exp2(s_2 - top)
    norm = 1.0 / (e_own + e_p + e_m + e_2)
    table = jnp.concatenate(
        [e_own * norm, e_p * norm, e_m * norm, e_2 * norm, jnp.zeros((96, TOK), jnp.float32)],
        axis=0,
    ).T
    for copy in (to_p, to_m, fw_p, fw_m):
        copy.wait_recv()
    for h in range(HEADS):
        lanes = slice(h * HD, (h + 1) * HD)
        out = o4_ref[y, :, lanes].astype(jnp.float32) * table[:, h : h + 1]
        out += part[0, :, lanes].astype(jnp.float32) * table[:, 8 + h : 9 + h]
        out += part[2, :, lanes].astype(jnp.float32) * table[:, 16 + h : 17 + h]
        out += part[1, :, lanes].astype(jnp.float32) * table[:, 24 + h : 25 + h]
        mine[:, lanes] = out.astype(jnp.bfloat16)

    own = x * 4 + y
    local = pltpu.make_async_copy(mine, att_ref.at[own], lsem.at[0])
    local.start()

    quarter = half // 2
    a, a0, a1 = t0, pl.ds(0, quarter), pl.ds(quarter, quarter)
    b, b0, b1 = t1, pl.ds(half, quarter), pl.ds(half + quarter, quarter)

    def pass_on(slot, rows, device):
        return send2(att_ref.at[slot, rows], att_ref.at[slot, rows], device)

    ax_p = send2(mine.at[a], att_ref.at[own, a], dxp)
    ax_m = send2(mine.at[a], att_ref.at[own, a], dxm)
    by_p = send2(mine.at[b], att_ref.at[own, b], dyp)
    by_m = send2(mine.at[b], att_ref.at[own, b], dym)
    ay = {}
    bx = {}
    ay[0] = (
        send2(mine.at[a], att_ref.at[own, a], dyp),
        send2(mine.at[a], att_ref.at[own, a], dym),
    )
    bx[0] = (
        send2(mine.at[b], att_ref.at[own, b], dxp),
        send2(mine.at[b], att_ref.at[own, b], dxm),
    )
    ax_p.wait_recv()
    axf_p = pass_on(xm * 4 + y, a0, dxp)
    by_p.wait_recv()
    byf_p = pass_on(x * 4 + ym, b0, dyp)
    ax_m.wait_recv()
    axf_m = pass_on(xp * 4 + y, a1, dxm)
    by_m.wait_recv()
    byf_m = pass_on(x * 4 + yp, b1, dym)
    ay[3] = (pass_on(xm * 4 + y, a, dyp), pass_on(xm * 4 + y, a, dym))
    bx[3] = (pass_on(x * 4 + ym, b, dxp), pass_on(x * 4 + ym, b, dxm))
    ay[1] = (pass_on(xp * 4 + y, a, dyp), pass_on(xp * 4 + y, a, dym))
    bx[1] = (pass_on(x * 4 + yp, b, dxp), pass_on(x * 4 + yp, b, dxm))
    last = []

    def relay(k):
        p, m = ay[k]
        xs = (x + k) % 4
        p.wait_recv()
        last.append(pass_on(xs * 4 + ym, a0, dyp))
        m.wait_recv()
        last.append(pass_on(xs * 4 + yp, a1, dym))
        p, m = bx[k]
        ys = (y + k) % 4
        p.wait_recv()
        last.append(pass_on(xm * 4 + ys, b0, dxp))
        m.wait_recv()
        last.append(pass_on(xp * 4 + ys, b1, dxm))

    relay(0)
    axf_p.wait_recv()
    axf_m.wait_recv()
    byf_p.wait_recv()
    byf_m.wait_recv()
    ay[2] = (pass_on(x2 * 4 + y, a, dyp), pass_on(x2 * 4 + y, a, dym))
    bx[2] = (pass_on(x * 4 + y2, b, dxp), pass_on(x * 4 + y2, b, dxm))
    relay(3)
    relay(1)
    relay(2)
    for copy in last:
        copy.wait_recv()
    swap.wait_recv()
    send.finish()
    send2.finish()
    local.wait()


def combine(o4, st, w):
    return pl.pallas_call(
        combine_kernel,
        name="combine",
        out_shape=(
            jax.ShapeDtypeStruct((16, TOK, HEADS * HD), jnp.bfloat16),
            jax.ShapeDtypeStruct(w.shape, jnp.bfloat16),
        ),
        in_specs=[pl.BlockSpec(memory_space=pltpu.VMEM)] * 3,
        out_specs=[pl.BlockSpec(memory_space=pltpu.VMEM)] * 2,
        scratch_shapes=[
            pltpu.VMEM((3, TOK, HEADS * HD), jnp.bfloat16),
            pltpu.VMEM((3, HEADS, TOK), jnp.float32),
            pltpu.VMEM((2, TOK // 2, HEADS * HD), jnp.bfloat16),
            pltpu.VMEM((TOK, HEADS * HD), jnp.bfloat16),
            pltpu.SemaphoreType.DMA((COMBINE_COPIES,)),
            pltpu.SemaphoreType.DMA((COMBINE_COPIES,)),
            pltpu.SemaphoreType.DMA((PLANE_COPIES + 2,)),
            pltpu.SemaphoreType.DMA((PLANE_COPIES + 2,)),
            pltpu.SemaphoreType.DMA((1,)),
        ],
        compiler_params=pltpu.CompilerParams(
            collective_id=1, has_side_effects=True, vmem_limit_bytes=24 << 20
        ),
    )(o4, st, w)


BLK = 512
COLS = 256


def project_kernel(
    att_ref, w_ref, wz_ref, out_ref, give, keep, got, box, core_s, core_r, z_s, z_r
):
    z, x, y = coords()
    tp = lax.axis_index("tp")
    core = tp % 2
    high = tp // 2
    other = {"tp": tp + 1 - 2 * core}
    pos = 2 * high + z
    column = []
    for d in range(1, 8):
        q = (pos + d) % 8
        column.append({"ctx": ctx_of(q % 2, x, y), "tp": (q // 2) * 2 + core})
    entry_barrier(column + [other])

    def product(block, weights):
        rows = att_ref[pl.ds(4 * block, 4)].reshape(BLK, HEADS * HD)
        return jnp.dot(rows, weights[...], preferred_element_type=jnp.float32)

    copies = []
    for upper in range(2):
        block = 2 * upper + 1 - core
        for far in range(2):
            n = 2 * upper + far
            give[n] = product(block, wz_ref if far else w_ref).astype(jnp.bfloat16)
            copy = pltpu.make_async_remote_copy(
                src_ref=give.at[n],
                dst_ref=got.at[n],
                send_sem=core_s.at[n],
                recv_sem=core_r.at[n],
                device_id=other,
                device_id_type=MESH,
            )
            copy.start()
            copies.append(copy)
    for upper in range(2):
        block = 2 * upper + core
        for far in range(2):
            n = 2 * upper + far
            mine = product(block, wz_ref if far else w_ref)
            copies[n].wait()
            keep[n] = (mine + got[n].astype(jnp.float32)).astype(jnp.bfloat16)
            dest_high = 2 * z + upper
            dest_z = 1 - z if far else z
            dest = {"ctx": ctx_of(dest_z, x, y), "tp": dest_high * 2 + core}
            remote = jnp.logical_or(dest_high != high, dest_z != z)

            @pl.when(remote)
            def _(n=n, dest=dest):
                pltpu.make_async_remote_copy(
                    src_ref=keep.at[n],
                    dst_ref=box.at[high],
                    send_sem=z_s.at[n],
                    recv_sem=z_r.at[high],
                    device_id=dest,
                    device_id_type=MESH,
                ).start()

            @pl.when(jnp.logical_not(remote))
            def _(n=n):
                box[high] = keep[n]

    source_z = high // 2
    for s in range(4):
        arrives = jnp.logical_or(high != s, z != source_z)

        @pl.when(arrives)
        def _(s=s):
            pltpu.make_async_remote_copy(
                src_ref=keep.at[0],
                dst_ref=box.at[s],
                send_sem=z_s.at[0],
                recv_sem=z_r.at[s],
                device_id=other,
                device_id_type=MESH,
            ).wait_recv()

    out = box[0].astype(jnp.float32) + box[1].astype(jnp.float32)
    out += box[2].astype(jnp.float32) + box[3].astype(jnp.float32)
    out_ref[...] = out.astype(jnp.bfloat16)
    for upper in range(2):
        for far in range(2):
            n = 2 * upper + far
            remote = jnp.logical_or(2 * z + upper != high, jnp.bool_(far == 1))

            @pl.when(remote)
            def _(n=n):
                pltpu.make_async_remote_copy(
                    src_ref=keep.at[n],
                    dst_ref=box.at[0],
                    send_sem=z_s.at[n],
                    recv_sem=z_r.at[0],
                    device_id=other,
                    device_id_type=MESH,
                ).wait_send()


def project(att, w, wz):
    return pl.pallas_call(
        project_kernel,
        name="project",
        out_shape=jax.ShapeDtypeStruct((BLK, COLS), jnp.bfloat16),
        in_specs=[pl.BlockSpec(memory_space=pltpu.VMEM)] * 3,
        out_specs=pl.BlockSpec(memory_space=pltpu.VMEM),
        scratch_shapes=[
            pltpu.VMEM((4, BLK, COLS), jnp.bfloat16),
            pltpu.VMEM((4, BLK, COLS), jnp.bfloat16),
            pltpu.VMEM((4, BLK, COLS), jnp.bfloat16),
            pltpu.VMEM((4, BLK, COLS), jnp.bfloat16),
            pltpu.SemaphoreType.DMA((4,)),
            pltpu.SemaphoreType.DMA((4,)),
            pltpu.SemaphoreType.DMA((4,)),
            pltpu.SemaphoreType.DMA((4,)),
        ],
        compiler_params=pltpu.CompilerParams(
            collective_id=2, has_side_effects=True, vmem_limit_bytes=24 << 20
        ),
    )(att, w, wz)


def body(queries, span_kv, cache_kv, out_weight, offset, lengths):
    first_token = lax.axis_index("ctx") * TOK
    positions = offset[0] + first_token + jnp.arange(TOK, dtype=jnp.int32)
    rotated = rotate(queries.reshape(TOK, HEADS, HD).astype(jnp.float32), positions)
    rotated = rotated.astype(jnp.bfloat16).reshape(TOK, HEADS * HD)
    keys = rotate(span_kv[:, :, 0, :].astype(jnp.float32), positions).astype(jnp.bfloat16)
    span = jnp.concatenate([keys[:, 0, :], span_kv[:, 0, 1, :]], axis=1)
    kv = jnp.concatenate([cache_kv.reshape(CACHE_ROWS, 2 * HD), span], axis=0)
    q4, kvg = gather(rotated, kv)
    o4, st = attention(lengths, q4, kvg)
    att, wz = combine(o4, st, out_weight)
    return project(att, out_weight, wz)


def solution(mesh):
    return jax.shard_map(
        body,
        mesh=mesh,
        in_specs=(
            P("ctx", "tp"),
            P("ctx", "tp", None, None),
            P("ctx", "tp", None, None),
            P("tp", "ctx"),
            P(),
            P(),
        ),
        out_specs=P("tp", "ctx"),
        check_vma=False,
    )
```

```python
import math

import jax
import jax.numpy as jnp
from jax import lax
from jax.experimental import pallas as pl
from jax.experimental.pallas import tpu as pltpu
from jax.sharding import PartitionSpec as P

SLOT = 256
HD = 128
TOK = 128
HEADS = 8
KV_ROWS = 640
CACHE_ROWS = 512
CH = 512
NCH = 10
A_ROWS = 256
lowest_score = -1e30
rope_base = 500000.0
MESH = pl.DeviceIdType.MESH
SCALE2 = math.log2(math.e) / math.sqrt(HD)


def rotate(values, positions):
    head_size = values.shape[-1]
    half_dim = head_size // 2
    frequency = jnp.exp(
        jnp.arange(half_dim, dtype=jnp.float32) * (-2.0 * math.log(rope_base) / head_size)
    )
    angles = positions.astype(jnp.float32)[:, None] * frequency[None, :]
    cosine = jnp.cos(angles)[:, None, :]
    sine_part = jnp.sin(angles)[:, None, :]
    first_half = values[..., :half_dim]
    second_half = values[..., half_dim:]
    return jnp.concatenate(
        [
            first_half * cosine - second_half * sine_part,
            second_half * cosine + first_half * sine_part,
        ],
        axis=-1,
    )


def coords():
    c = lax.axis_index("ctx")
    z = c // 16
    x = (c // 4) % 4
    y = c % 4
    return z, x, y


def ctx_of(z, x, y):
    return z * 16 + x * 4 + y


def entry_barrier(devices):
    barrier = pltpu.get_barrier_semaphore()
    for d in devices:
        pl.semaphore_signal(barrier, inc=1, device_id=d, device_id_type=MESH)
    pl.semaphore_wait(barrier, len(devices))


class Sender:
    def __init__(self, ssem, rsem):
        self.ssem, self.rsem, self.count, self.sent = ssem, rsem, 0, []

    def __call__(self, src, dst, device):
        n = self.count
        self.count += 1
        copy = pltpu.make_async_remote_copy(
            src_ref=src,
            dst_ref=dst,
            send_sem=self.ssem.at[n],
            recv_sem=self.rsem.at[n],
            device_id=device,
            device_id_type=MESH,
        )
        copy.start()
        self.sent.append(copy)
        return copy

    def finish(self):
        for copy in self.sent:
            copy.wait_send()


GATHER_COPIES = 22


def gather_kernel(q_ref, kv_ref, q4_ref, kvg_ref, ssem, rsem, lsem):
    z, x, y = coords()
    xp, xm, x2 = (x + 1) % 4, (x + 3) % 4, (x + 2) % 4
    yp, ym = (y + 1) % 4, (y + 3) % 4
    zo = 1 - z
    dz = {"ctx": ctx_of(zo, x, y)}
    dxp = {"ctx": ctx_of(z, xp, y)}
    dxm = {"ctx": ctx_of(z, xm, y)}
    dyp = {"ctx": ctx_of(z, x, yp)}
    dym = {"ctx": ctx_of(z, x, ym)}
    a = pl.ds(0, A_ROWS)
    a0 = pl.ds(0, A_ROWS // 2)
    a1 = pl.ds(A_ROWS // 2, A_ROWS // 2)
    nb = KV_ROWS - A_ROWS
    b = pl.ds(A_ROWS, nb)
    b0 = pl.ds(A_ROWS, nb // 2)
    b1 = pl.ds(A_ROWS + nb // 2, nb // 2)
    t0 = pl.ds(0, TOK // 2)
    t1 = pl.ds(TOK // 2, TOK // 2)

    own = z * 4 + x
    lq = pltpu.make_async_copy(q_ref, q4_ref.at[y], lsem.at[0])
    lkv = pltpu.make_async_copy(kv_ref, kvg_ref.at[own], lsem.at[1])
    entry_barrier([dz, dxp, dxm, dyp, dym])
    lq.start()
    lkv.start()
    send = Sender(ssem, rsem)

    def kv(j, rows):
        return kvg_ref.at[j, rows]

    def pass_on(j, rows, device):
        return send(kv(j, rows), kv(j, rows), device)

    b_z = send(kv_ref.at[b], kv(own, b), dz)
    b_xp = send(kv_ref.at[b], kv(own, b), dxp)
    b_xm = send(kv_ref.at[b], kv(own, b), dxm)
    q_yp = send(q_ref, q4_ref.at[y], dyp)
    q_ym = send(q_ref, q4_ref.at[y], dym)
    a_xp = send(kv_ref.at[a], kv(own, a), dxp)
    a_xm = send(kv_ref.at[a], kv(own, a), dxm)
    a_z = send(kv_ref.at[a], kv(own, a), dz)
    b_z.wait_recv()
    oz = zo * 4 + x
    bz_xp = pass_on(oz, b, dxp)
    bz_xm = pass_on(oz, b, dxm)
    b_xp.wait_recv()
    bf_xp = pass_on(z * 4 + xm, b0, dxp)
    b_xm.wait_recv()
    bf_xm = pass_on(z * 4 + xp, b1, dxm)
    q_yp.wait_recv()
    qf_yp = send(q4_ref.at[ym, t0], q4_ref.at[ym, t0], dyp)
    q_ym.wait_recv()
    qf_ym = send(q4_ref.at[yp, t1], q4_ref.at[yp, t1], dym)
    a_xp.wait_recv()
    af_xp = pass_on(z * 4 + xm, a0, dxp)
    az_m = pass_on(z * 4 + xm, a, dz)
    a_xm.wait_recv()
    af_xm = pass_on(z * 4 + xp, a1, dxm)
    az_p = pass_on(z * 4 + xp, a, dz)
    bz_xp.wait_recv()
    bzf_xp = pass_on(zo * 4 + xm, b0, dxp)
    bz_xm.wait_recv()
    bzf_xm = pass_on(zo * 4 + xp, b1, dxm)
    af_xp.wait_recv()
    az_2a = pass_on(z * 4 + x2, a0, dz)
    af_xm.wait_recv()
    az_2b = pass_on(z * 4 + x2, a1, dz)
    for copy in (a_z, bf_xp, bf_xm, qf_yp, qf_ym, az_m, az_p, bzf_xp, bzf_xm, az_2a, az_2b):
        copy.wait_recv()
    send.finish()
    lq.wait()
    lkv.wait()


def gather(q, kv):
    return pl.pallas_call(
        gather_kernel,
        name="gather_qkv",
        out_shape=(
            jax.ShapeDtypeStruct((4, TOK, HEADS * HD), jnp.bfloat16),
            jax.ShapeDtypeStruct((8, KV_ROWS, 2 * HD), jnp.bfloat16),
        ),
        in_specs=[pl.BlockSpec(memory_space=pltpu.VMEM)] * 2,
        out_specs=[pl.BlockSpec(memory_space=pltpu.VMEM)] * 2,
        scratch_shapes=[
            pltpu.SemaphoreType.DMA((GATHER_COPIES,)),
            pltpu.SemaphoreType.DMA((GATHER_COPIES,)),
            pltpu.SemaphoreType.DMA((2,)),
        ],
        compiler_params=pltpu.CompilerParams(
            collective_id=0, has_side_effects=True, vmem_limit_bytes=16 << 20
        ),
    )(q, kv)


ROWS = HEADS * TOK


def attention_kernel(
    lens_ref, q4_ref, kvg_ref, o4_ref, st_ref, qh, kbuf, vbuf, bias, sbuf, sown, mx, mc, lsum, acc
):
    z, x, y = coords()
    j0 = z * 4 + x
    for yy in range(4):
        for h in range(HEADS):
            qh[yy, h * TOK : (h + 1) * TOK, :] = q4_ref[yy, :, h * HD : (h + 1) * HD]

    pos = lax.broadcasted_iota(jnp.int32, bias.shape, 0) * CH + lax.broadcasted_iota(
        jnp.int32, bias.shape, 1
    )
    mask = jnp.full(bias.shape, lowest_score, jnp.float32)
    off = jnp.int32(0)
    for j in range(8):
        for s in range(2):
            n = lens_ref[2 * (4 * j + y) + s]
            o = pl.multiple_of(off, 16)
            rows = pl.ds(s * SLOT, SLOT)
            kbuf[pl.ds(o, SLOT), :] = kvg_ref[j, rows, 0:HD]
            vbuf[pl.ds(o, SLOT), :] = kvg_ref[j, rows, HD : 2 * HD]
            mask = jnp.where((pos >= off) & (pos < off + n), 0.0, mask)
            off = off + ((n + 15) // 16) * 16
    for j in range(7):
        o = pl.multiple_of(off + j * TOK, 16)
        rows = pl.ds(CACHE_ROWS, TOK)
        kbuf[pl.ds(o, TOK), :] = kvg_ref[j, rows, 0:HD]
        vbuf[pl.ds(o, TOK), :] = kvg_ref[j, rows, HD : 2 * HD]
    total = off + j0 * TOK
    mask = jnp.where((pos >= off) & (pos < total), 0.0, mask)
    bias[...] = mask
    o = pl.multiple_of(total, 16)
    kbuf[pl.ds(o, CH), :] = jnp.zeros((CH, HD), jnp.bfloat16)
    vbuf[pl.ds(o, CH), :] = jnp.zeros((CH, HD), jnp.bfloat16)
    chunks = (total + CH - 1) // CH

    row_tok = lax.broadcasted_iota(jnp.int32, (TOK, TOK), 0)
    key_tok = lax.broadcasted_iota(jnp.int32, (TOK, TOK), 1)

    def scores(rows, keys):
        return lax.dot_general(
            rows, keys, (((1,), (1,)), ((), ())), preferred_element_type=jnp.float32
        )

    def fold(op, values):
        out = values[:, 0:HD]
        for n in range(1, values.shape[1] // HD):
            out = op(out, values[:, n * HD : (n + 1) * HD])
        return out

    def first_own(i, slot):
        own_keys = kvg_ref[j0, CACHE_ROWS:KV_ROWS, 0:HD]
        s = scores(qh[i], own_keys)
        ok = (key_tok + (y - i) * TOK) <= row_tok
        own_bias = jnp.where(ok, 0.0, lowest_score)
        s = s + jnp.concatenate([own_bias] * HEADS, axis=0)
        sown[slot] = s
        mx[...] = s

    def first_step(kc, i, slot):
        k0 = pl.multiple_of(kc * CH, CH)
        s = scores(qh[i], kbuf[pl.ds(k0, CH), :]) + bias[pl.ds(kc, 1), :]
        sbuf[slot, kc] = s
        mx[...] = jnp.maximum(mx[...], fold(jnp.maximum, s))

    def first_end():
        m = jnp.max(mx[...], axis=1, keepdims=True)
        mc[...] = jnp.broadcast_to(m * SCALE2, (ROWS, HD))

    def second_own(slot):
        own_values = kvg_ref[j0, CACHE_ROWS:KV_ROWS, HD : 2 * HD]
        p = jnp.exp2(sown[slot] * SCALE2 - mc[...])
        lsum[...] = p
        acc[...] = jnp.dot(p.astype(jnp.bfloat16), own_values, preferred_element_type=jnp.float32)

    def second_step(kc, slot):
        k0 = pl.multiple_of(kc * CH, CH)
        m = mc[...]
        p = jnp.exp2(sbuf[slot, kc] * SCALE2 - jnp.concatenate([m] * (CH // HD), axis=1))
        lsum[...] += fold(jnp.add, p)
        acc[...] += jnp.dot(
            p.astype(jnp.bfloat16), vbuf[pl.ds(k0, CH), :], preferred_element_type=jnp.float32
        )

    def second_end(i):
        l = jnp.broadcast_to(jnp.sum(lsum[...], axis=1, keepdims=True), (ROWS, HD))
        o = acc[...] / l
        lse = mc[...] + jnp.log2(l)
        lane = lax.broadcasted_iota(jnp.int32, (TOK, HD), 1)
        packed = jnp.zeros((TOK, HD), jnp.float32)
        for h in range(HEADS):
            rows = slice(h * TOK, (h + 1) * TOK)
            o4_ref[i, :, h * HD : (h + 1) * HD] = o[rows].astype(jnp.bfloat16)
            packed = jnp.where(lane == h, lse[rows], packed)
        st_ref[i] = packed.T[0:HEADS]

    first_own(0, 0)

    @pl.loop(0, chunks)
    def _(kc):
        first_step(kc, 0, 0)

    first_end()

    for i in range(4):
        slot = i % 2
        second_own(slot)
        if i < 3:
            first_own(i + 1, 1 - slot)

        @pl.loop(0, chunks)
        def _(kc, i=i, slot=slot):
            if i < 3:
                first_step(kc, i + 1, 1 - slot)
            second_step(kc, slot)

        second_end(i)
        if i < 3:
            first_end()


def attention(lengths, q4, kvg):
    rows = NCH * CH + CH
    return pl.pallas_call(
        attention_kernel,
        name="attention",
        out_shape=(
            jax.ShapeDtypeStruct((4, TOK, HEADS * HD), jnp.bfloat16),
            jax.ShapeDtypeStruct((4, HEADS, TOK), jnp.float32),
        ),
        in_specs=[
            pl.BlockSpec(memory_space=pltpu.SMEM),
            pl.BlockSpec(memory_space=pltpu.VMEM),
            pl.BlockSpec(memory_space=pltpu.VMEM),
        ],
        out_specs=[pl.BlockSpec(memory_space=pltpu.VMEM)] * 2,
        scratch_shapes=[
            pltpu.VMEM((4, ROWS, HD), jnp.bfloat16),
            pltpu.VMEM((rows, HD), jnp.bfloat16),
            pltpu.VMEM((rows, HD), jnp.bfloat16),
            pltpu.VMEM((16, CH), jnp.float32),
            pltpu.VMEM((2, NCH, ROWS, CH), jnp.float32),
            pltpu.VMEM((2, ROWS, HD), jnp.float32),
            pltpu.VMEM((ROWS, HD), jnp.float32),
            pltpu.VMEM((ROWS, HD), jnp.float32),
            pltpu.VMEM((ROWS, HD), jnp.float32),
            pltpu.VMEM((ROWS, HD), jnp.float32),
        ],
        compiler_params=pltpu.CompilerParams(vmem_limit_bytes=62 << 20),
    )(lengths, q4, kvg)


COMBINE_COPIES = 9
PLANE_COPIES = 40
BLK = 512
COLS = 256


def combine_project_kernel(
    o4_ref,
    st_ref,
    w_ref,
    wz_ref,
    out_ref,
    att,
    part,
    stat,
    fwd,
    mine,
    prod,
    give,
    got,
    keep,
    box,
    ssem,
    rsem,
    ssem2,
    rsem2,
    core_s,
    core_r,
    z_s,
    z_r,
):
    z, x, y = coords()
    tp = lax.axis_index("tp")
    core = tp % 2
    high = tp // 2
    other = {"tp": tp + 1 - 2 * core}
    pos = 2 * high + z
    column = []
    for d in range(1, 8):
        q = (pos + d) % 8
        column.append({"ctx": ctx_of(q % 2, x, y), "tp": (q // 2) * 2 + core})
    xp, xm, x2 = (x + 1) % 4, (x + 3) % 4, (x + 2) % 4
    yp, ym, y2 = (y + 1) % 4, (y + 3) % 4, (y + 2) % 4
    dxp = {"ctx": ctx_of(z, xp, y)}
    dxm = {"ctx": ctx_of(z, xm, y)}
    dyp = {"ctx": ctx_of(z, x, yp)}
    dym = {"ctx": ctx_of(z, x, ym)}
    dy2 = {"ctx": ctx_of(z, x, y2)}
    half = TOK // 2
    t0 = pl.ds(0, half)
    t1 = pl.ds(half, half)
    entry_barrier([dxp, dxm, dyp, dym, dy2, other] + column)
    send = Sender(ssem, rsem)
    far_p = send(o4_ref.at[y2, t0], fwd.at[0], dyp)
    far_m = send(o4_ref.at[y2, t1], fwd.at[1], dym)
    st_p = send(st_ref.at[yp], stat.at[2], dyp)
    st_m = send(st_ref.at[ym], stat.at[0], dym)
    st_2 = send(st_ref.at[y2], stat.at[1], dy2)
    to_p = send(o4_ref.at[yp], part.at[2], dyp)
    to_m = send(o4_ref.at[ym], part.at[0], dym)
    far_p.wait_recv()
    fw_p = send(fwd.at[0], part.at[1, t0], dyp)
    far_m.wait_recv()
    fw_m = send(fwd.at[1], part.at[1, t1], dym)
    for copy in (st_p, st_m, st_2):
        copy.wait_recv()
    s_own = st_ref[y]
    s_p, s_m, s_2 = stat[0], stat[2], stat[1]
    top = jnp.maximum(jnp.maximum(s_own, s_p), jnp.maximum(s_m, s_2))
    e_own = jnp.exp2(s_own - top)
    e_p = jnp.exp2(s_p - top)
    e_m = jnp.exp2(s_m - top)
    e_2 = jnp.exp2(s_2 - top)
    norm = 1.0 / (e_own + e_p + e_m + e_2)
    table = jnp.concatenate(
        [e_own * norm, e_p * norm, e_m * norm, e_2 * norm, jnp.zeros((96, TOK), jnp.float32)],
        axis=0,
    ).T
    for copy in (to_p, to_m, fw_p, fw_m):
        copy.wait_recv()
    own = x * 4 + y
    for h in range(HEADS):
        lanes = slice(h * HD, (h + 1) * HD)
        out = o4_ref[y, :, lanes].astype(jnp.float32) * table[:, h : h + 1]
        out += part[0, :, lanes].astype(jnp.float32) * table[:, 8 + h : 9 + h]
        out += part[2, :, lanes].astype(jnp.float32) * table[:, 16 + h : 17 + h]
        out += part[1, :, lanes].astype(jnp.float32) * table[:, 24 + h : 25 + h]
        mine[:, lanes] = out.astype(jnp.bfloat16)

    send2 = Sender(ssem2, rsem2)
    quarter = half // 2
    a, a0, a1 = t0, pl.ds(0, quarter), pl.ds(quarter, quarter)
    b, b0, b1 = t1, pl.ds(half, quarter), pl.ds(half + quarter, quarter)

    def pass_on(slot, rows, device):
        return send2(att.at[slot, rows], att.at[slot, rows], device)

    ax_p = send2(mine.at[a], att.at[own, a], dxp)
    ax_m = send2(mine.at[a], att.at[own, a], dxm)
    by_p = send2(mine.at[b], att.at[own, b], dyp)
    by_m = send2(mine.at[b], att.at[own, b], dym)
    ay = {0: (send2(mine.at[a], att.at[own, a], dyp), send2(mine.at[a], att.at[own, a], dym))}
    bx = {0: (send2(mine.at[b], att.at[own, b], dxp), send2(mine.at[b], att.at[own, b], dxm))}
    att[own] = mine[...]
    ax_p.wait_recv()
    axf_p = pass_on(xm * 4 + y, a0, dxp)
    by_p.wait_recv()
    byf_p = pass_on(x * 4 + ym, b0, dyp)
    ax_m.wait_recv()
    axf_m = pass_on(xp * 4 + y, a1, dxm)
    by_m.wait_recv()
    byf_m = pass_on(x * 4 + yp, b1, dym)
    ay[3] = (pass_on(xm * 4 + y, a, dyp), pass_on(xm * 4 + y, a, dym))
    bx[3] = (pass_on(x * 4 + ym, b, dxp), pass_on(x * 4 + ym, b, dxm))
    ay[1] = (pass_on(xp * 4 + y, a, dyp), pass_on(xp * 4 + y, a, dym))
    bx[1] = (pass_on(x * 4 + yp, b, dxp), pass_on(x * 4 + yp, b, dxm))
    last = {}

    def relay(k):
        p, m = ay[k]
        xs = (x + k) % 4
        p.wait_recv()
        first = pass_on(xs * 4 + ym, a0, dyp)
        m.wait_recv()
        second = pass_on(xs * 4 + yp, a1, dym)
        p, m = bx[k]
        ys = (y + k) % 4
        p.wait_recv()
        third = pass_on(xm * 4 + ys, b0, dxp)
        m.wait_recv()
        fourth = pass_on(xp * 4 + ys, b1, dxm)
        last[k] = (first, second, third, fourth)

    def wait_all(copies):
        for copy in copies:
            copy.wait_recv()

    def row_copies(row, n):
        core_copy = pltpu.make_async_remote_copy(
            src_ref=give.at[n],
            dst_ref=got.at[n],
            send_sem=core_s.at[n],
            recv_sem=core_r.at[n],
            device_id=other,
            device_id_type=MESH,
        )
        out = []
        for far in range(2):
            dest_high = 2 * z + row // 2
            dest_z = 1 - z if far else z
            copy = pltpu.make_async_remote_copy(
                src_ref=keep.at[n, far],
                dst_ref=box.at[high],
                send_sem=z_s.at[2 * n + far],
                recv_sem=z_r.at[high],
                device_id={"ctx": ctx_of(dest_z, x, y), "tp": dest_high * 2 + core},
                device_id_type=MESH,
            )
            remote = (dest_high != high) if far == 0 else None
            out.append((copy, remote))
        return core_copy, out

    def product(row, n):
        keeps = row % 2 == core
        core_copy, _ = row_copies(row, n)
        rows = att[pl.ds(4 * row, 4)].reshape(BLK, HEADS * HD)
        for far, weights in enumerate((w_ref, wz_ref)):
            prod[n % 2, far] = jnp.dot(rows, weights[...], preferred_element_type=jnp.float32)

        @pl.when(jnp.logical_not(keeps))
        def _():
            give[n] = prod[n % 2].astype(jnp.bfloat16)
            core_copy.start()

    def settle(row, n):
        keeps = row % 2 == core
        core_copy, copies = row_copies(row, n)

        @pl.when(keeps)
        def _():
            core_copy.wait_recv()
            keep[n] = (prod[n % 2] + got[n].astype(jnp.float32)).astype(jnp.bfloat16)
            for far, (copy, remote) in enumerate(copies):
                if remote is None:
                    copy.start()
                else:
                    pl.when(remote)(copy.start)

                    @pl.when(jnp.logical_not(remote))
                    def _():
                        box[high] = keep[n, far]

    relay(0)
    wait_all((axf_p, axf_m, byf_p, byf_m))
    ay[2] = (pass_on(x2 * 4 + y, a, dyp), pass_on(x2 * 4 + y, a, dym))
    bx[2] = (pass_on(x * 4 + y2, b, dxp), pass_on(x * 4 + y2, b, dxm))
    wait_all(last[0][:2])
    product(x, 0)
    relay(3)
    settle(x, 0)
    relay(1)
    relay(2)
    wait_all(last[3][:2])
    product(xm, 1)
    settle(xm, 1)
    wait_all(last[1][:2])
    product(xp, 2)
    settle(xp, 2)
    wait_all(last[2][:2])
    for k in range(4):
        wait_all(last[k][2:])
    product(x2, 3)
    settle(x2, 3)

    source_z = high // 2
    for s in range(4):
        arrives = jnp.logical_or(high != s, z != source_z)

        @pl.when(arrives)
        def _(s=s):
            pltpu.make_async_remote_copy(
                src_ref=keep.at[0, 0],
                dst_ref=box.at[s],
                send_sem=z_s.at[0],
                recv_sem=z_r.at[s],
                device_id=other,
                device_id_type=MESH,
            ).wait_recv()

    total = box[0].astype(jnp.float32) + box[1].astype(jnp.float32)
    total += box[2].astype(jnp.float32) + box[3].astype(jnp.float32)
    out_ref[...] = total.astype(jnp.bfloat16)
    for n, row in enumerate((x, xm, xp, x2)):
        keeps = row % 2 == core
        core_copy, copies = row_copies(row, n)

        @pl.when(keeps)
        def _(copies=copies):
            for copy, remote in copies:
                if remote is None:
                    copy.wait_send()
                else:
                    pl.when(remote)(copy.wait_send)

        pl.when(jnp.logical_not(keeps))(core_copy.wait_send)
    send.finish()
    send2.finish()


def combine_project(o4, st, w, wz):
    return pl.pallas_call(
        combine_project_kernel,
        name="combine_project",
        out_shape=jax.ShapeDtypeStruct((BLK, COLS), jnp.bfloat16),
        in_specs=[pl.BlockSpec(memory_space=pltpu.VMEM)] * 4,
        out_specs=pl.BlockSpec(memory_space=pltpu.VMEM),
        scratch_shapes=[
            pltpu.VMEM((16, TOK, HEADS * HD), jnp.bfloat16),
            pltpu.VMEM((3, TOK, HEADS * HD), jnp.bfloat16),
            pltpu.VMEM((3, HEADS, TOK), jnp.float32),
            pltpu.VMEM((2, TOK // 2, HEADS * HD), jnp.bfloat16),
            pltpu.VMEM((TOK, HEADS * HD), jnp.bfloat16),
            pltpu.VMEM((2, 2, BLK, COLS), jnp.float32),
            pltpu.VMEM((4, 2, BLK, COLS), jnp.bfloat16),
            pltpu.VMEM((4, 2, BLK, COLS), jnp.bfloat16),
            pltpu.VMEM((4, 2, BLK, COLS), jnp.bfloat16),
            pltpu.VMEM((4, BLK, COLS), jnp.bfloat16),
            pltpu.SemaphoreType.DMA((COMBINE_COPIES,)),
            pltpu.SemaphoreType.DMA((COMBINE_COPIES,)),
            pltpu.SemaphoreType.DMA((PLANE_COPIES,)),
            pltpu.SemaphoreType.DMA((PLANE_COPIES,)),
            pltpu.SemaphoreType.DMA((4,)),
            pltpu.SemaphoreType.DMA((4,)),
            pltpu.SemaphoreType.DMA((8,)),
            pltpu.SemaphoreType.DMA((4,)),
        ],
        compiler_params=pltpu.CompilerParams(
            collective_id=1, has_side_effects=True, vmem_limit_bytes=32 << 20
        ),
    )(o4, st, w, wz)


def body(queries, span_kv, cache_kv, out_weight, offset, lengths):
    first_token = lax.axis_index("ctx") * TOK
    positions = offset[0] + first_token + jnp.arange(TOK, dtype=jnp.int32)
    rotated = rotate(queries.reshape(TOK, HEADS, HD).astype(jnp.float32), positions)
    rotated = rotated.astype(jnp.bfloat16).reshape(TOK, HEADS * HD)
    keys = rotate(span_kv[:, :, 0, :].astype(jnp.float32), positions).astype(jnp.bfloat16)
    span = jnp.concatenate([keys[:, 0, :], span_kv[:, 0, 1, :]], axis=1)
    kv = jnp.concatenate([cache_kv.reshape(CACHE_ROWS, 2 * HD), span], axis=0)
    wz = lax.ppermute(out_weight, "ctx", [(c, (c + 16) % 32) for c in range(32)])
    q4, kvg = gather(rotated, kv)
    o4, st = attention(lengths, q4, kvg)
    return combine_project(o4, st, out_weight, wz)


def solution(mesh):
    return jax.shard_map(
        body,
        mesh=mesh,
        in_specs=(
            P("ctx", "tp"),
            P("ctx", "tp", None, None),
            P("ctx", "tp", None, None),
            P("tp", "ctx"),
            P(),
            P(),
        ),
        out_specs=P("tp", "ctx"),
        check_vma=False,
    )
```

```python
import math

import jax
import jax.numpy as jnp
from jax import lax
from jax.experimental import pallas as pl
from jax.experimental.pallas import tpu as pltpu
from jax.sharding import PartitionSpec as P

SLOT = 256
HD = 128
TOK = 128
HEADS = 8
KV_ROWS = 640
CACHE_ROWS = 512
CH = 512
NCH = 10
A_ROWS = 256
lowest_score = -1e30
rope_base = 500000.0
MESH = pl.DeviceIdType.MESH
SCALE2 = math.log2(math.e) / math.sqrt(HD)


def rotate(values, positions):
    head_size = values.shape[-1]
    half_dim = head_size // 2
    frequency = jnp.exp(
        jnp.arange(half_dim, dtype=jnp.float32) * (-2.0 * math.log(rope_base) / head_size)
    )
    angles = positions.astype(jnp.float32)[:, None] * frequency[None, :]
    cosine = jnp.cos(angles)[:, None, :]
    sine_part = jnp.sin(angles)[:, None, :]
    first_half = values[..., :half_dim]
    second_half = values[..., half_dim:]
    return jnp.concatenate(
        [
            first_half * cosine - second_half * sine_part,
            second_half * cosine + first_half * sine_part,
        ],
        axis=-1,
    )


def coords():
    c = lax.axis_index("ctx")
    z = c // 16
    x = (c // 4) % 4
    y = c % 4
    return z, x, y


def ctx_of(z, x, y):
    return z * 16 + x * 4 + y


def entry_barrier(devices):
    barrier = pltpu.get_barrier_semaphore()
    for d in devices:
        pl.semaphore_signal(barrier, inc=1, device_id=d, device_id_type=MESH)
    pl.semaphore_wait(barrier, len(devices))


class Sender:
    def __init__(self, ssem, rsem):
        self.ssem, self.rsem, self.count, self.sent = ssem, rsem, 0, []

    def __call__(self, src, dst, device):
        n = self.count
        self.count += 1
        copy = pltpu.make_async_remote_copy(
            src_ref=src,
            dst_ref=dst,
            send_sem=self.ssem.at[n],
            recv_sem=self.rsem.at[n],
            device_id=device,
            device_id_type=MESH,
        )
        copy.start()
        self.sent.append(copy)
        return copy

    def finish(self):
        for copy in self.sent:
            copy.wait_send()


GATHER_COPIES = 22


def gather_kernel(q_ref, kv_ref, q4_ref, kvg_ref, ssem, rsem, lsem):
    z, x, y = coords()
    xp, xm, x2 = (x + 1) % 4, (x + 3) % 4, (x + 2) % 4
    yp, ym = (y + 1) % 4, (y + 3) % 4
    zo = 1 - z
    dz = {"ctx": ctx_of(zo, x, y)}
    dxp = {"ctx": ctx_of(z, xp, y)}
    dxm = {"ctx": ctx_of(z, xm, y)}
    dyp = {"ctx": ctx_of(z, x, yp)}
    dym = {"ctx": ctx_of(z, x, ym)}
    a = pl.ds(0, A_ROWS)
    a0 = pl.ds(0, A_ROWS // 2)
    a1 = pl.ds(A_ROWS // 2, A_ROWS // 2)
    nb = KV_ROWS - A_ROWS
    b = pl.ds(A_ROWS, nb)
    b0 = pl.ds(A_ROWS, nb // 2)
    b1 = pl.ds(A_ROWS + nb // 2, nb // 2)
    t0 = pl.ds(0, TOK // 2)
    t1 = pl.ds(TOK // 2, TOK // 2)

    own = z * 4 + x
    lq = pltpu.make_async_copy(q_ref, q4_ref.at[y], lsem.at[0])
    lkv = pltpu.make_async_copy(kv_ref, kvg_ref.at[own], lsem.at[1])
    entry_barrier([dz, dxp, dxm, dyp, dym])
    lq.start()
    lkv.start()
    send = Sender(ssem, rsem)

    def kv(j, rows):
        return kvg_ref.at[j, rows]

    def pass_on(j, rows, device):
        return send(kv(j, rows), kv(j, rows), device)

    b_z = send(kv_ref.at[b], kv(own, b), dz)
    b_xp = send(kv_ref.at[b], kv(own, b), dxp)
    b_xm = send(kv_ref.at[b], kv(own, b), dxm)
    q_yp = send(q_ref, q4_ref.at[y], dyp)
    q_ym = send(q_ref, q4_ref.at[y], dym)
    a_xp = send(kv_ref.at[a], kv(own, a), dxp)
    a_xm = send(kv_ref.at[a], kv(own, a), dxm)
    a_z = send(kv_ref.at[a], kv(own, a), dz)
    b_z.wait_recv()
    oz = zo * 4 + x
    bz_xp = pass_on(oz, b, dxp)
    bz_xm = pass_on(oz, b, dxm)
    b_xp.wait_recv()
    bf_xp = pass_on(z * 4 + xm, b0, dxp)
    b_xm.wait_recv()
    bf_xm = pass_on(z * 4 + xp, b1, dxm)
    q_yp.wait_recv()
    qf_yp = send(q4_ref.at[ym, t0], q4_ref.at[ym, t0], dyp)
    q_ym.wait_recv()
    qf_ym = send(q4_ref.at[yp, t1], q4_ref.at[yp, t1], dym)
    a_xp.wait_recv()
    af_xp = pass_on(z * 4 + xm, a0, dxp)
    az_m = pass_on(z * 4 + xm, a, dz)
    a_xm.wait_recv()
    af_xm = pass_on(z * 4 + xp, a1, dxm)
    az_p = pass_on(z * 4 + xp, a, dz)
    bz_xp.wait_recv()
    bzf_xp = pass_on(zo * 4 + xm, b0, dxp)
    bz_xm.wait_recv()
    bzf_xm = pass_on(zo * 4 + xp, b1, dxm)
    af_xp.wait_recv()
    az_2a = pass_on(z * 4 + x2, a0, dz)
    af_xm.wait_recv()
    az_2b = pass_on(z * 4 + x2, a1, dz)
    for copy in (a_z, bf_xp, bf_xm, qf_yp, qf_ym, az_m, az_p, bzf_xp, bzf_xm, az_2a, az_2b):
        copy.wait_recv()
    send.finish()
    lq.wait()
    lkv.wait()


def gather(q, kv):
    return pl.pallas_call(
        gather_kernel,
        name="gather_qkv",
        out_shape=(
            jax.ShapeDtypeStruct((4, TOK, HEADS * HD), jnp.bfloat16),
            jax.ShapeDtypeStruct((8, KV_ROWS, 2 * HD), jnp.bfloat16),
        ),
        in_specs=[pl.BlockSpec(memory_space=pltpu.VMEM)] * 2,
        out_specs=[pl.BlockSpec(memory_space=pltpu.VMEM)] * 2,
        scratch_shapes=[
            pltpu.SemaphoreType.DMA((GATHER_COPIES,)),
            pltpu.SemaphoreType.DMA((GATHER_COPIES,)),
            pltpu.SemaphoreType.DMA((2,)),
        ],
        compiler_params=pltpu.CompilerParams(
            collective_id=0, has_side_effects=True, vmem_limit_bytes=16 << 20
        ),
    )(q, kv)


ROWS = HEADS * TOK


def attention_kernel(
    lens_ref, q4_ref, kvg_ref, o4_ref, st_ref, qh, kbuf, vbuf, bias, sbuf, sown, mx, mc, lsum, acc
):
    z, x, y = coords()
    j0 = z * 4 + x
    for yy in range(4):
        for h in range(HEADS):
            qh[yy, h * TOK : (h + 1) * TOK, :] = q4_ref[yy, :, h * HD : (h + 1) * HD]

    pos = lax.broadcasted_iota(jnp.int32, bias.shape, 0) * CH + lax.broadcasted_iota(
        jnp.int32, bias.shape, 1
    )
    mask = jnp.full(bias.shape, lowest_score, jnp.float32)
    off = jnp.int32(0)
    for j in range(8):
        for s in range(2):
            n = lens_ref[2 * (4 * j + y) + s]
            o = pl.multiple_of(off, 16)
            rows = pl.ds(s * SLOT, SLOT)
            kbuf[pl.ds(o, SLOT), :] = kvg_ref[j, rows, 0:HD]
            vbuf[pl.ds(o, SLOT), :] = kvg_ref[j, rows, HD : 2 * HD]
            mask = jnp.where((pos >= off) & (pos < off + n), 0.0, mask)
            off = off + ((n + 15) // 16) * 16
    for j in range(7):
        o = pl.multiple_of(off + j * TOK, 16)
        rows = pl.ds(CACHE_ROWS, TOK)
        kbuf[pl.ds(o, TOK), :] = kvg_ref[j, rows, 0:HD]
        vbuf[pl.ds(o, TOK), :] = kvg_ref[j, rows, HD : 2 * HD]
    total = off + j0 * TOK
    mask = jnp.where((pos >= off) & (pos < total), 0.0, mask)
    bias[...] = mask
    o = pl.multiple_of(total, 16)
    kbuf[pl.ds(o, CH), :] = jnp.zeros((CH, HD), jnp.bfloat16)
    vbuf[pl.ds(o, CH), :] = jnp.zeros((CH, HD), jnp.bfloat16)
    chunks = (total + CH - 1) // CH

    row_tok = lax.broadcasted_iota(jnp.int32, (TOK, TOK), 0)
    key_tok = lax.broadcasted_iota(jnp.int32, (TOK, TOK), 1)

    def scores(rows, keys):
        return lax.dot_general(
            rows, keys, (((1,), (1,)), ((), ())), preferred_element_type=jnp.float32
        )

    def fold(op, values):
        out = values[:, 0:HD]
        for n in range(1, values.shape[1] // HD):
            out = op(out, values[:, n * HD : (n + 1) * HD])
        return out

    def first_own(i, slot):
        own_keys = kvg_ref[j0, CACHE_ROWS:KV_ROWS, 0:HD]
        s = scores(qh[i], own_keys)
        ok = (key_tok + (y - i) * TOK) <= row_tok
        own_bias = jnp.where(ok, 0.0, lowest_score)
        s = s + jnp.concatenate([own_bias] * HEADS, axis=0)
        sown[slot] = s
        mx[...] = s

    def first_step(kc, i, slot):
        k0 = pl.multiple_of(kc * CH, CH)
        s = scores(qh[i], kbuf[pl.ds(k0, CH), :]) + bias[pl.ds(kc, 1), :]
        sbuf[slot, kc] = s
        mx[...] = jnp.maximum(mx[...], fold(jnp.maximum, s))

    def first_end():
        m = jnp.max(mx[...], axis=1, keepdims=True)
        mc[...] = jnp.broadcast_to(m * SCALE2, (ROWS, HD))

    def second_own(slot):
        own_values = kvg_ref[j0, CACHE_ROWS:KV_ROWS, HD : 2 * HD]
        p = jnp.exp2(sown[slot] * SCALE2 - mc[...])
        lsum[...] = p
        acc[...] = jnp.dot(p.astype(jnp.bfloat16), own_values, preferred_element_type=jnp.float32)

    def second_step(kc, slot):
        k0 = pl.multiple_of(kc * CH, CH)
        m = mc[...]
        p = jnp.exp2(sbuf[slot, kc] * SCALE2 - jnp.concatenate([m] * (CH // HD), axis=1))
        lsum[...] += fold(jnp.add, p)
        acc[...] += jnp.dot(
            p.astype(jnp.bfloat16), vbuf[pl.ds(k0, CH), :], preferred_element_type=jnp.float32
        )

    def second_end(i):
        l = jnp.broadcast_to(jnp.sum(lsum[...], axis=1, keepdims=True), (ROWS, HD))
        o = acc[...] / l
        lse = mc[...] + jnp.log2(l)
        lane = lax.broadcasted_iota(jnp.int32, (TOK, HD), 1)
        packed = jnp.zeros((TOK, HD), jnp.float32)
        for h in range(HEADS):
            rows = slice(h * TOK, (h + 1) * TOK)
            o4_ref[i, :, h * HD : (h + 1) * HD] = o[rows].astype(jnp.bfloat16)
            packed = jnp.where(lane == h, lse[rows], packed)
        st_ref[i] = packed.T[0:HEADS]

    first_own(0, 0)

    @pl.loop(0, chunks)
    def _(kc):
        first_step(kc, 0, 0)

    first_end()

    for i in range(4):
        slot = i % 2
        second_own(slot)
        if i < 3:
            first_own(i + 1, 1 - slot)

        @pl.loop(0, chunks)
        def _(kc, i=i, slot=slot):
            if i < 3:
                first_step(kc, i + 1, 1 - slot)
            second_step(kc, slot)

        second_end(i)
        if i < 3:
            first_end()


def attention(lengths, q4, kvg):
    rows = NCH * CH + CH
    return pl.pallas_call(
        attention_kernel,
        name="attention",
        out_shape=(
            jax.ShapeDtypeStruct((4, TOK, HEADS * HD), jnp.bfloat16),
            jax.ShapeDtypeStruct((4, HEADS, TOK), jnp.float32),
        ),
        in_specs=[
            pl.BlockSpec(memory_space=pltpu.SMEM),
            pl.BlockSpec(memory_space=pltpu.VMEM),
            pl.BlockSpec(memory_space=pltpu.VMEM),
        ],
        out_specs=[pl.BlockSpec(memory_space=pltpu.VMEM)] * 2,
        scratch_shapes=[
            pltpu.VMEM((4, ROWS, HD), jnp.bfloat16),
            pltpu.VMEM((rows, HD), jnp.bfloat16),
            pltpu.VMEM((rows, HD), jnp.bfloat16),
            pltpu.VMEM((16, CH), jnp.float32),
            pltpu.VMEM((2, NCH, ROWS, CH), jnp.float32),
            pltpu.VMEM((2, ROWS, HD), jnp.float32),
            pltpu.VMEM((ROWS, HD), jnp.float32),
            pltpu.VMEM((ROWS, HD), jnp.float32),
            pltpu.VMEM((ROWS, HD), jnp.float32),
            pltpu.VMEM((ROWS, HD), jnp.float32),
        ],
        compiler_params=pltpu.CompilerParams(vmem_limit_bytes=62 << 20),
    )(lengths, q4, kvg)


COMBINE_COPIES = 9
PLANE_COPIES = 40
BLK = 512
COLS = 256


def combine_project_kernel(
    o4_ref,
    st_ref,
    w_ref,
    wz_ref,
    wh_ref,
    wzh_ref,
    out_ref,
    att,
    part,
    stat,
    table,
    fwd,
    away,
    prod,
    give,
    got,
    keep,
    box,
    ssem,
    rsem,
    ssem2,
    rsem2,
    core_s,
    core_r,
    z_s,
    z_r,
):
    z, x, y = coords()
    tp = lax.axis_index("tp")
    core = tp % 2
    high = tp // 2
    even = high % 2
    other = {"tp": tp + 1 - 2 * core}
    pair = {"tp": tp + 2 - 4 * even}
    pos = 2 * high + z
    column = []
    for d in range(1, 8):
        q = (pos + d) % 8
        column.append({"ctx": ctx_of(q % 2, x, y), "tp": (q // 2) * 2 + core})
    xp, xm, x2 = (x + 1) % 4, (x + 3) % 4, (x + 2) % 4
    yp, ym, y2 = (y + 1) % 4, (y + 3) % 4, (y + 2) % 4
    dxp = {"ctx": ctx_of(z, xp, y)}
    dxm = {"ctx": ctx_of(z, xm, y)}
    dyp = {"ctx": ctx_of(z, x, yp)}
    dym = {"ctx": ctx_of(z, x, ym)}
    dy2 = {"ctx": ctx_of(z, x, y2)}
    half = TOK // 2
    t0 = pl.ds(0, half)
    t1 = pl.ds(half, half)
    entry_barrier([dxp, dxm, dyp, dym, dy2, other] + column)
    send = Sender(ssem, rsem)
    far_p = send(o4_ref.at[y2, t0], fwd.at[0], dyp)
    far_m = send(o4_ref.at[y2, t1], fwd.at[1], dym)
    st_p = send(st_ref.at[yp], stat.at[2], dyp)
    st_m = send(st_ref.at[ym], stat.at[0], dym)
    st_2 = send(st_ref.at[y2], stat.at[1], dy2)
    to_p = send(o4_ref.at[yp], part.at[2], dyp)
    to_m = send(o4_ref.at[ym], part.at[0], dym)
    far_p.wait_recv()
    fw_p = send(fwd.at[0], part.at[1, t0], dyp)
    far_m.wait_recv()
    fw_m = send(fwd.at[1], part.at[1, t1], dym)
    for copy in (st_p, st_m, st_2):
        copy.wait_recv()
    s_own = st_ref[y]
    s_p, s_m, s_2 = stat[0], stat[2], stat[1]
    top = jnp.maximum(jnp.maximum(s_own, s_p), jnp.maximum(s_m, s_2))
    e_own = jnp.exp2(s_own - top)
    e_p = jnp.exp2(s_p - top)
    e_m = jnp.exp2(s_m - top)
    e_2 = jnp.exp2(s_2 - top)
    norm = 1.0 / (e_own + e_p + e_m + e_2)
    table[...] = jnp.concatenate(
        [e_own * norm, e_p * norm, e_m * norm, e_2 * norm, jnp.zeros((96, TOK), jnp.float32)],
        axis=0,
    ).T
    for copy in (to_p, to_m, fw_p, fw_m):
        copy.wait_recv()
    own = x * 4 + y

    def combined(first, dest):
        rows = pl.ds(pl.multiple_of(first, half), half)
        for h in range(HEADS):
            lanes = slice(h * HD, (h + 1) * HD)
            out = o4_ref[y, rows, lanes].astype(jnp.float32) * table[rows, h : h + 1]
            out += part[0, rows, lanes].astype(jnp.float32) * table[rows, 8 + h : 9 + h]
            out += part[2, rows, lanes].astype(jnp.float32) * table[rows, 16 + h : 17 + h]
            out += part[1, rows, lanes].astype(jnp.float32) * table[rows, 24 + h : 25 + h]
            dest[:, lanes] = out.astype(jnp.bfloat16)

    send2 = Sender(ssem2, rsem2)
    combined((1 - even) * half, away)
    swap = send2(away, att.at[1, own], pair)
    combined(even * half, att.at[0, own])
    quarter = half // 2
    lo, hi, full = pl.ds(0, quarter), pl.ds(quarter, quarter), pl.ds(0, half)

    def pass_on(k, slot, rows, device):
        return send2(att.at[k, slot, rows], att.at[k, slot, rows], device)

    ax_p = pass_on(0, own, full, dxp)
    ax_m = pass_on(0, own, full, dxm)
    ay = {0: (pass_on(0, own, full, dyp), pass_on(0, own, full, dym))}
    bx = {}
    ax_p.wait_recv()
    axf_p = pass_on(0, xm * 4 + y, lo, dxp)
    ay[3] = (pass_on(0, xm * 4 + y, full, dyp), pass_on(0, xm * 4 + y, full, dym))
    ax_m.wait_recv()
    axf_m = pass_on(0, xp * 4 + y, hi, dxm)
    ay[1] = (pass_on(0, xp * 4 + y, full, dyp), pass_on(0, xp * 4 + y, full, dym))
    swap.wait_recv()
    by_p = pass_on(1, own, full, dyp)
    by_m = pass_on(1, own, full, dym)
    bx[0] = (pass_on(1, own, full, dxp), pass_on(1, own, full, dxm))
    last = {}

    def relay_a(k):
        p, m = ay[k]
        xs = (x + k) % 4
        p.wait_recv()
        first = pass_on(0, xs * 4 + ym, lo, dyp)
        m.wait_recv()
        second = pass_on(0, xs * 4 + yp, hi, dym)
        last[0, k] = (first, second)

    def relay_b(k):
        p, m = bx[k]
        ys = (y + k) % 4
        p.wait_recv()
        third = pass_on(1, xm * 4 + ys, lo, dxp)
        m.wait_recv()
        fourth = pass_on(1, xp * 4 + ys, hi, dxm)
        last[1, k] = (third, fourth)

    def wait_all(copies):
        for copy in copies:
            copy.wait_recv()

    def core_copy(n):
        return pltpu.make_async_remote_copy(
            src_ref=give.at[n],
            dst_ref=got.at[n],
            send_sem=core_s.at[n],
            recv_sem=core_r.at[n],
            device_id=other,
            device_id_type=MESH,
        )

    def z_copy(row, n, far):
        return pltpu.make_async_remote_copy(
            src_ref=keep.at[n, far],
            dst_ref=box.at[high],
            send_sem=z_s.at[2 * n + far],
            recv_sem=z_r.at[high],
            device_id={
                "ctx": ctx_of(1 - z if far else z, x, y),
                "tp": (2 * z + row // 2) * 2 + core,
            },
            device_id_type=MESH,
        )

    def product(row, n):
        keeps = row % 2 == core
        slots = pl.ds(4 * row, 4)
        rows_a = att[0, slots].reshape(BLK // 2, HEADS * HD)
        rows_b = att[1, slots].reshape(BLK // 2, HEADS * HD)
        for far, (wa, wb) in enumerate(((w_ref, wh_ref), (wz_ref, wzh_ref))):
            prod[n % 2, far] = jnp.dot(
                rows_a, wa[...], preferred_element_type=jnp.float32
            ) + jnp.dot(rows_b, wb[...], preferred_element_type=jnp.float32)

        @pl.when(jnp.logical_not(keeps))
        def _():
            give[n] = prod[n % 2].astype(jnp.bfloat16)
            core_copy(n).start()

    def settle(row, n):
        keeps = row % 2 == core
        remote = 2 * z + row // 2 != high

        @pl.when(keeps)
        def _():
            core_copy(n).wait_recv()
            keep[n] = (prod[n % 2] + got[n].astype(jnp.float32)).astype(jnp.bfloat16)
            z_copy(row, n, 1).start()

            @pl.when(remote)
            def _():
                z_copy(row, n, 0).start()

            @pl.when(jnp.logical_not(remote))
            def _():
                box[high] = keep[n, 0]

    relay_a(0)
    by_p.wait_recv()
    byf_p = pass_on(1, x * 4 + ym, lo, dyp)
    bx[3] = (pass_on(1, x * 4 + ym, full, dxp), pass_on(1, x * 4 + ym, full, dxm))
    by_m.wait_recv()
    byf_m = pass_on(1, x * 4 + yp, hi, dym)
    bx[1] = (pass_on(1, x * 4 + yp, full, dxp), pass_on(1, x * 4 + yp, full, dxm))
    wait_all((axf_p, axf_m))
    ay[2] = (pass_on(0, x2 * 4 + y, full, dyp), pass_on(0, x2 * 4 + y, full, dym))
    relay_a(3)
    relay_b(0)
    wait_all((byf_p, byf_m))
    bx[2] = (pass_on(1, x * 4 + y2, full, dxp), pass_on(1, x * 4 + y2, full, dxm))
    wait_all(last[0, 0])
    product(x, 0)
    relay_a(1)
    settle(x, 0)
    relay_b(3)
    relay_b(1)
    relay_a(2)
    relay_b(2)
    wait_all(last[0, 3])
    product(xm, 1)
    settle(xm, 1)
    wait_all(last[0, 1])
    product(xp, 2)
    settle(xp, 2)
    wait_all(last[0, 2])
    for k in range(4):
        wait_all(last[1, k])
    product(x2, 3)
    settle(x2, 3)

    source_z = high // 2
    for s in range(4):
        arrives = jnp.logical_or(high != s, z != source_z)

        @pl.when(arrives)
        def _(s=s):
            pltpu.make_async_remote_copy(
                src_ref=keep.at[0, 0],
                dst_ref=box.at[s],
                send_sem=z_s.at[0],
                recv_sem=z_r.at[s],
                device_id=other,
                device_id_type=MESH,
            ).wait_recv()

    for e in range(2):
        total = box[e].astype(jnp.float32) + box[2 + e].astype(jnp.float32)
        total = total.astype(jnp.bfloat16)
        for g in range(4):
            first = g * TOK + e * half
            out_ref[first : first + half] = total[g * half : (g + 1) * half]
    for n, row in enumerate((x, xm, xp, x2)):
        keeps = row % 2 == core
        remote = 2 * z + row // 2 != high

        @pl.when(keeps)
        def _(n=n, row=row, remote=remote):
            z_copy(row, n, 1).wait_send()

            @pl.when(remote)
            def _():
                z_copy(row, n, 0).wait_send()

        @pl.when(jnp.logical_not(keeps))
        def _(n=n):
            core_copy(n).wait_send()

    send.finish()
    send2.finish()


def combine_project(o4, st, *weights):
    return pl.pallas_call(
        combine_project_kernel,
        name="combine_project",
        out_shape=jax.ShapeDtypeStruct((BLK, COLS), jnp.bfloat16),
        in_specs=[pl.BlockSpec(memory_space=pltpu.VMEM)] * 6,
        out_specs=pl.BlockSpec(memory_space=pltpu.VMEM),
        scratch_shapes=[
            pltpu.VMEM((2, 16, TOK // 2, HEADS * HD), jnp.bfloat16),
            pltpu.VMEM((3, TOK, HEADS * HD), jnp.bfloat16),
            pltpu.VMEM((3, HEADS, TOK), jnp.float32),
            pltpu.VMEM((TOK, TOK), jnp.float32),
            pltpu.VMEM((2, TOK // 2, HEADS * HD), jnp.bfloat16),
            pltpu.VMEM((TOK // 2, HEADS * HD), jnp.bfloat16),
            pltpu.VMEM((2, 2, BLK // 2, COLS), jnp.float32),
            pltpu.VMEM((4, 2, BLK // 2, COLS), jnp.bfloat16),
            pltpu.VMEM((4, 2, BLK // 2, COLS), jnp.bfloat16),
            pltpu.VMEM((4, 2, BLK // 2, COLS), jnp.bfloat16),
            pltpu.VMEM((4, BLK // 2, COLS), jnp.bfloat16),
            pltpu.SemaphoreType.DMA((COMBINE_COPIES,)),
            pltpu.SemaphoreType.DMA((COMBINE_COPIES,)),
            pltpu.SemaphoreType.DMA((PLANE_COPIES + 1,)),
            pltpu.SemaphoreType.DMA((PLANE_COPIES + 1,)),
            pltpu.SemaphoreType.DMA((4,)),
            pltpu.SemaphoreType.DMA((4,)),
            pltpu.SemaphoreType.DMA((8,)),
            pltpu.SemaphoreType.DMA((4,)),
        ],
        compiler_params=pltpu.CompilerParams(
            collective_id=1, has_side_effects=True, vmem_limit_bytes=32 << 20
        ),
    )(o4, st, *weights)


def body(queries, span_kv, cache_kv, out_weight, offset, lengths):
    first_token = lax.axis_index("ctx") * TOK
    positions = offset[0] + first_token + jnp.arange(TOK, dtype=jnp.int32)
    rotated = rotate(queries.reshape(TOK, HEADS, HD).astype(jnp.float32), positions)
    rotated = rotated.astype(jnp.bfloat16).reshape(TOK, HEADS * HD)
    keys = rotate(span_kv[:, :, 0, :].astype(jnp.float32), positions).astype(jnp.bfloat16)
    span = jnp.concatenate([keys[:, 0, :], span_kv[:, 0, 1, :]], axis=1)
    kv = jnp.concatenate([cache_kv.reshape(CACHE_ROWS, 2 * HD), span], axis=0)
    q4, kvg = gather(rotated, kv)
    w = lax.optimization_barrier((out_weight, kvg))[0]
    wz = lax.ppermute(w, "ctx", [(c, (c + 16) % 32) for c in range(32)])
    swap_pair = [(t, t + 2 - 4 * (t // 2 % 2)) for t in range(8)]
    wh = lax.ppermute(w, "tp", swap_pair)
    swap_both = [
        (c * 8 + t, (c + 16) % 32 * 8 + u) for c in range(32) for t, u in swap_pair
    ]
    wzh = lax.ppermute(w, ("ctx", "tp"), swap_both)
    o4, st = attention(lengths, q4, kvg)
    return combine_project(o4, st, out_weight, wz, wh, wzh)


def solution(mesh):
    return jax.shard_map(
        body,
        mesh=mesh,
        in_specs=(
            P("ctx", "tp"),
            P("ctx", "tp", None, None),
            P("ctx", "tp", None, None),
            P("tp", "ctx"),
            P(),
            P(),
        ),
        out_specs=P("tp", "ctx"),
        check_vma=False,
    )
```

```python
import math

import jax
import jax.numpy as jnp
from jax import lax
from jax.experimental import pallas as pl
from jax.experimental.pallas import tpu as pltpu
from jax.sharding import PartitionSpec as P

SLOT = 256
HD = 128
TOK = 128
HEADS = 8
KV_ROWS = 640
CH = 512
A_ROWS = 256
ROWS = HEADS * TOK
BLK = 512
COLS = 256
HALF = TOK // 2
COPIES = 80
lowest_score = -1e30
rope_base = 500000.0
MESH = pl.DeviceIdType.MESH
SCALE2 = math.log2(math.e) / math.sqrt(HD)


def rotate(values, positions):
    head_size = values.shape[-1]
    half_dim = head_size // 2
    frequency = jnp.exp(
        jnp.arange(half_dim, dtype=jnp.float32) * (-2.0 * math.log(rope_base) / head_size)
    )
    angles = positions.astype(jnp.float32)[:, None] * frequency[None, :]
    cosine = jnp.cos(angles)[:, None, :]
    sine_part = jnp.sin(angles)[:, None, :]
    first_half = values[..., :half_dim]
    second_half = values[..., half_dim:]
    return jnp.concatenate(
        [
            first_half * cosine - second_half * sine_part,
            second_half * cosine + first_half * sine_part,
        ],
        axis=-1,
    )


def coords():
    c = lax.axis_index("ctx")
    z = c // 16
    x = (c // 4) % 4
    y = c % 4
    return z, x, y


def ctx_of(z, x, y):
    return z * 16 + x * 4 + y


def entry_barrier(devices):
    barrier = pltpu.get_barrier_semaphore()
    for d in devices:
        pl.semaphore_signal(barrier, inc=1, device_id=d, device_id_type=MESH)
    pl.semaphore_wait(barrier, len(devices))


def fold(op, values):
    out = values[:, 0:HD]
    for n in range(1, values.shape[1] // HD):
        out = op(out, values[:, n * HD : (n + 1) * HD])
    return out


def wide(values):
    return jnp.concatenate([values] * (CH // HD), axis=1)


def fused_kernel(
    lens_ref,
    q_ref,
    kv_ref,
    w_ref,
    out_ref,
    qh,
    kvg,
    bias,
    sbuf,
    mx,
    top,
    den,
    acc,
    o4,
    st,
    part,
    stat,
    table,
    fwd,
    away,
    wz,
    wh,
    wzh,
    att,
    prod,
    give,
    got,
    keep,
    box,
    ssem,
    rsem,
    core_s,
    core_r,
    z_s,
    z_r,
):
    z, x, y = coords()
    tp = lax.axis_index("tp")
    core = tp % 2
    high = tp // 2
    even = high % 2
    zo = 1 - z
    other = {"tp": tp + 1 - 2 * core}
    pair = {"tp": tp + 2 - 4 * even}
    pos = 2 * high + z
    column = []
    for d in range(1, 8):
        q = (pos + d) % 8
        column.append({"ctx": ctx_of(q % 2, x, y), "tp": (q // 2) * 2 + core})
    xp, xm, x2 = (x + 1) % 4, (x + 3) % 4, (x + 2) % 4
    yp, ym, y2 = (y + 1) % 4, (y + 3) % 4, (y + 2) % 4
    dz = {"ctx": ctx_of(zo, x, y)}
    dxp = {"ctx": ctx_of(z, xp, y)}
    dxm = {"ctx": ctx_of(z, xm, y)}
    dyp = {"ctx": ctx_of(z, x, yp)}
    dym = {"ctx": ctx_of(z, x, ym)}
    dy2 = {"ctx": ctx_of(z, x, y2)}

    table_of = {}

    def view(place):
        if isinstance(place, tuple):
            return place[0].at[place[1:]]
        return place

    def copy(name, src, dst, device):
        n = table_of.setdefault(name, len(table_of))
        return pltpu.make_async_remote_copy(
            src_ref=view(src),
            dst_ref=view(dst),
            send_sem=ssem.at[n],
            recv_sem=rsem.at[n],
            device_id=device,
            device_id_type=MESH,
        )

    makers = {}

    def start(name, src, dst, device):
        def make():
            return copy(name, src, dst, device)

        makers[name] = make
        make().start()

    def wait(*names):
        for name in names:
            makers[name]().wait_recv()

    own = z * 4 + x
    a = pl.ds(0, A_ROWS)
    a0 = pl.ds(0, A_ROWS // 2)
    a1 = pl.ds(A_ROWS // 2, A_ROWS // 2)
    nb = KV_ROWS - A_ROWS
    b = pl.ds(A_ROWS, nb)
    b0 = pl.ds(A_ROWS, nb // 2)
    b1 = pl.ds(A_ROWS + nb // 2, nb // 2)
    h0 = pl.ds(0, ROWS // 2)
    h1 = pl.ds(ROWS // 2, ROWS // 2)

    entry_barrier([dxp, dxm, dyp, dym, dy2, other] + column)

    def kv_send(name, j, rows, device):
        start(name, (kvg, j, rows), (kvg, j, rows), device)

    def kv_own(name, rows, device):
        start(name, (kv_ref, rows), (kvg, own, rows), device)

    kv_own("b_z", b, dz)
    kv_own("b_xp", b, dxp)
    kv_own("b_xm", b, dxm)
    for h in range(HEADS):
        qh[y, h * TOK : (h + 1) * TOK, :] = q_ref[:, h * HD : (h + 1) * HD]
    start("q_yp", (qh, y), (qh, y), dyp)
    start("q_ym", (qh, y), (qh, y), dym)
    kv_own("a_xp", a, dxp)
    kv_own("a_xm", a, dxm)
    kv_own("a_z", a, dz)
    kvg[own] = kv_ref[...]

    lane = lax.broadcasted_iota(jnp.int32, (1, SLOT), 1)
    for j in range(8):
        for s in range(2):
            n = lens_ref[2 * (4 * j + y) + s]
            bias[j : j + 1, s * SLOT : (s + 1) * SLOT] = jnp.where(lane < n, 0.0, lowest_score)
    top[...] = jnp.full(top.shape, lowest_score, jnp.float32)
    den[...] = jnp.zeros_like(den)
    acc[...] = jnp.zeros_like(acc)

    def first(i, j, slot):
        s = lax.dot_general(
            qh[i],
            kvg[j, 0:CH, 0:HD],
            (((1,), (1,)), ((), ())),
            preferred_element_type=jnp.float32,
        )
        s = s + bias[pl.ds(j, 1), :]
        sbuf[slot] = s
        mx[slot] = fold(jnp.maximum, s)

    def span_part(g, lanes):
        return jnp.concatenate([kvg[4 * g + k, CH:KV_ROWS, lanes] for k in range(4)], axis=0)

    def first_span(i, g, slot):
        s = lax.dot_general(
            qh[i],
            span_part(g, slice(0, HD)),
            (((1,), (1,)), ((), ())),
            preferred_element_type=jnp.float32,
        )
        parts = []
        row = lax.broadcasted_iota(jnp.int32, (TOK, TOK), 0)
        col = lax.broadcasted_iota(jnp.int32, (TOK, TOK), 1)
        for k in range(4):
            ahead = (4 * (4 * g + k) + y - 4 * own - i) * TOK
            parts.append(jnp.where(col + ahead <= row, 0.0, lowest_score))
        mask = jnp.concatenate(parts, axis=1)
        s = s + jnp.concatenate([mask] * HEADS, axis=0)
        sbuf[slot] = s
        mx[slot] = fold(jnp.maximum, s)

    def fold_in(i, slot, values):
        old = top[i]
        peak = jnp.max(mx[slot], axis=1, keepdims=True) * SCALE2
        new = jnp.maximum(old, jnp.broadcast_to(peak, (ROWS, HD)))
        factor = jnp.exp2(old - new)
        top[i] = new
        p = jnp.exp2(sbuf[slot] * SCALE2 - wide(new)).astype(jnp.bfloat16)
        both = jnp.dot(
            p,
            jnp.concatenate([values, jnp.ones_like(values)], axis=1),
            preferred_element_type=jnp.float32,
        )
        acc[i] = acc[i] * factor + both[:, 0:HD]
        den[i] = den[i] * factor + both[:, HD : 2 * HD]

    def second(i, j, slot):
        fold_in(i, slot, kvg[j, 0:CH, HD : 2 * HD])

    def second_span(i, g, slot):
        fold_in(i, slot, span_part(g, slice(HD, 2 * HD)))

    first(y, own, 0)

    wait("b_z")
    oz = zo * 4 + x
    own2, far_m, far_p, far_2 = z * 4 + x2, zo * 4 + xm, zo * 4 + xp, zo * 4 + x2
    kv_send("bz_xp", oz, b, dxp)
    kv_send("bz_xm", oz, b, dxm)
    wait("b_xp")
    kv_send("bf_xp", z * 4 + xm, b0, dxp)
    wait("b_xm")
    kv_send("bf_xm", z * 4 + xp, b1, dxm)
    wait("q_yp")
    start("qf_yp", (qh, ym, h0), (qh, ym, h0), dyp)
    wait("q_ym")
    start("qf_ym", (qh, yp, h1), (qh, yp, h1), dym)
    wait("a_xp")
    kv_send("af_xp", z * 4 + xm, a0, dxp)
    kv_send("az_m", z * 4 + xm, a, dz)
    wait("a_xm")
    kv_send("af_xm", z * 4 + xp, a1, dxm)
    kv_send("az_p", z * 4 + xp, a, dz)
    wait("a_z")

    def early(k):
        step = k % 3
        return (z + k // 3) % 2 * 4 + (x + step + step // 2) % 4

    def tile(d):
        return (y + d) % 4

    def pass_queries():
        wait("qf_yp", "qf_ym")

    def pass_b():
        wait("bz_xp")
        kv_send("bzf_xp", far_m, b0, dxp)
        wait("bz_xm")
        kv_send("bzf_xm", far_p, b1, dxm)

    def pass_a():
        wait("af_xp")
        kv_send("az_2a", own2, a0, dz)
        wait("af_xm")
        kv_send("az_2b", own2, a1, dz)

    def start_weights():
        start("w_z", w_ref, wz, dz)
        start("w_h", w_ref, wh, pair)

    points = {2: pass_queries, 3: pass_b, 5: pass_a, 6: start_weights}

    @pl.loop(0, 7)
    def _(step):
        for at, action in points.items():
            pl.when(step == at)(action)
        for u in range(2):
            n = 2 * step + u
            first(tile((n + 1) // 4), early((n + 1) % 4), 1 - u)
            second(tile(n // 4), early(n % 4), u)

    late = (own2, far_p, far_m, far_2)
    first(tile(3), early(3), 1)
    second(tile(3), early(2), 0)
    wait("bf_xp", "bf_xm", "bzf_xp", "bzf_xm", "az_m", "az_p", "az_2a", "az_2b")
    first(tile(1), late[0], 0)
    second(tile(3), early(3), 1)

    lane_t = lax.broadcasted_iota(jnp.int32, (TOK, HD), 1)
    t0 = pl.ds(0, HALF)
    t1 = pl.ds(HALF, HALF)

    def send_yp():
        start("to_p", (o4, 0), (part, 2), dyp)
        start("st_p", (st, 0), (stat, 2), dyp)

    def send_far():
        start("far_p", (o4, 1, t0), (fwd, 0), dyp)
        start("far_m", (o4, 1, t1), (fwd, 1), dym)
        start("st_2", (st, 1), (stat, 1), dy2)

    def send_ym():
        start("to_m", (o4, 2), (part, 0), dym)
        start("st_m", (st, 2), (stat, 0), dym)
        wait("far_p")
        start("fw_p", (fwd, 0), (part, 1, t0), dyp)
        wait("far_m")
        start("fw_m", (fwd, 1), (part, 1, t1), dym)

    @pl.loop(0, 4)
    def _(t):
        i = tile(t + 1)
        for k in range(3):
            first(i, late[k + 1], (k + 1) % 2)
            second(i, late[k], k % 2)
        first_span(i, 0, 0)
        second(i, late[3], 1)
        first_span(i, 1, 1)
        second_span(i, 0, 0)
        first(tile(t + 2), late[0], 0)
        second_span(i, 1, 1)
        total = den[i]
        o = acc[i] / total
        lse = top[i] + jnp.log2(total)
        packed = jnp.zeros((TOK, HD), jnp.float32)
        for h in range(HEADS):
            rows = slice(h * TOK, (h + 1) * TOK)
            o4[t, :, h * HD : (h + 1) * HD] = o[rows].astype(jnp.bfloat16)
            packed = jnp.where(lane_t == h, lse[rows], packed)
        st[t] = packed.T[0:HEADS]
        pl.when(t == 0)(send_yp)
        pl.when(t == 1)(send_far)
        pl.when(t == 2)(send_ym)

    wait("st_p", "st_m", "st_2")
    s_own = st[3]
    s_p, s_m, s_2 = stat[0], stat[2], stat[1]
    best = jnp.maximum(jnp.maximum(s_own, s_p), jnp.maximum(s_m, s_2))
    e_own = jnp.exp2(s_own - best)
    e_p = jnp.exp2(s_p - best)
    e_m = jnp.exp2(s_m - best)
    e_2 = jnp.exp2(s_2 - best)
    norm = 1.0 / (e_own + e_p + e_m + e_2)
    table[...] = jnp.concatenate(
        [e_own * norm, e_p * norm, e_m * norm, e_2 * norm, jnp.zeros((96, TOK), jnp.float32)],
        axis=0,
    ).T
    wait("to_p", "to_m", "fw_p", "fw_m")
    slot_own = x * 4 + y

    def combined(begin, dest):
        rows = pl.ds(pl.multiple_of(begin, HALF), HALF)
        for h in range(HEADS):
            lanes = slice(h * HD, (h + 1) * HD)
            out = o4[3, rows, lanes].astype(jnp.float32) * table[rows, h : h + 1]
            out += part[0, rows, lanes].astype(jnp.float32) * table[rows, 8 + h : 9 + h]
            out += part[2, rows, lanes].astype(jnp.float32) * table[rows, 16 + h : 17 + h]
            out += part[1, rows, lanes].astype(jnp.float32) * table[rows, 24 + h : 25 + h]
            dest[:, lanes] = out.astype(jnp.bfloat16)

    combined((1 - even) * HALF, away)
    start("swap", away, (att, 1, slot_own), pair)
    combined(even * HALF, att.at[0, slot_own])
    lo, hi, full = pl.ds(0, HALF // 2), pl.ds(HALF // 2, HALF // 2), pl.ds(0, HALF)

    def send(name, k, slot, rows, device):
        start(name, (att, k, slot, rows), (att, k, slot, rows), device)

    def both_y(r, xs):
        send("ayp%d" % r, 0, xs * 4 + y, full, dyp)
        send("aym%d" % r, 0, xs * 4 + y, full, dym)

    def both_x(r, ys):
        send("bxp%d" % r, 1, x * 4 + ys, full, dxp)
        send("bxm%d" % r, 1, x * 4 + ys, full, dxm)

    send("axp", 0, slot_own, full, dxp)
    send("axm", 0, slot_own, full, dxm)
    both_y(0, x)
    wait("axp")
    send("axfp", 0, xm * 4 + y, lo, dxp)
    both_y(3, xm)
    wait("axm")
    send("axfm", 0, xp * 4 + y, hi, dxm)
    both_y(1, xp)
    wait("swap")
    send("byp", 1, slot_own, full, dyp)
    send("bym", 1, slot_own, full, dym)
    both_x(0, y)
    wait("w_h")
    start("w_zh", wh, wzh, dz)

    def relay_a(r):
        xs = (x + r) % 4
        wait("ayp%d" % r)
        send("lap%d" % r, 0, xs * 4 + ym, lo, dyp)
        wait("aym%d" % r)
        send("lam%d" % r, 0, xs * 4 + yp, hi, dym)

    def relay_b(r):
        ys = (y + r) % 4
        wait("bxp%d" % r)
        send("lbp%d" % r, 1, xm * 4 + ys, lo, dxp)
        wait("bxm%d" % r)
        send("lbm%d" % r, 1, xp * 4 + ys, hi, dxm)

    def core_copy(n):
        return pltpu.make_async_remote_copy(
            src_ref=give.at[n],
            dst_ref=got.at[n],
            send_sem=core_s.at[n],
            recv_sem=core_r.at[n],
            device_id=other,
            device_id_type=MESH,
        )

    def z_copy(row, n, far):
        return pltpu.make_async_remote_copy(
            src_ref=keep.at[n, far],
            dst_ref=box.at[high],
            send_sem=z_s.at[2 * n + far],
            recv_sem=z_r.at[high],
            device_id={
                "ctx": ctx_of(zo if far else z, x, y),
                "tp": (2 * z + row // 2) * 2 + core,
            },
            device_id_type=MESH,
        )

    def product(row, n):
        keeps = row % 2 == core
        slots = pl.ds(4 * row, 4)
        rows_a = att[0, slots].reshape(BLK // 2, HEADS * HD)
        rows_b = att[1, slots].reshape(BLK // 2, HEADS * HD)
        for far, (wa, wb) in enumerate(((w_ref, wh), (wz, wzh))):
            prod[n % 2, far] = jnp.dot(
                rows_a, wa[...], preferred_element_type=jnp.float32
            ) + jnp.dot(rows_b, wb[...], preferred_element_type=jnp.float32)

        @pl.when(jnp.logical_not(keeps))
        def _():
            give[n] = prod[n % 2].astype(jnp.bfloat16)
            core_copy(n).start()

    def settle(row, n):
        keeps = row % 2 == core
        remote = 2 * z + row // 2 != high

        @pl.when(keeps)
        def _():
            core_copy(n).wait_recv()
            keep[n] = (prod[n % 2] + got[n].astype(jnp.float32)).astype(jnp.bfloat16)
            z_copy(row, n, 1).start()

            @pl.when(remote)
            def _():
                z_copy(row, n, 0).start()

            @pl.when(jnp.logical_not(remote))
            def _():
                box[high] = keep[n, 0]

    relay_a(0)
    wait("byp")
    send("byfp", 1, x * 4 + ym, lo, dyp)
    both_x(3, ym)
    wait("bym")
    send("byfm", 1, x * 4 + yp, hi, dym)
    both_x(1, yp)
    wait("axfp", "axfm")
    both_y(2, x2)
    relay_a(3)
    relay_b(0)
    wait("byfp", "byfm")
    both_x(2, y2)
    wait("lap0", "lam0", "w_z", "w_zh")
    product(x, 0)
    relay_a(1)
    settle(x, 0)
    relay_b(3)
    relay_b(1)
    relay_a(2)
    relay_b(2)
    wait("lap3", "lam3")
    product(xm, 1)
    settle(xm, 1)
    wait("lap1", "lam1")
    product(xp, 2)
    settle(xp, 2)
    wait("lap2", "lam2")
    for r in range(4):
        wait("lbp%d" % r, "lbm%d" % r)
    product(x2, 3)
    settle(x2, 3)

    source_z = high // 2
    for s in range(4):
        arrives = jnp.logical_or(high != s, z != source_z)

        @pl.when(arrives)
        def _(s=s):
            pltpu.make_async_remote_copy(
                src_ref=keep.at[0, 0],
                dst_ref=box.at[s],
                send_sem=z_s.at[0],
                recv_sem=z_r.at[s],
                device_id=other,
                device_id_type=MESH,
            ).wait_recv()

    for e in range(2):
        total = box[e].astype(jnp.float32) + box[2 + e].astype(jnp.float32)
        total = total.astype(jnp.bfloat16)
        for g in range(4):
            begin = g * TOK + e * HALF
            out_ref[begin : begin + HALF] = total[g * HALF : (g + 1) * HALF]
    for n, row in enumerate((x, xm, xp, x2)):
        keeps = row % 2 == core
        remote = 2 * z + row // 2 != high

        @pl.when(keeps)
        def _(n=n, row=row, remote=remote):
            z_copy(row, n, 1).wait_send()

            @pl.when(remote)
            def _():
                z_copy(row, n, 0).wait_send()

        @pl.when(jnp.logical_not(keeps))
        def _(n=n):
            core_copy(n).wait_send()

    for make in makers.values():
        make().wait_send()


def fused(lengths, q, kv, w):
    bf16, f32 = jnp.bfloat16, jnp.float32
    return pl.pallas_call(
        fused_kernel,
        name="attention_block",
        out_shape=jax.ShapeDtypeStruct((BLK, COLS), bf16),
        in_specs=[pl.BlockSpec(memory_space=pltpu.SMEM)]
        + [pl.BlockSpec(memory_space=pltpu.VMEM)] * 3,
        out_specs=pl.BlockSpec(memory_space=pltpu.VMEM),
        scratch_shapes=[
            pltpu.VMEM((4, ROWS, HD), bf16),
            pltpu.VMEM((8, KV_ROWS, 2 * HD), bf16),
            pltpu.VMEM((8, CH), f32),
            pltpu.VMEM((2, ROWS, CH), f32),
            pltpu.VMEM((2, ROWS, HD), f32),
            pltpu.VMEM((4, ROWS, HD), f32),
            pltpu.VMEM((4, ROWS, HD), f32),
            pltpu.VMEM((4, ROWS, HD), f32),
            pltpu.VMEM((4, TOK, HEADS * HD), bf16),
            pltpu.VMEM((4, HEADS, TOK), f32),
            pltpu.VMEM((3, TOK, HEADS * HD), bf16),
            pltpu.VMEM((3, HEADS, TOK), f32),
            pltpu.VMEM((TOK, TOK), f32),
            pltpu.VMEM((2, HALF, HEADS * HD), bf16),
            pltpu.VMEM((HALF, HEADS * HD), bf16),
            pltpu.VMEM((HEADS * HD, COLS), bf16),
            pltpu.VMEM((HEADS * HD, COLS), bf16),
            pltpu.VMEM((HEADS * HD, COLS), bf16),
            pltpu.VMEM((2, 16, HALF, HEADS * HD), bf16),
            pltpu.VMEM((2, 2, BLK // 2, COLS), f32),
            pltpu.VMEM((4, 2, BLK // 2, COLS), bf16),
            pltpu.VMEM((4, 2, BLK // 2, COLS), bf16),
            pltpu.VMEM((4, 2, BLK // 2, COLS), bf16),
            pltpu.VMEM((4, BLK // 2, COLS), bf16),
            pltpu.SemaphoreType.DMA((COPIES,)),
            pltpu.SemaphoreType.DMA((COPIES,)),
            pltpu.SemaphoreType.DMA((4,)),
            pltpu.SemaphoreType.DMA((4,)),
            pltpu.SemaphoreType.DMA((8,)),
            pltpu.SemaphoreType.DMA((4,)),
        ],
        compiler_params=pltpu.CompilerParams(
            collective_id=0, has_side_effects=True, vmem_limit_bytes=48 << 20
        ),
    )(lengths, q, kv, w)


def body(queries, span_kv, cache_kv, out_weight, offset, lengths):
    first_token = lax.axis_index("ctx") * TOK
    positions = offset[0] + first_token + jnp.arange(TOK, dtype=jnp.int32)
    rotated = rotate(queries.reshape(TOK, HEADS, HD).astype(jnp.float32), positions)
    rotated = rotated.astype(jnp.bfloat16).reshape(TOK, HEADS * HD)
    keys = rotate(span_kv[:, :, 0, :].astype(jnp.float32), positions).astype(jnp.bfloat16)
    span = jnp.concatenate([keys[:, 0, :], span_kv[:, 0, 1, :]], axis=1)
    kv = jnp.concatenate([cache_kv.reshape(CH, 2 * HD), span], axis=0)
    return fused(lengths, rotated, kv, out_weight)


def solution(mesh):
    return jax.shard_map(
        body,
        mesh=mesh,
        in_specs=(
            P("ctx", "tp"),
            P("ctx", "tp", None, None),
            P("ctx", "tp", None, None),
            P("tp", "ctx"),
            P(),
            P(),
        ),
        out_specs=P("tp", "ctx"),
        check_vma=False,
    )
```

```python
import math

import jax
import jax.numpy as jnp
from jax import lax
from jax.experimental import pallas as pl
from jax.experimental.pallas import tpu as pltpu
from jax.sharding import PartitionSpec as P

SLOT = 256
HD = 128
TOK = 128
HEADS = 8
KV_ROWS = 640
CH = 512
A_ROWS = 256
ROWS = HEADS * TOK
BLK = 512
COLS = 256
HALF = TOK // 2
WP = 128
COPIES = 80
lowest_score = -1e30
rope_base = 500000.0
MESH = pl.DeviceIdType.MESH
SCALE2 = math.log2(math.e) / math.sqrt(HD)


def rotate(values, positions):
    head_size = values.shape[-1]
    half_dim = head_size // 2
    frequency = jnp.exp(
        jnp.arange(half_dim, dtype=jnp.float32) * (-2.0 * math.log(rope_base) / head_size)
    )
    angles = positions.astype(jnp.float32)[:, None] * frequency[None, :]
    cosine = jnp.cos(angles)[:, None, :]
    sine_part = jnp.sin(angles)[:, None, :]
    first_half = values[..., :half_dim]
    second_half = values[..., half_dim:]
    return jnp.concatenate(
        [
            first_half * cosine - second_half * sine_part,
            second_half * cosine + first_half * sine_part,
        ],
        axis=-1,
    )


def coords():
    c = lax.axis_index("ctx")
    z = c // 16
    x = (c // 4) % 4
    y = c % 4
    return z, x, y


def ctx_of(z, x, y):
    return z * 16 + x * 4 + y


def entry_barrier(devices):
    barrier = pltpu.get_barrier_semaphore()
    for d in devices:
        pl.semaphore_signal(barrier, inc=1, device_id=d, device_id_type=MESH)
    pl.semaphore_wait(barrier, len(devices))


def fold(op, values):
    out = values[:, 0:HD]
    for n in range(1, values.shape[1] // HD):
        out = op(out, values[:, n * HD : (n + 1) * HD])
    return out


def wide(values):
    return jnp.concatenate([values] * (CH // HD), axis=1)


def fused_kernel(
    lens_ref,
    q_ref,
    kv_ref,
    w_ref,
    out_ref,
    qh,
    kvg,
    bias,
    sbuf,
    mx,
    top,
    den,
    acc,
    o4,
    st,
    part,
    stat,
    table,
    fwd,
    away,
    wz,
    wh,
    wzh,
    att,
    prod,
    give,
    got,
    keep,
    box,
    ssem,
    rsem,
    w_s,
    w_r,
    core_s,
    core_r,
    z_s,
    z_r,
):
    z, x, y = coords()
    tp = lax.axis_index("tp")
    core = tp % 2
    high = tp // 2
    even = high % 2
    zo = 1 - z
    other = {"tp": tp + 1 - 2 * core}
    pair = {"tp": tp + 2 - 4 * even}
    pos = 2 * high + z
    column = []
    for d in range(1, 8):
        q = (pos + d) % 8
        column.append({"ctx": ctx_of(q % 2, x, y), "tp": (q // 2) * 2 + core})
    xp, xm, x2 = (x + 1) % 4, (x + 3) % 4, (x + 2) % 4
    yp, ym, y2 = (y + 1) % 4, (y + 3) % 4, (y + 2) % 4
    dz = {"ctx": ctx_of(zo, x, y)}
    dxp = {"ctx": ctx_of(z, xp, y)}
    dxm = {"ctx": ctx_of(z, xm, y)}
    dyp = {"ctx": ctx_of(z, x, yp)}
    dym = {"ctx": ctx_of(z, x, ym)}
    dy2 = {"ctx": ctx_of(z, x, y2)}

    table_of = {}

    def view(place):
        if isinstance(place, tuple):
            return place[0].at[place[1:]]
        return place

    def copy(name, src, dst, device):
        n = table_of.setdefault(name, len(table_of))
        return pltpu.make_async_remote_copy(
            src_ref=view(src),
            dst_ref=view(dst),
            send_sem=ssem.at[n],
            recv_sem=rsem.at[n],
            device_id=device,
            device_id_type=MESH,
        )

    makers = {}

    def start(name, src, dst, device):
        def make():
            return copy(name, src, dst, device)

        makers[name] = make
        make().start()

    def wait(*names):
        for name in names:
            makers[name]().wait_recv()

    own = z * 4 + x
    a = pl.ds(0, A_ROWS)
    a0 = pl.ds(0, A_ROWS // 2)
    a1 = pl.ds(A_ROWS // 2, A_ROWS // 2)
    nb = KV_ROWS - A_ROWS
    b = pl.ds(A_ROWS, nb)
    b0 = pl.ds(A_ROWS, nb // 2)
    b1 = pl.ds(A_ROWS + nb // 2, nb // 2)
    h0 = pl.ds(0, ROWS // 2)
    h1 = pl.ds(ROWS // 2, ROWS // 2)

    entry_barrier([dxp, dxm, dyp, dym, dy2, other] + column)

    def kv_send(name, j, rows, device):
        start(name, (kvg, j, rows), (kvg, j, rows), device)

    def kv_own(name, rows, device):
        start(name, (kv_ref, rows), (kvg, own, rows), device)

    kv_own("b_z", b, dz)
    kv_own("b_xp", b, dxp)
    kv_own("b_xm", b, dxm)
    for h in range(HEADS):
        qh[y, h * TOK : (h + 1) * TOK, :] = q_ref[:, h * HD : (h + 1) * HD]
    start("q_yp", (qh, y), (qh, y), dyp)
    start("q_ym", (qh, y), (qh, y), dym)
    kv_own("a_xp", a, dxp)
    kv_own("a_xm", a, dxm)
    kv_own("a_z", a, dz)
    kvg[own] = kv_ref[...]

    lane = lax.broadcasted_iota(jnp.int32, (1, SLOT), 1)
    for j in range(8):
        for s in range(2):
            n = lens_ref[2 * (4 * j + y) + s]
            bias[j : j + 1, s * SLOT : (s + 1) * SLOT] = jnp.where(lane < n, 0.0, lowest_score)
    top[...] = jnp.full(top.shape, lowest_score, jnp.float32)
    den[...] = jnp.zeros_like(den)
    acc[...] = jnp.zeros_like(acc)

    def first(i, j, slot):
        s = lax.dot_general(
            qh[i],
            kvg[j, 0:CH, 0:HD],
            (((1,), (1,)), ((), ())),
            preferred_element_type=jnp.float32,
        )
        s = s + bias[pl.ds(j, 1), :]
        sbuf[slot] = s
        mx[slot] = fold(jnp.maximum, s)

    def span_part(g, lanes):
        return jnp.concatenate([kvg[4 * g + k, CH:KV_ROWS, lanes] for k in range(4)], axis=0)

    def first_span(i, g, slot):
        s = lax.dot_general(
            qh[i],
            span_part(g, slice(0, HD)),
            (((1,), (1,)), ((), ())),
            preferred_element_type=jnp.float32,
        )
        parts = []
        row = lax.broadcasted_iota(jnp.int32, (TOK, TOK), 0)
        col = lax.broadcasted_iota(jnp.int32, (TOK, TOK), 1)
        for k in range(4):
            ahead = (4 * (4 * g + k) + y - 4 * own - i) * TOK
            parts.append(jnp.where(col + ahead <= row, 0.0, lowest_score))
        mask = jnp.concatenate(parts, axis=1)
        s = s + jnp.concatenate([mask] * HEADS, axis=0)
        sbuf[slot] = s
        mx[slot] = fold(jnp.maximum, s)

    def fold_in(i, slot, values):
        old = top[i]
        peak = jnp.max(mx[slot], axis=1, keepdims=True) * SCALE2
        new = jnp.maximum(old, jnp.broadcast_to(peak, (ROWS, HD)))
        factor = jnp.exp2(old - new)
        top[i] = new
        p = jnp.exp2(sbuf[slot] * SCALE2 - wide(new)).astype(jnp.bfloat16)
        both = jnp.dot(
            p,
            jnp.concatenate([values, jnp.ones_like(values)], axis=1),
            preferred_element_type=jnp.float32,
        )
        acc[i] = acc[i] * factor + both[:, 0:HD]
        den[i] = den[i] * factor + both[:, HD : 2 * HD]

    def second(i, j, slot):
        fold_in(i, slot, kvg[j, 0:CH, HD : 2 * HD])

    def second_span(i, g, slot):
        fold_in(i, slot, span_part(g, slice(HD, 2 * HD)))

    first(y, own, 0)

    oz = zo * 4 + x
    own2, far_m, far_p, far_2 = z * 4 + x2, zo * 4 + xm, zo * 4 + xp, zo * 4 + x2
    own_m, own_p = z * 4 + xm, z * 4 + xp
    wait("b_z", "b_xp", "b_xm", "a_xp", "a_xm", "a_z")
    kv_send("bz_xp", oz, b, dxp)
    kv_send("bz_xm", oz, b, dxm)
    kv_send("az_m", own_m, a, dz)
    kv_send("az_p", own_p, a, dz)
    kv_send("bf_xp", own_m, b0, dxp)
    kv_send("bf_xm", own_p, b1, dxm)
    kv_send("af_xp", own_m, a0, dxp)
    kv_send("af_xm", own_p, a1, dxm)

    def early(k):
        step = k % 3
        return (z + k // 3) % 2 * 4 + (x + step + step // 2) % 4

    def tile(d):
        return (y + d) % 4

    def pass_queries():
        wait("q_yp")
        start("qf_yp", (qh, ym, h0), (qh, ym, h0), dyp)
        wait("q_ym")
        start("qf_ym", (qh, yp, h1), (qh, yp, h1), dym)

    def wait_queries():
        wait("qf_yp", "qf_ym")

    def pass_b():
        wait("bz_xp")
        kv_send("bzf_xp", far_m, b0, dxp)
        wait("bz_xm")
        kv_send("bzf_xm", far_p, b1, dxm)

    def pass_a():
        wait("af_xp")
        kv_send("az_2a", own2, a0, dz)
        wait("af_xm")
        kv_send("az_2b", own2, a1, dz)

    points = {0: pass_queries, 3: wait_queries, 4: pass_b, 5: pass_a}

    @pl.loop(0, 7)
    def _(step):
        for at, action in points.items():
            pl.when(step == at)(action)
        for u in range(2):
            n = 2 * step + u
            first(tile((n + 1) // 4), early((n + 1) % 4), 1 - u)
            second(tile(n // 4), early(n % 4), u)

    late = (own2, far_p, far_m, far_2)
    first(tile(3), early(3), 1)
    second(tile(3), early(2), 0)
    wait("bf_xp", "bf_xm", "bzf_xp", "bzf_xm", "az_m", "az_p", "az_2a", "az_2b")
    first(tile(1), late[0], 0)
    second(tile(3), early(3), 1)

    def piece(kind, c):
        src, dst, device = ((w_ref, wh, pair), (w_ref, wz, dz), (wh, wzh, dz))[kind]
        rows = pl.ds(pl.multiple_of(c * WP, WP), WP)
        return pltpu.make_async_remote_copy(
            src_ref=src.at[rows],
            dst_ref=dst.at[rows],
            send_sem=w_s.at[kind, c],
            recv_sem=w_r.at[kind, c],
            device_id=device,
            device_id_type=MESH,
        )

    def send_piece(n):
        c = n % 8

        @pl.when(n // 8 == 0)
        def _():
            piece(0, c).start()

        @pl.when(n // 8 == 1)
        def _():
            piece(1, c).start()

        @pl.when(n // 8 == 2)
        def _():
            piece(0, c).wait_recv()
            piece(2, c).start()

    lane_t = lax.broadcasted_iota(jnp.int32, (TOK, HD), 1)
    t0 = pl.ds(0, HALF)
    t1 = pl.ds(HALF, HALF)

    def send_yp():
        start("to_p", (o4, 0), (part, 2), dyp)
        start("st_p", (st, 0), (stat, 2), dyp)

    def send_far():
        start("far_p", (o4, 1, t0), (fwd, 0), dyp)
        start("far_m", (o4, 1, t1), (fwd, 1), dym)
        start("st_2", (st, 1), (stat, 1), dy2)

    def send_ym():
        start("to_m", (o4, 2), (part, 0), dym)
        start("st_m", (st, 2), (stat, 0), dym)
        wait("far_p")
        start("fw_p", (fwd, 0), (part, 1, t0), dyp)
        wait("far_m")
        start("fw_m", (fwd, 1), (part, 1, t1), dym)

    @pl.loop(0, 4)
    def _(t):
        i = tile(t + 1)
        for k in range(3):
            send_piece(6 * t + k)
            first(i, late[k + 1], (k + 1) % 2)
            second(i, late[k], k % 2)
        send_piece(6 * t + 3)
        first_span(i, 0, 0)
        second(i, late[3], 1)
        send_piece(6 * t + 4)
        first_span(i, 1, 1)
        second_span(i, 0, 0)
        send_piece(6 * t + 5)
        first(tile(t + 2), late[0], 0)
        second_span(i, 1, 1)
        total = den[i]
        o = acc[i] / total
        lse = top[i] + jnp.log2(total)
        packed = jnp.zeros((TOK, HD), jnp.float32)
        for h in range(HEADS):
            rows = slice(h * TOK, (h + 1) * TOK)
            o4[t, :, h * HD : (h + 1) * HD] = o[rows].astype(jnp.bfloat16)
            packed = jnp.where(lane_t == h, lse[rows], packed)
        st[t] = packed.T[0:HEADS]
        pl.when(t == 0)(send_yp)
        pl.when(t == 1)(send_far)
        pl.when(t == 2)(send_ym)

    wait("st_p", "st_m", "st_2")
    s_own = st[3]
    s_p, s_m, s_2 = stat[0], stat[2], stat[1]
    best = jnp.maximum(jnp.maximum(s_own, s_p), jnp.maximum(s_m, s_2))
    e_own = jnp.exp2(s_own - best)
    e_p = jnp.exp2(s_p - best)
    e_m = jnp.exp2(s_m - best)
    e_2 = jnp.exp2(s_2 - best)
    norm = 1.0 / (e_own + e_p + e_m + e_2)
    table[...] = jnp.concatenate(
        [e_own * norm, e_p * norm, e_m * norm, e_2 * norm, jnp.zeros((96, TOK), jnp.float32)],
        axis=0,
    ).T
    wait("to_p", "to_m", "fw_p", "fw_m")
    slot_own = x * 4 + y

    def combined(begin, dest):
        rows = pl.ds(pl.multiple_of(begin, HALF), HALF)
        for h in range(HEADS):
            lanes = slice(h * HD, (h + 1) * HD)
            out = o4[3, rows, lanes].astype(jnp.float32) * table[rows, h : h + 1]
            out += part[0, rows, lanes].astype(jnp.float32) * table[rows, 8 + h : 9 + h]
            out += part[2, rows, lanes].astype(jnp.float32) * table[rows, 16 + h : 17 + h]
            out += part[1, rows, lanes].astype(jnp.float32) * table[rows, 24 + h : 25 + h]
            dest[:, lanes] = out.astype(jnp.bfloat16)

    combined((1 - even) * HALF, away)
    start("swap", away, (att, 1, slot_own), pair)
    combined(even * HALF, att.at[0, slot_own])
    lo, hi, full = pl.ds(0, HALF // 2), pl.ds(HALF // 2, HALF // 2), pl.ds(0, HALF)

    def send(name, k, slot, rows, device):
        start(name, (att, k, slot, rows), (att, k, slot, rows), device)

    def both_y(r, xs):
        send("ayp%d" % r, 0, xs * 4 + y, full, dyp)
        send("aym%d" % r, 0, xs * 4 + y, full, dym)

    def both_x(r, ys):
        send("bxp%d" % r, 1, x * 4 + ys, full, dxp)
        send("bxm%d" % r, 1, x * 4 + ys, full, dxm)

    send("axp", 0, slot_own, full, dxp)
    send("axm", 0, slot_own, full, dxm)
    both_y(0, x)
    wait("axp")
    send("axfp", 0, xm * 4 + y, lo, dxp)
    both_y(3, xm)
    wait("axm")
    send("axfm", 0, xp * 4 + y, hi, dxm)
    both_y(1, xp)
    wait("swap")
    send("byp", 1, slot_own, full, dyp)
    send("bym", 1, slot_own, full, dym)
    both_x(0, y)

    def relay_a(r):
        xs = (x + r) % 4
        wait("ayp%d" % r)
        send("lap%d" % r, 0, xs * 4 + ym, lo, dyp)
        wait("aym%d" % r)
        send("lam%d" % r, 0, xs * 4 + yp, hi, dym)

    def relay_b(r):
        ys = (y + r) % 4
        wait("bxp%d" % r)
        send("lbp%d" % r, 1, xm * 4 + ys, lo, dxp)
        wait("bxm%d" % r)
        send("lbm%d" % r, 1, xp * 4 + ys, hi, dxm)

    def core_copy(n):
        return pltpu.make_async_remote_copy(
            src_ref=give.at[n],
            dst_ref=got.at[n],
            send_sem=core_s.at[n],
            recv_sem=core_r.at[n],
            device_id=other,
            device_id_type=MESH,
        )

    def z_copy(row, n, far):
        return pltpu.make_async_remote_copy(
            src_ref=keep.at[n, far],
            dst_ref=box.at[high],
            send_sem=z_s.at[2 * n + far],
            recv_sem=z_r.at[high],
            device_id={
                "ctx": ctx_of(zo if far else z, x, y),
                "tp": (2 * z + row // 2) * 2 + core,
            },
            device_id_type=MESH,
        )

    def product(row, n):
        keeps = row % 2 == core
        slots = pl.ds(4 * row, 4)
        rows_a = att[0, slots].reshape(BLK // 2, HEADS * HD)
        rows_b = att[1, slots].reshape(BLK // 2, HEADS * HD)
        for far, (wa, wb) in enumerate(((w_ref, wh), (wz, wzh))):
            prod[n % 2, far] = jnp.dot(
                rows_a, wa[...], preferred_element_type=jnp.float32
            ) + jnp.dot(rows_b, wb[...], preferred_element_type=jnp.float32)

        @pl.when(jnp.logical_not(keeps))
        def _():
            give[n] = prod[n % 2].astype(jnp.bfloat16)
            core_copy(n).start()

    def settle(row, n):
        keeps = row % 2 == core
        remote = 2 * z + row // 2 != high

        @pl.when(keeps)
        def _():
            core_copy(n).wait_recv()
            keep[n] = (prod[n % 2] + got[n].astype(jnp.float32)).astype(jnp.bfloat16)
            z_copy(row, n, 1).start()

            @pl.when(remote)
            def _():
                z_copy(row, n, 0).start()

            @pl.when(jnp.logical_not(remote))
            def _():
                box[high] = keep[n, 0]

    relay_a(0)
    wait("byp")
    send("byfp", 1, x * 4 + ym, lo, dyp)
    both_x(3, ym)
    wait("bym")
    send("byfm", 1, x * 4 + yp, hi, dym)
    both_x(1, yp)
    wait("axfp", "axfm")
    both_y(2, x2)
    relay_a(3)
    relay_b(0)
    wait("byfp", "byfm")
    both_x(2, y2)
    wait("lap0", "lam0")
    for c in range(8):
        piece(1, c).wait_recv()
        piece(2, c).wait_recv()
    product(x, 0)
    relay_a(1)
    settle(x, 0)
    relay_b(3)
    relay_b(1)
    relay_a(2)
    relay_b(2)
    wait("lap3", "lam3")
    product(xm, 1)
    settle(xm, 1)
    wait("lap1", "lam1")
    product(xp, 2)
    settle(xp, 2)
    wait("lap2", "lam2")
    for r in range(4):
        wait("lbp%d" % r, "lbm%d" % r)
    product(x2, 3)
    settle(x2, 3)

    source_z = high // 2
    for s in range(4):
        arrives = jnp.logical_or(high != s, z != source_z)

        @pl.when(arrives)
        def _(s=s):
            pltpu.make_async_remote_copy(
                src_ref=keep.at[0, 0],
                dst_ref=box.at[s],
                send_sem=z_s.at[0],
                recv_sem=z_r.at[s],
                device_id=other,
                device_id_type=MESH,
            ).wait_recv()

    for e in range(2):
        total = box[e].astype(jnp.float32) + box[2 + e].astype(jnp.float32)
        total = total.astype(jnp.bfloat16)
        for g in range(4):
            begin = g * TOK + e * HALF
            out_ref[begin : begin + HALF] = total[g * HALF : (g + 1) * HALF]
    for n, row in enumerate((x, xm, xp, x2)):
        keeps = row % 2 == core
        remote = 2 * z + row // 2 != high

        @pl.when(keeps)
        def _(n=n, row=row, remote=remote):
            z_copy(row, n, 1).wait_send()

            @pl.when(remote)
            def _():
                z_copy(row, n, 0).wait_send()

        @pl.when(jnp.logical_not(keeps))
        def _(n=n):
            core_copy(n).wait_send()

    for make in makers.values():
        make().wait_send()
    for kind in range(3):
        for c in range(8):
            piece(kind, c).wait_send()


def fused(lengths, q, kv, w):
    bf16, f32 = jnp.bfloat16, jnp.float32
    return pl.pallas_call(
        fused_kernel,
        name="attention_block",
        out_shape=jax.ShapeDtypeStruct((BLK, COLS), bf16),
        in_specs=[pl.BlockSpec(memory_space=pltpu.SMEM)]
        + [pl.BlockSpec(memory_space=pltpu.VMEM)] * 3,
        out_specs=pl.BlockSpec(memory_space=pltpu.VMEM),
        scratch_shapes=[
            pltpu.VMEM((4, ROWS, HD), bf16),
            pltpu.VMEM((8, KV_ROWS, 2 * HD), bf16),
            pltpu.VMEM((8, CH), f32),
            pltpu.VMEM((2, ROWS, CH), f32),
            pltpu.VMEM((2, ROWS, HD), f32),
            pltpu.VMEM((4, ROWS, HD), f32),
            pltpu.VMEM((4, ROWS, HD), f32),
            pltpu.VMEM((4, ROWS, HD), f32),
            pltpu.VMEM((4, TOK, HEADS * HD), bf16),
            pltpu.VMEM((4, HEADS, TOK), f32),
            pltpu.VMEM((3, TOK, HEADS * HD), bf16),
            pltpu.VMEM((3, HEADS, TOK), f32),
            pltpu.VMEM((TOK, TOK), f32),
            pltpu.VMEM((2, HALF, HEADS * HD), bf16),
            pltpu.VMEM((HALF, HEADS * HD), bf16),
            pltpu.VMEM((HEADS * HD, COLS), bf16),
            pltpu.VMEM((HEADS * HD, COLS), bf16),
            pltpu.VMEM((HEADS * HD, COLS), bf16),
            pltpu.VMEM((2, 16, HALF, HEADS * HD), bf16),
            pltpu.VMEM((2, 2, BLK // 2, COLS), f32),
            pltpu.VMEM((4, 2, BLK // 2, COLS), bf16),
            pltpu.VMEM((4, 2, BLK // 2, COLS), bf16),
            pltpu.VMEM((4, 2, BLK // 2, COLS), bf16),
            pltpu.VMEM((4, BLK // 2, COLS), bf16),
            pltpu.SemaphoreType.DMA((COPIES,)),
            pltpu.SemaphoreType.DMA((COPIES,)),
            pltpu.SemaphoreType.DMA((3, 8)),
            pltpu.SemaphoreType.DMA((3, 8)),
            pltpu.SemaphoreType.DMA((4,)),
            pltpu.SemaphoreType.DMA((4,)),
            pltpu.SemaphoreType.DMA((8,)),
            pltpu.SemaphoreType.DMA((4,)),
        ],
        compiler_params=pltpu.CompilerParams(
            collective_id=0, has_side_effects=True, vmem_limit_bytes=48 << 20
        ),
    )(lengths, q, kv, w)


def body(queries, span_kv, cache_kv, out_weight, offset, lengths):
    first_token = lax.axis_index("ctx") * TOK
    positions = offset[0] + first_token + jnp.arange(TOK, dtype=jnp.int32)
    rotated = rotate(queries.reshape(TOK, HEADS, HD).astype(jnp.float32), positions)
    rotated = rotated.astype(jnp.bfloat16).reshape(TOK, HEADS * HD)
    keys = rotate(span_kv[:, :, 0, :].astype(jnp.float32), positions).astype(jnp.bfloat16)
    span = jnp.concatenate([keys[:, 0, :], span_kv[:, 0, 1, :]], axis=1)
    kv = jnp.concatenate([cache_kv.reshape(CH, 2 * HD), span], axis=0)
    return fused(lengths, rotated, kv, out_weight)


def solution(mesh):
    return jax.shard_map(
        body,
        mesh=mesh,
        in_specs=(
            P("ctx", "tp"),
            P("ctx", "tp", None, None),
            P("ctx", "tp", None, None),
            P("tp", "ctx"),
            P(),
            P(),
        ),
        out_specs=P("tp", "ctx"),
        check_vma=False,
    )
```

```python
import math

import jax
import jax.numpy as jnp
from jax import lax
from jax.experimental import pallas as pl
from jax.experimental.pallas import tpu as pltpu
from jax.sharding import PartitionSpec as P

SLOT = 256
HD = 128
TOK = 128
HEADS = 8
KV_ROWS = 640
CH = 512
A_ROWS = 256
ROWS = HEADS * TOK
BLK = 512
COLS = 256
HALF = TOK // 2
WP = 256
COPIES = 72
lowest_score = -1e30
rope_base = 500000.0
MESH = pl.DeviceIdType.MESH
SCALE2 = math.log2(math.e) / math.sqrt(HD)


def rotary_tables(positions):
    half = HD // 2
    frequency = jnp.exp(
        jnp.arange(half, dtype=jnp.float32) * (-2.0 * math.log(rope_base) / HD)
    )
    angles = positions.astype(jnp.float32)[:, None] * frequency[None, :]
    cosine, sine = jnp.cos(angles), jnp.sin(angles)
    return jnp.concatenate([cosine, cosine], axis=1), jnp.concatenate([-sine, sine], axis=1)


def coords():
    c = lax.axis_index("ctx")
    z = c // 16
    x = (c // 4) % 4
    y = c % 4
    return z, x, y


def ctx_of(z, x, y):
    return z * 16 + x * 4 + y


def entry_barrier(devices):
    barrier = pltpu.get_barrier_semaphore()
    for d in devices:
        pl.semaphore_signal(barrier, inc=1, device_id=d, device_id_type=MESH)
    pl.semaphore_wait(barrier, len(devices))


def fold(op, values):
    out = values[:, 0:HD]
    for n in range(1, values.shape[1] // HD):
        out = op(out, values[:, n * HD : (n + 1) * HD])
    return out


def wide(values):
    return jnp.concatenate([values] * (CH // HD), axis=1)


def fused_kernel(
    lens_ref,
    q_ref,
    cache_ref,
    span_ref,
    cos_ref,
    sin_ref,
    w_hbm,
    out_ref,
    w_ref,
    qh,
    kvg,
    bias,
    sbuf,
    mx,
    top,
    den,
    acc,
    o4,
    st,
    part,
    stat,
    table,
    fwd,
    away,
    wz,
    wh,
    wzh,
    att,
    prod,
    give,
    got,
    keep,
    box,
    ssem,
    rsem,
    w_s,
    w_r,
    w_local,
    near,
    core_s,
    core_r,
    z_s,
    z_r,
):
    z, x, y = coords()
    tp = lax.axis_index("tp")
    core = tp % 2
    high = tp // 2
    even = high % 2
    zo = 1 - z
    other = {"tp": tp + 1 - 2 * core}
    pair = {"tp": tp + 2 - 4 * even}
    pos = 2 * high + z
    column = []
    for d in range(1, 8):
        q = (pos + d) % 8
        column.append({"ctx": ctx_of(q % 2, x, y), "tp": (q // 2) * 2 + core})
    xp, xm, x2 = (x + 1) % 4, (x + 3) % 4, (x + 2) % 4
    yp, ym, y2 = (y + 1) % 4, (y + 3) % 4, (y + 2) % 4
    dz = {"ctx": ctx_of(zo, x, y)}
    dxp = {"ctx": ctx_of(z, xp, y)}
    dxm = {"ctx": ctx_of(z, xm, y)}
    dyp = {"ctx": ctx_of(z, x, yp)}
    dym = {"ctx": ctx_of(z, x, ym)}
    dy2 = {"ctx": ctx_of(z, x, y2)}

    table_of = {}

    def view(place):
        if isinstance(place, tuple):
            return place[0].at[place[1:]]
        return place

    def copy(name, src, dst, device):
        n = table_of.setdefault(name, len(table_of))
        return pltpu.make_async_remote_copy(
            src_ref=view(src),
            dst_ref=view(dst),
            send_sem=ssem.at[n],
            recv_sem=rsem.at[n],
            device_id=device,
            device_id_type=MESH,
        )

    makers = {}

    def start(name, src, dst, device):
        def make():
            return copy(name, src, dst, device)

        makers[name] = make
        make().start()

    def wait(*names):
        for name in names:
            makers[name]().wait_recv()

    own = z * 4 + x
    a = pl.ds(0, A_ROWS)
    a0 = pl.ds(0, A_ROWS // 2)
    a1 = pl.ds(A_ROWS // 2, A_ROWS // 2)
    nb = KV_ROWS - A_ROWS
    b = pl.ds(A_ROWS, nb)
    b0 = pl.ds(A_ROWS, nb // 2)
    b1 = pl.ds(A_ROWS + nb // 2, nb // 2)
    h0 = pl.ds(0, ROWS // 2)
    h1 = pl.ds(ROWS // 2, ROWS // 2)

    next_z, last_z = column[0], column[6]
    entry_barrier([dxp, dxm, dyp, dym, other, next_z, last_z])

    def near_signal(r):
        for device in (next_z, last_z):
            pl.semaphore_signal(near.at[r], inc=1, device_id=device, device_id_type=MESH)

    def near_wait(r):
        pl.semaphore_wait(near.at[r], 2)

    near_signal(0)

    def kv_send(name, j, rows, device):
        start(name, (kvg, j, rows), (kvg, j, rows), device)

    def rotated(values):
        values = values.astype(jnp.float32)
        turned = jnp.concatenate([values[:, HD // 2 :], values[:, : HD // 2]], axis=1)
        return (values * cos_ref[...] + turned * sin_ref[...]).astype(jnp.bfloat16)

    def kv_own(name, rows, device):
        kv_send(name, own, rows, device)

    kvg[own, 0:CH] = cache_ref[...]
    kvg[own, CH:KV_ROWS, 0:HD] = rotated(span_ref[:, 0:HD])
    kvg[own, CH:KV_ROWS, HD : 2 * HD] = span_ref[:, HD : 2 * HD]
    kv_own("b_z", b, dz)
    kv_own("b_xp", b, dxp)
    kv_own("b_xm", b, dxm)
    for h in range(HEADS):
        qh[y, h * TOK : (h + 1) * TOK, :] = rotated(q_ref[:, h * HD : (h + 1) * HD])
    start("q_yp", (qh, y), (qh, y), dyp)
    start("q_ym", (qh, y), (qh, y), dym)
    kv_own("a_xp", a, dxp)
    kv_own("a_xm", a, dxm)
    kv_own("a_z", a, dz)
    weights_here = pltpu.make_async_copy(w_hbm, w_ref, w_local)
    weights_here.start()

    lane = lax.broadcasted_iota(jnp.int32, (1, SLOT), 1)
    for j in range(8):
        for s in range(2):
            n = lens_ref[2 * (4 * j + y) + s]
            bias[j : j + 1, s * SLOT : (s + 1) * SLOT] = jnp.where(lane < n, 0.0, lowest_score)
    top[...] = jnp.full(top.shape, lowest_score, jnp.float32)
    den[...] = jnp.zeros_like(den)
    acc[...] = jnp.zeros_like(acc)

    def first(i, j, slot):
        s = lax.dot_general(
            qh[i],
            kvg[j, 0:CH, 0:HD],
            (((1,), (1,)), ((), ())),
            preferred_element_type=jnp.float32,
        )
        s = s + bias[pl.ds(j, 1), :]
        sbuf[slot] = s
        mx[slot] = fold(jnp.maximum, s)

    def span_part(g, lanes):
        return jnp.concatenate([kvg[4 * g + k, CH:KV_ROWS, lanes] for k in range(4)], axis=0)

    def first_span(i, g, slot):
        s = lax.dot_general(
            qh[i],
            span_part(g, slice(0, HD)),
            (((1,), (1,)), ((), ())),
            preferred_element_type=jnp.float32,
        )
        parts = []
        row = lax.broadcasted_iota(jnp.int32, (TOK, TOK), 0)
        col = lax.broadcasted_iota(jnp.int32, (TOK, TOK), 1)
        for k in range(4):
            ahead = (4 * (4 * g + k) + y - 4 * own - i) * TOK
            parts.append(jnp.where(col + ahead <= row, 0.0, lowest_score))
        mask = jnp.concatenate(parts, axis=1)
        s = s + jnp.concatenate([mask] * HEADS, axis=0)
        sbuf[slot] = s
        mx[slot] = fold(jnp.maximum, s)

    def fold_in(i, slot, values):
        old = top[i]
        peak = jnp.max(mx[slot], axis=1, keepdims=True) * SCALE2
        new = jnp.maximum(old, jnp.broadcast_to(peak, (ROWS, HD)))
        factor = jnp.exp2(old - new)
        top[i] = new
        p = jnp.exp2(sbuf[slot] * SCALE2 - wide(new)).astype(jnp.bfloat16)
        both = jnp.dot(
            p,
            jnp.concatenate([values, jnp.ones_like(values)], axis=1),
            preferred_element_type=jnp.float32,
        )
        acc[i] = acc[i] * factor + both[:, 0:HD]
        den[i] = den[i] * factor + both[:, HD : 2 * HD]

    def second(i, j, slot):
        fold_in(i, slot, kvg[j, 0:CH, HD : 2 * HD])

    def second_span(i, g, slot):
        fold_in(i, slot, span_part(g, slice(HD, 2 * HD)))

    first(y, own, 0)

    oz = zo * 4 + x
    own2, far_m, far_p, far_2 = z * 4 + x2, zo * 4 + xm, zo * 4 + xp, zo * 4 + x2
    own_m, own_p = z * 4 + xm, z * 4 + xp
    def early(k):
        step = k % 3
        return (z + k // 3) % 2 * 4 + (x + step + step // 2) % 4

    def tile(d):
        return (y + d) % 4

    def early_tile(n):
        k = n % 4
        return tile(k + k // 2 - 2 * (k // 3))

    def piece(kind, c):
        src, dst, device = ((w_hbm, wh, pair), (w_hbm, wz, dz), (wh, wzh, dz))[kind]
        rows = pl.ds(c * WP, WP)
        return pltpu.make_async_remote_copy(
            src_ref=src.at[rows],
            dst_ref=dst.at[rows],
            send_sem=w_s.at[kind, c],
            recv_sem=w_r.at[kind, c],
            device_id=device,
            device_id_type=MESH,
        )

    def pass_first():
        wait("b_z", "b_xp", "b_xm", "a_xp", "a_xm", "a_z")
        kv_send("bz_xp", oz, b, dxp)
        kv_send("bz_xm", oz, b, dxm)
        kv_send("az_m", own_m, a, dz)
        kv_send("az_p", own_p, a, dz)
        kv_send("bf_xp", own_m, b0, dxp)
        kv_send("bf_xm", own_p, b1, dxm)
        kv_send("af_xp", own_m, a0, dxp)
        kv_send("af_xm", own_p, a1, dxm)
        wait("qf_yp", "qf_ym")

    def pass_weights(c):
        def action():
            if c == 0:
                near_wait(0)
                near_signal(1)
            piece(0, c).start()
            if c == 2:
                near_wait(1)
                near_signal(2)

        return action

    def pass_b():
        wait("bz_xp")
        kv_send("bzf_xp", far_m, b0, dxp)
        wait("bz_xm")
        kv_send("bzf_xm", far_p, b1, dxm)
        pass_weights(3)()

    def pass_a():
        wait("af_xp")
        kv_send("az_2a", own2, a0, dz)
        wait("af_xm")
        kv_send("az_2b", own2, a1, dz)

    oz = zo * 4 + x
    own2, far_m, far_p, far_2 = z * 4 + x2, zo * 4 + xm, zo * 4 + xp, zo * 4 + x2
    own_m, own_p = z * 4 + xm, z * 4 + xp
    wait("q_yp")
    start("qf_yp", (qh, ym, h0), (qh, ym, h0), dyp)
    wait("q_ym")
    start("qf_ym", (qh, yp, h1), (qh, yp, h1), dym)
    points = {
        1: pass_first,
        2: pass_weights(0),
        3: pass_weights(1),
        4: pass_weights(2),
        5: pass_b,
        6: pass_a,
    }

    @pl.loop(0, 7)
    def _(step):
        for at, action in points.items():
            pl.when(step == at)(action)
        for u in range(2):
            n = 2 * step + u
            first(early_tile(n + 1), early((n + 1) // 4), 1 - u)
            second(early_tile(n), early(n // 4), u)

    late = (own2, far_p, far_m, far_2)
    first(tile(2), early(3), 1)
    second(tile(3), early(3), 0)
    wait("bf_xp", "bf_xm", "az_m", "az_p")
    first(tile(1), late[0], 0)
    second(tile(2), early(3), 1)

    def wait_last():
        wait("bzf_xp", "bzf_xm", "az_2a", "az_2b")
        near_wait(2)

    def send_piece(t, k):
        if k < 4:

            @pl.when(t == 0)
            def _():
                piece(1, k).start()

        if k > 1:

            @pl.when(t == 3)
            def _():
                piece(0, k - 2).wait_recv()
                piece(2, k - 2).start()

    lane_t = lax.broadcasted_iota(jnp.int32, (TOK, HD), 1)
    t0 = pl.ds(0, HALF)
    t1 = pl.ds(HALF, HALF)

    def send_yp():
        start("to_p", (o4, 0), (part, 2), dyp)
        start("st_p", (st, 0), (stat, 2), dyp)

    def send_far():
        start("far_p", (o4, 1, t0), (fwd, 0), dyp)
        start("far_m", (o4, 1, t1), (fwd, 1), dym)
        start("st_2", (st, 1), (stat, 1), dy2)

    def send_ym():
        start("to_m", (o4, 2), (part, 0), dym)
        start("st_m", (st, 2), (stat, 0), dym)
        wait("far_p")
        start("fw_p", (fwd, 0), (part, 1, t0), dyp)
        wait("far_m")
        start("fw_m", (fwd, 1), (part, 1, t1), dym)

    @pl.loop(0, 4)
    def _(t):
        i = tile(t + 1)
        for k in range(3):
            send_piece(t, k)
            if k == 2:
                pl.when(t == 0)(wait_last)
            first(i, late[k + 1], (k + 1) % 2)
            second(i, late[k], k % 2)
        send_piece(t, 3)
        first_span(i, 0, 0)
        second(i, late[3], 1)
        send_piece(t, 4)
        first_span(i, 1, 1)
        second_span(i, 0, 0)
        send_piece(t, 5)
        first(tile(t + 2), late[0], 0)
        second_span(i, 1, 1)
        total = den[i]
        o = acc[i] / total
        lse = top[i] + jnp.log2(total)
        packed = jnp.zeros((TOK, HD), jnp.float32)
        for h in range(HEADS):
            rows = slice(h * TOK, (h + 1) * TOK)
            o4[t, :, h * HD : (h + 1) * HD] = o[rows].astype(jnp.bfloat16)
            packed = jnp.where(lane_t == h, lse[rows], packed)
        st[t] = packed.T[0:HEADS]
        pl.when(t == 0)(send_yp)
        pl.when(t == 1)(send_far)
        pl.when(t == 2)(send_ym)

    wait("st_p", "st_m", "st_2")
    s_own = st[3]
    s_p, s_m, s_2 = stat[0], stat[2], stat[1]
    best = jnp.maximum(jnp.maximum(s_own, s_p), jnp.maximum(s_m, s_2))
    e_own = jnp.exp2(s_own - best)
    e_p = jnp.exp2(s_p - best)
    e_m = jnp.exp2(s_m - best)
    e_2 = jnp.exp2(s_2 - best)
    norm = 1.0 / (e_own + e_p + e_m + e_2)
    table[...] = jnp.concatenate(
        [e_own * norm, e_p * norm, e_m * norm, e_2 * norm, jnp.zeros((96, TOK), jnp.float32)],
        axis=0,
    ).T
    wait("to_p", "to_m", "fw_p", "fw_m")
    slot_own = x * 4 + y

    def combined(begin, dest):
        rows = pl.ds(pl.multiple_of(begin, HALF), HALF)
        for h in range(HEADS):
            lanes = slice(h * HD, (h + 1) * HD)
            out = o4[3, rows, lanes].astype(jnp.float32) * table[rows, h : h + 1]
            out += part[0, rows, lanes].astype(jnp.float32) * table[rows, 8 + h : 9 + h]
            out += part[2, rows, lanes].astype(jnp.float32) * table[rows, 16 + h : 17 + h]
            out += part[1, rows, lanes].astype(jnp.float32) * table[rows, 24 + h : 25 + h]
            dest[:, lanes] = out.astype(jnp.bfloat16)

    combined(even * HALF, att.at[0, slot_own])
    lo, hi, full = pl.ds(0, HALF // 2), pl.ds(HALF // 2, HALF // 2), pl.ds(0, HALF)

    def send(name, k, slot, rows, device):
        start(name, (att, k, slot, rows), (att, k, slot, rows), device)

    def both_y(r, xs):
        send("ayp%d" % r, 0, xs * 4 + y, full, dyp)
        send("aym%d" % r, 0, xs * 4 + y, full, dym)

    def both_x(r, ys):
        send("bxp%d" % r, 1, x * 4 + ys, full, dxp)
        send("bxm%d" % r, 1, x * 4 + ys, full, dxm)

    send("axp", 0, slot_own, full, dxp)
    send("axm", 0, slot_own, full, dxm)
    both_y(0, x)
    combined((1 - even) * HALF, away)
    start("swap", away, (att, 1, slot_own), pair)
    wait("axp")
    send("axfp", 0, xm * 4 + y, lo, dxp)
    both_y(3, xm)
    wait("axm")
    send("axfm", 0, xp * 4 + y, hi, dxm)
    both_y(1, xp)
    wait("swap")
    send("byp", 1, slot_own, full, dyp)
    send("bym", 1, slot_own, full, dym)
    both_x(0, y)

    def relay_a(r):
        xs = (x + r) % 4
        wait("ayp%d" % r)
        send("lap%d" % r, 0, xs * 4 + ym, lo, dyp)
        wait("aym%d" % r)
        send("lam%d" % r, 0, xs * 4 + yp, hi, dym)

    def relay_b(r):
        ys = (y + r) % 4
        wait("bxp%d" % r)
        send("lbp%d" % r, 1, xm * 4 + ys, lo, dxp)
        wait("bxm%d" % r)
        send("lbm%d" % r, 1, xp * 4 + ys, hi, dxm)

    def core_copy(n):
        return pltpu.make_async_remote_copy(
            src_ref=give.at[n],
            dst_ref=got.at[n],
            send_sem=core_s.at[n],
            recv_sem=core_r.at[n],
            device_id=other,
            device_id_type=MESH,
        )

    def z_copy(row, n, far):
        return pltpu.make_async_remote_copy(
            src_ref=keep.at[n, far],
            dst_ref=box.at[high],
            send_sem=z_s.at[2 * n + far],
            recv_sem=z_r.at[high],
            device_id={
                "ctx": ctx_of(zo if far else z, x, y),
                "tp": (2 * z + row // 2) * 2 + core,
            },
            device_id_type=MESH,
        )

    def product(row, n):
        keeps = row % 2 == core
        slots = pl.ds(4 * row, 4)
        rows_a = att[0, slots].reshape(BLK // 2, HEADS * HD)
        rows_b = att[1, slots].reshape(BLK // 2, HEADS * HD)
        for far, (wa, wb) in enumerate(((w_ref, wh), (wz, wzh))):
            prod[n % 2, far] = jnp.dot(
                rows_a, wa[...], preferred_element_type=jnp.float32
            ) + jnp.dot(rows_b, wb[...], preferred_element_type=jnp.float32)

        @pl.when(jnp.logical_not(keeps))
        def _():
            give[n] = prod[n % 2].astype(jnp.bfloat16)
            core_copy(n).start()

    def settle(row, n):
        keeps = row % 2 == core
        remote = 2 * z + row // 2 != high

        @pl.when(keeps)
        def _():
            core_copy(n).wait_recv()
            keep[n] = (prod[n % 2] + got[n].astype(jnp.float32)).astype(jnp.bfloat16)
            z_copy(row, n, 1).start()

            @pl.when(remote)
            def _():
                z_copy(row, n, 0).start()

            @pl.when(jnp.logical_not(remote))
            def _():
                box[high] = keep[n, 0]

    relay_a(0)
    wait("byp")
    send("byfp", 1, x * 4 + ym, lo, dyp)
    both_x(3, ym)
    wait("bym")
    send("byfm", 1, x * 4 + yp, hi, dym)
    both_x(1, yp)
    wait("axfp", "axfm")
    both_y(2, x2)
    relay_a(3)
    relay_b(0)
    wait("byfp", "byfm")
    both_x(2, y2)
    wait("lap0", "lam0")
    for c in range(4):
        piece(1, c).wait_recv()
        piece(2, c).wait_recv()
    weights_here.wait()
    product(x, 0)
    relay_a(1)
    settle(x, 0)
    relay_b(3)
    relay_b(1)
    relay_a(2)
    relay_b(2)
    wait("lap3", "lam3")
    product(xm, 1)
    settle(xm, 1)
    wait("lap1", "lam1")
    product(xp, 2)
    settle(xp, 2)
    wait("lap2", "lam2")
    for r in range(4):
        wait("lbp%d" % r, "lbm%d" % r)
    product(x2, 3)
    settle(x2, 3)

    source_z = high // 2
    for s in range(4):
        arrives = jnp.logical_or(high != s, z != source_z)

        @pl.when(arrives)
        def _(s=s):
            pltpu.make_async_remote_copy(
                src_ref=keep.at[0, 0],
                dst_ref=box.at[s],
                send_sem=z_s.at[0],
                recv_sem=z_r.at[s],
                device_id=other,
                device_id_type=MESH,
            ).wait_recv()

    for e in range(2):
        total = box[e].astype(jnp.float32) + box[2 + e].astype(jnp.float32)
        total = total.astype(jnp.bfloat16)
        for g in range(4):
            begin = g * TOK + e * HALF
            out_ref[begin : begin + HALF] = total[g * HALF : (g + 1) * HALF]
    for n, row in enumerate((x, xm, xp, x2)):
        keeps = row % 2 == core
        remote = 2 * z + row // 2 != high

        @pl.when(keeps)
        def _(n=n, row=row, remote=remote):
            z_copy(row, n, 1).wait_send()

            @pl.when(remote)
            def _():
                z_copy(row, n, 0).wait_send()

        @pl.when(jnp.logical_not(keeps))
        def _(n=n):
            core_copy(n).wait_send()

    for make in makers.values():
        make().wait_send()
    for kind in range(3):
        for c in range(4):
            piece(kind, c).wait_send()


def fused(lengths, q, cache, span, cosine, sine, w):
    bf16, f32 = jnp.bfloat16, jnp.float32
    return pl.pallas_call(
        fused_kernel,
        name="attention_block",
        out_shape=jax.ShapeDtypeStruct((BLK, COLS), bf16),
        in_specs=[pl.BlockSpec(memory_space=pltpu.SMEM)]
        + [pl.BlockSpec(memory_space=pltpu.VMEM)] * 5
        + [pl.BlockSpec(memory_space=pltpu.HBM)],
        out_specs=pl.BlockSpec(memory_space=pltpu.VMEM),
        scratch_shapes=[
            pltpu.VMEM((HEADS * HD, COLS), bf16),
            pltpu.VMEM((4, ROWS, HD), bf16),
            pltpu.VMEM((8, KV_ROWS, 2 * HD), bf16),
            pltpu.VMEM((8, CH), f32),
            pltpu.VMEM((2, ROWS, CH), f32),
            pltpu.VMEM((2, ROWS, HD), f32),
            pltpu.VMEM((4, ROWS, HD), f32),
            pltpu.VMEM((4, ROWS, HD), f32),
            pltpu.VMEM((4, ROWS, HD), f32),
            pltpu.VMEM((4, TOK, HEADS * HD), bf16),
            pltpu.VMEM((4, HEADS, TOK), f32),
            pltpu.VMEM((3, TOK, HEADS * HD), bf16),
            pltpu.VMEM((3, HEADS, TOK), f32),
            pltpu.VMEM((TOK, TOK), f32),
            pltpu.VMEM((2, HALF, HEADS * HD), bf16),
            pltpu.VMEM((HALF, HEADS * HD), bf16),
            pltpu.VMEM((HEADS * HD, COLS), bf16),
            pltpu.VMEM((HEADS * HD, COLS), bf16),
            pltpu.VMEM((HEADS * HD, COLS), bf16),
            pltpu.VMEM((2, 16, HALF, HEADS * HD), bf16),
            pltpu.VMEM((2, 2, BLK // 2, COLS), f32),
            pltpu.VMEM((4, 2, BLK // 2, COLS), bf16),
            pltpu.VMEM((4, 2, BLK // 2, COLS), bf16),
            pltpu.VMEM((4, 2, BLK // 2, COLS), bf16),
            pltpu.VMEM((4, BLK // 2, COLS), bf16),
            pltpu.SemaphoreType.DMA((COPIES,)),
            pltpu.SemaphoreType.DMA((COPIES,)),
            pltpu.SemaphoreType.DMA((3, 4)),
            pltpu.SemaphoreType.DMA((3, 4)),
            pltpu.SemaphoreType.DMA,
            pltpu.SemaphoreType.REGULAR((3,)),
            pltpu.SemaphoreType.DMA((4,)),
            pltpu.SemaphoreType.DMA((4,)),
            pltpu.SemaphoreType.DMA((8,)),
            pltpu.SemaphoreType.DMA((4,)),
        ],
        compiler_params=pltpu.CompilerParams(
            collective_id=0, has_side_effects=True, vmem_limit_bytes=48 << 20
        ),
    )(lengths, q, cache, span, cosine, sine, w)


def body(queries, span_kv, cache_kv, out_weight, offset, lengths):
    first_token = lax.axis_index("ctx") * TOK
    positions = offset[0] + first_token + jnp.arange(TOK, dtype=jnp.int32)
    cosine, sine = rotary_tables(positions)
    cache = cache_kv.reshape(CH, 2 * HD)
    span = span_kv.reshape(TOK, 2 * HD)
    return fused(lengths, queries, cache, span, cosine, sine, out_weight)


def solution(mesh):
    return jax.shard_map(
        body,
        mesh=mesh,
        in_specs=(
            P("ctx", "tp"),
            P("ctx", "tp", None, None),
            P("ctx", "tp", None, None),
            P("tp", "ctx"),
            P(),
            P(),
        ),
        out_specs=P("tp", "ctx"),
        check_vma=False,
    )
```

```python
import math

import jax
import jax.numpy as jnp
from jax import lax
from jax.experimental import pallas as pl
from jax.experimental.pallas import tpu as pltpu
from jax.sharding import PartitionSpec as P

SLOT = 256
HD = 128
TOK = 128
HEADS = 8
KV_ROWS = 640
CH = 512
A_ROWS = 256
ROWS = HEADS * TOK
BLK = 512
COLS = 256
HALF = TOK // 2
WP = 256
COPIES = 72
lowest_score = -1e30
rope_base = 500000.0
MESH = pl.DeviceIdType.MESH
SCALE2 = math.log2(math.e) / math.sqrt(HD)


def rotary_tables(positions):
    half = HD // 2
    frequency = jnp.exp(
        jnp.arange(half, dtype=jnp.float32) * (-2.0 * math.log(rope_base) / HD)
    )
    angles = positions.astype(jnp.float32)[:, None] * frequency[None, :]
    cosine, sine = jnp.cos(angles), jnp.sin(angles)
    return jnp.concatenate([cosine, cosine], axis=1), jnp.concatenate([-sine, sine], axis=1)


def coords():
    c = lax.axis_index("ctx")
    z = c // 16
    x = (c // 4) % 4
    y = c % 4
    return z, x, y


def ctx_of(z, x, y):
    return z * 16 + x * 4 + y


def entry_barrier(devices):
    barrier = pltpu.get_barrier_semaphore()
    for d in devices:
        pl.semaphore_signal(barrier, inc=1, device_id=d, device_id_type=MESH)
    pl.semaphore_wait(barrier, len(devices))


def fold(op, values):
    out = values[:, 0:HD]
    for n in range(1, values.shape[1] // HD):
        out = op(out, values[:, n * HD : (n + 1) * HD])
    return out


def wide(values):
    return jnp.concatenate([values] * (CH // HD), axis=1)


def fused_kernel(
    lens_ref,
    q_ref,
    cache_ref,
    span_ref,
    cos_ref,
    sin_ref,
    w_hbm,
    out_ref,
    w_ref,
    qh,
    kvg,
    bias,
    sbuf,
    mx,
    top,
    den,
    acc,
    o4,
    st,
    part,
    stat,
    table,
    fwd,
    away,
    wz,
    wh,
    wzh,
    att,
    prod,
    give,
    got,
    keep,
    box,
    ssem,
    rsem,
    w_s,
    w_r,
    w_local,
    near,
    core_s,
    core_r,
    z_s,
    z_r,
):
    z, x, y = coords()
    tp = lax.axis_index("tp")
    core = tp % 2
    high = tp // 2
    even = high % 2
    zo = 1 - z
    other = {"tp": tp + 1 - 2 * core}
    pair = {"tp": tp + 2 - 4 * even}
    pos = 2 * high + z
    column = []
    for d in range(1, 8):
        q = (pos + d) % 8
        column.append({"ctx": ctx_of(q % 2, x, y), "tp": (q // 2) * 2 + core})
    xp, xm, x2 = (x + 1) % 4, (x + 3) % 4, (x + 2) % 4
    yp, ym, y2 = (y + 1) % 4, (y + 3) % 4, (y + 2) % 4
    dz = {"ctx": ctx_of(zo, x, y)}
    dxp = {"ctx": ctx_of(z, xp, y)}
    dxm = {"ctx": ctx_of(z, xm, y)}
    dyp = {"ctx": ctx_of(z, x, yp)}
    dym = {"ctx": ctx_of(z, x, ym)}
    dy2 = {"ctx": ctx_of(z, x, y2)}

    table_of = {}

    def view(place):
        if isinstance(place, tuple):
            return place[0].at[place[1:]]
        return place

    def copy(name, src, dst, device):
        n = table_of.setdefault(name, len(table_of))
        return pltpu.make_async_remote_copy(
            src_ref=view(src),
            dst_ref=view(dst),
            send_sem=ssem.at[n],
            recv_sem=rsem.at[n],
            device_id=device,
            device_id_type=MESH,
        )

    makers = {}

    def start(name, src, dst, device):
        def make():
            return copy(name, src, dst, device)

        makers[name] = make
        make().start()

    def wait(*names):
        for name in names:
            makers[name]().wait_recv()

    own = z * 4 + x
    a = pl.ds(0, A_ROWS)
    a0 = pl.ds(0, A_ROWS // 2)
    a1 = pl.ds(A_ROWS // 2, A_ROWS // 2)
    nb = KV_ROWS - A_ROWS
    b = pl.ds(A_ROWS, nb)
    b0 = pl.ds(A_ROWS, nb // 2)
    b1 = pl.ds(A_ROWS + nb // 2, nb // 2)
    h0 = pl.ds(0, ROWS // 2)
    h1 = pl.ds(ROWS // 2, ROWS // 2)

    next_z, last_z = column[0], column[6]
    entry_barrier([dxp, dxm, dyp, dym, other, next_z, last_z])

    def near_signal(r):
        for device in (next_z, last_z):
            pl.semaphore_signal(near.at[r], inc=1, device_id=device, device_id_type=MESH)

    def near_wait(r):
        pl.semaphore_wait(near.at[r], 2)

    near_signal(0)

    def kv_send(name, j, rows, device):
        start(name, (kvg, j, rows), (kvg, j, rows), device)

    def rotated(values):
        values = values.astype(jnp.float32)
        turned = jnp.concatenate([values[:, HD // 2 :], values[:, : HD // 2]], axis=1)
        return (values * cos_ref[...] + turned * sin_ref[...]).astype(jnp.bfloat16)

    def kv_own(name, rows, device):
        kv_send(name, own, rows, device)

    kvg[own, 0:CH] = cache_ref[...]
    kvg[own, CH:KV_ROWS, 0:HD] = rotated(span_ref[:, 0:HD])
    kvg[own, CH:KV_ROWS, HD : 2 * HD] = span_ref[:, HD : 2 * HD]
    kv_own("b_z", b, dz)
    kv_own("b_xp", b, dxp)
    kv_own("b_xm", b, dxm)
    for h in range(HEADS):
        qh[y, h * TOK : (h + 1) * TOK, :] = rotated(q_ref[:, h * HD : (h + 1) * HD])
    start("q_yp", (qh, y), (qh, y), dyp)
    start("q_ym", (qh, y), (qh, y), dym)
    kv_own("a_xp", a, dxp)
    kv_own("a_xm", a, dxm)
    kv_own("a_z", a, dz)
    weights_here = pltpu.make_async_copy(w_hbm, w_ref, w_local)
    weights_here.start()

    lane = lax.broadcasted_iota(jnp.int32, (1, SLOT), 1)
    for j in range(8):
        for s in range(2):
            n = lens_ref[2 * (4 * j + y) + s]
            bias[j : j + 1, s * SLOT : (s + 1) * SLOT] = jnp.where(lane < n, 0.0, lowest_score)
    top[...] = jnp.full(top.shape, lowest_score, jnp.float32)
    den[...] = jnp.zeros_like(den)
    acc[...] = jnp.zeros_like(acc)

    def first(i, j, slot):
        s = lax.dot_general(
            qh[i],
            kvg[j, 0:CH, 0:HD],
            (((1,), (1,)), ((), ())),
            preferred_element_type=jnp.float32,
        )
        s = s + bias[pl.ds(j, 1), :]
        sbuf[slot] = s
        mx[slot] = fold(jnp.maximum, s)

    def span_part(g, lanes):
        return jnp.concatenate([kvg[4 * g + k, CH:KV_ROWS, lanes] for k in range(4)], axis=0)

    def first_span(i, g, slot):
        s = lax.dot_general(
            qh[i],
            span_part(g, slice(0, HD)),
            (((1,), (1,)), ((), ())),
            preferred_element_type=jnp.float32,
        )
        parts = []
        row = lax.broadcasted_iota(jnp.int32, (TOK, TOK), 0)
        col = lax.broadcasted_iota(jnp.int32, (TOK, TOK), 1)
        for k in range(4):
            ahead = (4 * (4 * g + k) + y - 4 * own - i) * TOK
            parts.append(jnp.where(col + ahead <= row, 0.0, lowest_score))
        mask = jnp.concatenate(parts, axis=1)
        s = s + jnp.concatenate([mask] * HEADS, axis=0)
        sbuf[slot] = s
        mx[slot] = fold(jnp.maximum, s)

    def fold_in(i, slot, values):
        old = top[i]
        peak = jnp.max(mx[slot], axis=1, keepdims=True) * SCALE2
        new = jnp.maximum(old, jnp.broadcast_to(peak, (ROWS, HD)))
        factor = jnp.exp2(old - new)
        top[i] = new
        p = jnp.exp2(sbuf[slot] * SCALE2 - wide(new)).astype(jnp.bfloat16)
        both = jnp.dot(
            p,
            jnp.concatenate([values, jnp.ones_like(values)], axis=1),
            preferred_element_type=jnp.float32,
        )
        acc[i] = acc[i] * factor + both[:, 0:HD]
        den[i] = den[i] * factor + both[:, HD : 2 * HD]

    def second(i, j, slot):
        fold_in(i, slot, kvg[j, 0:CH, HD : 2 * HD])

    def second_span(i, g, slot):
        fold_in(i, slot, span_part(g, slice(HD, 2 * HD)))

    first(y, own, 0)

    oz = zo * 4 + x
    own2, far_m, far_p, far_2 = z * 4 + x2, zo * 4 + xm, zo * 4 + xp, zo * 4 + x2
    own_m, own_p = z * 4 + xm, z * 4 + xp
    def early(k):
        step = k % 3
        return (z + k // 3) % 2 * 4 + (x + step + step // 2) % 4

    def tile(d):
        return (y + d) % 4

    def early_tile(n):
        k = n % 4
        return tile(k + k // 2 - 2 * (k // 3))

    def piece(kind, c):
        src, dst, device = ((w_hbm, wh, pair), (w_hbm, wz, dz), (wh, wzh, dz))[kind]
        rows = pl.ds(c * WP, WP)
        return pltpu.make_async_remote_copy(
            src_ref=src.at[rows],
            dst_ref=dst.at[rows],
            send_sem=w_s.at[kind, c],
            recv_sem=w_r.at[kind, c],
            device_id=device,
            device_id_type=MESH,
        )

    def pass_first():
        wait("b_z", "b_xp", "b_xm", "a_xp", "a_xm", "a_z")
        kv_send("bz_xp", oz, b, dxp)
        kv_send("bz_xm", oz, b, dxm)
        kv_send("az_m", own_m, a, dz)
        kv_send("az_p", own_p, a, dz)
        kv_send("bf_xp", own_m, b0, dxp)
        kv_send("bf_xm", own_p, b1, dxm)
        kv_send("af_xp", own_m, a0, dxp)
        kv_send("af_xm", own_p, a1, dxm)
        wait("qf_yp", "qf_ym")

    def round_one():
        near_wait(0)
        near_signal(1)

    def round_two():
        near_wait(1)
        near_signal(2)

    def pass_b():
        wait("bz_xp")
        kv_send("bzf_xp", far_m, b0, dxp)
        wait("bz_xm")
        kv_send("bzf_xm", far_p, b1, dxm)

    def pass_a():
        wait("af_xp")
        kv_send("az_2a", own2, a0, dz)
        wait("af_xm")
        kv_send("az_2b", own2, a1, dz)

    oz = zo * 4 + x
    own2, far_m, far_p, far_2 = z * 4 + x2, zo * 4 + xm, zo * 4 + xp, zo * 4 + x2
    own_m, own_p = z * 4 + xm, z * 4 + xp
    wait("q_yp")
    start("qf_yp", (qh, ym, h0), (qh, ym, h0), dyp)
    wait("q_ym")
    start("qf_ym", (qh, yp, h1), (qh, yp, h1), dym)
    points = {
        1: pass_first,
        2: round_one,
        4: round_two,
        5: pass_b,
        6: pass_a,
    }

    @pl.loop(0, 7)
    def _(step):
        for at, action in points.items():
            pl.when(step == at)(action)
        for u in range(2):
            n = 2 * step + u
            first(early_tile(n + 1), early((n + 1) // 4), 1 - u)
            second(early_tile(n), early(n // 4), u)

    late = (own2, far_p, far_m, far_2)
    first(tile(2), early(3), 1)
    second(tile(3), early(3), 0)
    wait("bf_xp", "bf_xm", "az_m", "az_p")
    first(tile(1), late[0], 0)
    second(tile(2), early(3), 1)

    def wait_last():
        wait("bzf_xp", "bzf_xm", "az_2a", "az_2b")
        near_wait(2)

    def forward_piece(c):
        piece(0, c).wait_recv()
        piece(2, c).start()

    pieces = {
        (0, 0): lambda: piece(0, 0).start(),
        (0, 1): lambda: piece(0, 1).start(),
        (0, 2): lambda: piece(1, 0).start(),
        (0, 3): lambda: piece(0, 2).start(),
        (0, 4): lambda: piece(0, 3).start(),
        (0, 5): lambda: piece(1, 1).start(),
        (1, 2): lambda: piece(1, 2).start(),
        (1, 4): lambda: piece(1, 3).start(),
        (2, 2): lambda: forward_piece(0),
        (2, 5): lambda: forward_piece(1),
        (3, 5): lambda: forward_piece(2),
    }

    def send_piece(t, k):
        for (at, item), action in pieces.items():
            if item == k:
                pl.when(t == at)(action)

    lane_t = lax.broadcasted_iota(jnp.int32, (TOK, HD), 1)
    t0 = pl.ds(0, HALF)
    t1 = pl.ds(HALF, HALF)

    def send_yp():
        start("to_p", (o4, 0), (part, 2), dyp)
        start("st_p", (st, 0), (stat, 2), dyp)

    def send_far():
        start("far_p", (o4, 1, t0), (fwd, 0), dyp)
        start("far_m", (o4, 1, t1), (fwd, 1), dym)
        start("st_2", (st, 1), (stat, 1), dy2)

    def send_ym():
        start("to_m", (o4, 2), (part, 0), dym)
        start("st_m", (st, 2), (stat, 0), dym)
        wait("far_p")
        start("fw_p", (fwd, 0), (part, 1, t0), dyp)
        wait("far_m")
        start("fw_m", (fwd, 1), (part, 1, t1), dym)

    @pl.loop(0, 4)
    def _(t):
        i = tile(t + 1)
        for k in range(3):
            send_piece(t, k)
            if k == 2:
                pl.when(t == 0)(wait_last)
            first(i, late[k + 1], (k + 1) % 2)
            second(i, late[k], k % 2)
        send_piece(t, 3)
        first_span(i, 0, 0)
        second(i, late[3], 1)
        send_piece(t, 4)
        first_span(i, 1, 1)
        second_span(i, 0, 0)
        send_piece(t, 5)
        first(tile(t + 2), late[0], 0)
        second_span(i, 1, 1)
        total = den[i]
        o = acc[i] / total
        lse = top[i] + jnp.log2(total)
        packed = jnp.zeros((TOK, HD), jnp.float32)
        for h in range(HEADS):
            rows = slice(h * TOK, (h + 1) * TOK)
            o4[t, :, h * HD : (h + 1) * HD] = o[rows].astype(jnp.bfloat16)
            packed = jnp.where(lane_t == h, lse[rows], packed)
        st[t] = packed.T[0:HEADS]
        pl.when(t == 0)(send_yp)
        pl.when(t == 1)(send_far)
        pl.when(t == 2)(send_ym)

    wait("st_p", "st_m", "st_2")
    s_own = st[3]
    s_p, s_m, s_2 = stat[0], stat[2], stat[1]
    best = jnp.maximum(jnp.maximum(s_own, s_p), jnp.maximum(s_m, s_2))
    e_own = jnp.exp2(s_own - best)
    e_p = jnp.exp2(s_p - best)
    e_m = jnp.exp2(s_m - best)
    e_2 = jnp.exp2(s_2 - best)
    norm = 1.0 / (e_own + e_p + e_m + e_2)
    table[...] = jnp.concatenate(
        [e_own * norm, e_p * norm, e_m * norm, e_2 * norm, jnp.zeros((96, TOK), jnp.float32)],
        axis=0,
    ).T
    wait("to_p", "to_m", "fw_p", "fw_m")
    slot_own = x * 4 + y

    def combined(begin, dest):
        rows = pl.ds(pl.multiple_of(begin, HALF), HALF)
        for h in range(HEADS):
            lanes = slice(h * HD, (h + 1) * HD)
            out = o4[3, rows, lanes].astype(jnp.float32) * table[rows, h : h + 1]
            out += part[0, rows, lanes].astype(jnp.float32) * table[rows, 8 + h : 9 + h]
            out += part[2, rows, lanes].astype(jnp.float32) * table[rows, 16 + h : 17 + h]
            out += part[1, rows, lanes].astype(jnp.float32) * table[rows, 24 + h : 25 + h]
            dest[:, lanes] = out.astype(jnp.bfloat16)

    combined(even * HALF, att.at[0, slot_own])
    lo, hi, full = pl.ds(0, HALF // 2), pl.ds(HALF // 2, HALF // 2), pl.ds(0, HALF)

    def send(name, k, slot, rows, device):
        start(name, (att, k, slot, rows), (att, k, slot, rows), device)

    def both_y(r, xs):
        send("ayp%d" % r, 0, xs * 4 + y, full, dyp)
        send("aym%d" % r, 0, xs * 4 + y, full, dym)

    def both_x(r, ys):
        send("bxp%d" % r, 1, x * 4 + ys, full, dxp)
        send("bxm%d" % r, 1, x * 4 + ys, full, dxm)

    send("axp", 0, slot_own, full, dxp)
    send("axm", 0, slot_own, full, dxm)
    both_y(0, x)
    combined((1 - even) * HALF, away)
    start("swap", away, (att, 1, slot_own), pair)
    wait("axp")
    send("axfp", 0, xm * 4 + y, lo, dxp)
    both_y(3, xm)
    wait("axm")
    send("axfm", 0, xp * 4 + y, hi, dxm)
    both_y(1, xp)
    wait("swap")
    forward_piece(3)
    send("byp", 1, slot_own, full, dyp)
    send("bym", 1, slot_own, full, dym)
    both_x(0, y)

    def relay_a(r):
        xs = (x + r) % 4
        wait("ayp%d" % r)
        send("lap%d" % r, 0, xs * 4 + ym, lo, dyp)
        wait("aym%d" % r)
        send("lam%d" % r, 0, xs * 4 + yp, hi, dym)

    def relay_b(r):
        ys = (y + r) % 4
        wait("bxp%d" % r)
        send("lbp%d" % r, 1, xm * 4 + ys, lo, dxp)
        wait("bxm%d" % r)
        send("lbm%d" % r, 1, xp * 4 + ys, hi, dxm)

    def core_copy(n):
        return pltpu.make_async_remote_copy(
            src_ref=give.at[n],
            dst_ref=got.at[n],
            send_sem=core_s.at[n],
            recv_sem=core_r.at[n],
            device_id=other,
            device_id_type=MESH,
        )

    def z_copy(row, n, far):
        return pltpu.make_async_remote_copy(
            src_ref=keep.at[n, far],
            dst_ref=box.at[high],
            send_sem=z_s.at[2 * n + far],
            recv_sem=z_r.at[high],
            device_id={
                "ctx": ctx_of(zo if far else z, x, y),
                "tp": (2 * z + row // 2) * 2 + core,
            },
            device_id_type=MESH,
        )

    def half_product(row, n, far):
        wa, wb = (wz, wzh) if far else (w_ref, wh)
        slots = pl.ds(4 * row, 4)
        rows_a = att[0, slots].reshape(BLK // 2, HEADS * HD)
        rows_b = att[1, slots].reshape(BLK // 2, HEADS * HD)
        prod[n % 2, far] = jnp.dot(rows_a, wa[...], preferred_element_type=jnp.float32) + jnp.dot(
            rows_b, wb[...], preferred_element_type=jnp.float32
        )

    def hand_over(row, n):
        keeps = row % 2 == core

        @pl.when(jnp.logical_not(keeps))
        def _():
            give[n] = prod[n % 2].astype(jnp.bfloat16)
            core_copy(n).start()

    def product(row, n):
        half_product(row, n, 0)
        half_product(row, n, 1)
        hand_over(row, n)

    def settle(row, n):
        keeps = row % 2 == core
        remote = 2 * z + row // 2 != high

        @pl.when(keeps)
        def _():
            core_copy(n).wait_recv()
            keep[n] = (prod[n % 2] + got[n].astype(jnp.float32)).astype(jnp.bfloat16)
            z_copy(row, n, 1).start()

            @pl.when(remote)
            def _():
                z_copy(row, n, 0).start()

            @pl.when(jnp.logical_not(remote))
            def _():
                box[high] = keep[n, 0]

    relay_a(0)
    wait("byp")
    send("byfp", 1, x * 4 + ym, lo, dyp)
    both_x(3, ym)
    wait("bym")
    send("byfm", 1, x * 4 + yp, hi, dym)
    both_x(1, yp)
    wait("axfp", "axfm")
    both_y(2, x2)
    relay_a(3)
    relay_b(0)
    wait("byfp", "byfm")
    both_x(2, y2)
    wait("lap0", "lam0")
    weights_here.wait()
    half_product(x, 0, 0)
    relay_a(1)
    relay_b(3)
    relay_b(1)
    for c in range(4):
        piece(1, c).wait_recv()
        piece(2, c).wait_recv()
    half_product(x, 0, 1)
    hand_over(x, 0)
    relay_a(2)
    relay_b(2)
    settle(x, 0)
    wait("lap3", "lam3")
    product(xm, 1)
    settle(xm, 1)
    wait("lap1", "lam1")
    product(xp, 2)
    settle(xp, 2)
    wait("lap2", "lam2")
    for r in range(4):
        wait("lbp%d" % r, "lbm%d" % r)
    product(x2, 3)
    settle(x2, 3)

    source_z = high // 2
    for s in range(4):
        arrives = jnp.logical_or(high != s, z != source_z)

        @pl.when(arrives)
        def _(s=s):
            pltpu.make_async_remote_copy(
                src_ref=keep.at[0, 0],
                dst_ref=box.at[s],
                send_sem=z_s.at[0],
                recv_sem=z_r.at[s],
                device_id=other,
                device_id_type=MESH,
            ).wait_recv()

    for e in range(2):
        total = box[e].astype(jnp.float32) + box[2 + e].astype(jnp.float32)
        total = total.astype(jnp.bfloat16)
        for g in range(4):
            begin = g * TOK + e * HALF
            out_ref[begin : begin + HALF] = total[g * HALF : (g + 1) * HALF]
    for n, row in enumerate((x, xm, xp, x2)):
        keeps = row % 2 == core
        remote = 2 * z + row // 2 != high

        @pl.when(keeps)
        def _(n=n, row=row, remote=remote):
            z_copy(row, n, 1).wait_send()

            @pl.when(remote)
            def _():
                z_copy(row, n, 0).wait_send()

        @pl.when(jnp.logical_not(keeps))
        def _(n=n):
            core_copy(n).wait_send()

    for make in makers.values():
        make().wait_send()
    for kind in range(3):
        for c in range(4):
            piece(kind, c).wait_send()


def fused(lengths, q, cache, span, cosine, sine, w):
    bf16, f32 = jnp.bfloat16, jnp.float32
    return pl.pallas_call(
        fused_kernel,
        name="attention_block",
        out_shape=jax.ShapeDtypeStruct((BLK, COLS), bf16),
        in_specs=[pl.BlockSpec(memory_space=pltpu.SMEM)]
        + [pl.BlockSpec(memory_space=pltpu.VMEM)] * 5
        + [pl.BlockSpec(memory_space=pltpu.HBM)],
        out_specs=pl.BlockSpec(memory_space=pltpu.VMEM),
        scratch_shapes=[
            pltpu.VMEM((HEADS * HD, COLS), bf16),
            pltpu.VMEM((4, ROWS, HD), bf16),
            pltpu.VMEM((8, KV_ROWS, 2 * HD), bf16),
            pltpu.VMEM((8, CH), f32),
            pltpu.VMEM((2, ROWS, CH), f32),
            pltpu.VMEM((2, ROWS, HD), f32),
            pltpu.VMEM((4, ROWS, HD), f32),
            pltpu.VMEM((4, ROWS, HD), f32),
            pltpu.VMEM((4, ROWS, HD), f32),
            pltpu.VMEM((4, TOK, HEADS * HD), bf16),
            pltpu.VMEM((4, HEADS, TOK), f32),
            pltpu.VMEM((3, TOK, HEADS * HD), bf16),
            pltpu.VMEM((3, HEADS, TOK), f32),
            pltpu.VMEM((TOK, TOK), f32),
            pltpu.VMEM((2, HALF, HEADS * HD), bf16),
            pltpu.VMEM((HALF, HEADS * HD), bf16),
            pltpu.VMEM((HEADS * HD, COLS), bf16),
            pltpu.VMEM((HEADS * HD, COLS), bf16),
            pltpu.VMEM((HEADS * HD, COLS), bf16),
            pltpu.VMEM((2, 16, HALF, HEADS * HD), bf16),
            pltpu.VMEM((2, 2, BLK // 2, COLS), f32),
            pltpu.VMEM((4, 2, BLK // 2, COLS), bf16),
            pltpu.VMEM((4, 2, BLK // 2, COLS), bf16),
            pltpu.VMEM((4, 2, BLK // 2, COLS), bf16),
            pltpu.VMEM((4, BLK // 2, COLS), bf16),
            pltpu.SemaphoreType.DMA((COPIES,)),
            pltpu.SemaphoreType.DMA((COPIES,)),
            pltpu.SemaphoreType.DMA((3, 4)),
            pltpu.SemaphoreType.DMA((3, 4)),
            pltpu.SemaphoreType.DMA,
            pltpu.SemaphoreType.REGULAR((3,)),
            pltpu.SemaphoreType.DMA((4,)),
            pltpu.SemaphoreType.DMA((4,)),
            pltpu.SemaphoreType.DMA((8,)),
            pltpu.SemaphoreType.DMA((4,)),
        ],
        compiler_params=pltpu.CompilerParams(
            collective_id=0, has_side_effects=True, vmem_limit_bytes=48 << 20
        ),
    )(lengths, q, cache, span, cosine, sine, w)


def body(queries, span_kv, cache_kv, out_weight, offset, lengths):
    first_token = lax.axis_index("ctx") * TOK
    positions = offset[0] + first_token + jnp.arange(TOK, dtype=jnp.int32)
    cosine, sine = rotary_tables(positions)
    cache = cache_kv.reshape(CH, 2 * HD)
    span = span_kv.reshape(TOK, 2 * HD)
    return fused(lengths, queries, cache, span, cosine, sine, out_weight)


def solution(mesh):
    return jax.shard_map(
        body,
        mesh=mesh,
        in_specs=(
            P("ctx", "tp"),
            P("ctx", "tp", None, None),
            P("ctx", "tp", None, None),
            P("tp", "ctx"),
            P(),
            P(),
        ),
        out_specs=P("tp", "ctx"),
        check_vma=False,
    )
```

```python
import math

import jax
import jax.numpy as jnp
from jax import lax
from jax.experimental import pallas as pl
from jax.experimental.pallas import tpu as pltpu
from jax.sharding import PartitionSpec as P

SLOT = 256
HD = 128
TOK = 128
HEADS = 8
KV_ROWS = 640
CH = 512
A_ROWS = 256
ROWS = HEADS * TOK
BLK = 512
COLS = 256
HALF = TOK // 2
WP = 128
COPIES = 72
lowest_score = -1e30
rope_base = 500000.0
MESH = pl.DeviceIdType.MESH
SCALE2 = math.log2(math.e) / math.sqrt(HD)


def rotary_tables(positions):
    half = HD // 2
    frequency = jnp.exp(
        jnp.arange(half, dtype=jnp.float32) * (-2.0 * math.log(rope_base) / HD)
    )
    angles = positions.astype(jnp.float32)[:, None] * frequency[None, :]
    cosine, sine = jnp.cos(angles), jnp.sin(angles)
    return jnp.concatenate([cosine, cosine], axis=1), jnp.concatenate([-sine, sine], axis=1)


def coords():
    c = lax.axis_index("ctx")
    z = c // 16
    x = (c // 4) % 4
    y = c % 4
    return z, x, y


def ctx_of(z, x, y):
    return z * 16 + x * 4 + y


def entry_barrier(devices):
    barrier = pltpu.get_barrier_semaphore()
    for d in devices:
        pl.semaphore_signal(barrier, inc=1, device_id=d, device_id_type=MESH)
    pl.semaphore_wait(barrier, len(devices))


def fold(op, values):
    out = values[:, 0:HD]
    for n in range(1, values.shape[1] // HD):
        out = op(out, values[:, n * HD : (n + 1) * HD])
    return out


def wide(values):
    return jnp.concatenate([values] * (CH // HD), axis=1)


def fused_kernel(
    lens_ref,
    q_ref,
    cache_ref,
    span_ref,
    cos_ref,
    sin_ref,
    w_hbm,
    out_ref,
    w_ref,
    qh,
    kvg,
    bias,
    sbuf,
    mx,
    top,
    den,
    acc,
    o4,
    st,
    part,
    stat,
    table,
    fwd,
    away,
    wz,
    wh,
    wzh,
    att,
    prod,
    give,
    got,
    keep,
    box,
    ssem,
    rsem,
    w_s,
    w_r,
    w_local,
    near,
    core_s,
    core_r,
    z_s,
    z_r,
):
    z, x, y = coords()
    tp = lax.axis_index("tp")
    core = tp % 2
    high = tp // 2
    even = high % 2
    zo = 1 - z
    other = {"tp": tp + 1 - 2 * core}
    pair = {"tp": tp + 2 - 4 * even}
    pos = 2 * high + z
    column = []
    for d in range(1, 8):
        q = (pos + d) % 8
        column.append({"ctx": ctx_of(q % 2, x, y), "tp": (q // 2) * 2 + core})
    xp, xm, x2 = (x + 1) % 4, (x + 3) % 4, (x + 2) % 4
    yp, ym, y2 = (y + 1) % 4, (y + 3) % 4, (y + 2) % 4
    dz = {"ctx": ctx_of(zo, x, y)}
    dxp = {"ctx": ctx_of(z, xp, y)}
    dxm = {"ctx": ctx_of(z, xm, y)}
    dyp = {"ctx": ctx_of(z, x, yp)}
    dym = {"ctx": ctx_of(z, x, ym)}
    dy2 = {"ctx": ctx_of(z, x, y2)}

    table_of = {}

    def view(place):
        if isinstance(place, tuple):
            return place[0].at[place[1:]]
        return place

    def copy(name, src, dst, device):
        n = table_of.setdefault(name, len(table_of))
        return pltpu.make_async_remote_copy(
            src_ref=view(src),
            dst_ref=view(dst),
            send_sem=ssem.at[n],
            recv_sem=rsem.at[n],
            device_id=device,
            device_id_type=MESH,
        )

    makers = {}

    def start(name, src, dst, device):
        def make():
            return copy(name, src, dst, device)

        makers[name] = make
        make().start()

    def wait(*names):
        for name in names:
            makers[name]().wait_recv()

    own = z * 4 + x
    a = pl.ds(0, A_ROWS)
    a0 = pl.ds(0, A_ROWS // 2)
    a1 = pl.ds(A_ROWS // 2, A_ROWS // 2)
    nb = KV_ROWS - A_ROWS
    b = pl.ds(A_ROWS, nb)
    b0 = pl.ds(A_ROWS, nb // 2)
    b1 = pl.ds(A_ROWS + nb // 2, nb // 2)
    h0 = pl.ds(0, ROWS // 2)
    h1 = pl.ds(ROWS // 2, ROWS // 2)

    next_z, last_z = column[0], column[6]
    entry_barrier([dxp, dxm, dyp, dym, other, next_z, last_z])

    def near_signal(r):
        for device in (next_z, last_z):
            pl.semaphore_signal(near.at[r], inc=1, device_id=device, device_id_type=MESH)

    def near_wait(r):
        pl.semaphore_wait(near.at[r], 2)

    near_signal(0)

    def kv_send(name, j, rows, device):
        start(name, (kvg, j, rows), (kvg, j, rows), device)

    def rotated(values):
        values = values.astype(jnp.float32)
        turned = jnp.concatenate([values[:, HD // 2 :], values[:, : HD // 2]], axis=1)
        return (values * cos_ref[...] + turned * sin_ref[...]).astype(jnp.bfloat16)

    def kv_own(name, rows, device):
        kv_send(name, own, rows, device)

    kvg[own, 0:CH] = cache_ref[...]
    kvg[own, CH:KV_ROWS, 0:HD] = rotated(span_ref[:, 0:HD])
    kvg[own, CH:KV_ROWS, HD : 2 * HD] = span_ref[:, HD : 2 * HD]
    kv_own("b_z", b, dz)
    kv_own("b_xp", b, dxp)
    kv_own("b_xm", b, dxm)
    for h in range(HEADS):
        qh[y, h * TOK : (h + 1) * TOK, :] = rotated(q_ref[:, h * HD : (h + 1) * HD])
    start("q_yp", (qh, y), (qh, y), dyp)
    start("q_ym", (qh, y), (qh, y), dym)
    kv_own("a_xp", a, dxp)
    kv_own("a_xm", a, dxm)
    kv_own("a_z", a, dz)
    weights_here = pltpu.make_async_copy(w_hbm, w_ref, w_local)
    weights_here.start()

    lane = lax.broadcasted_iota(jnp.int32, (1, SLOT), 1)
    for j in range(8):
        for s in range(2):
            n = lens_ref[2 * (4 * j + y) + s]
            bias[j : j + 1, s * SLOT : (s + 1) * SLOT] = jnp.where(lane < n, 0.0, lowest_score)
    top[...] = jnp.full(top.shape, lowest_score, jnp.float32)
    den[...] = jnp.zeros_like(den)
    acc[...] = jnp.zeros_like(acc)

    def first(i, j, slot):
        s = lax.dot_general(
            qh[i],
            kvg[j, 0:CH, 0:HD],
            (((1,), (1,)), ((), ())),
            preferred_element_type=jnp.float32,
        )
        s = s + bias[pl.ds(j, 1), :]
        sbuf[slot] = s
        mx[slot] = fold(jnp.maximum, s)

    def span_part(g, lanes):
        return jnp.concatenate([kvg[4 * g + k, CH:KV_ROWS, lanes] for k in range(4)], axis=0)

    def first_span(i, g, slot):
        s = lax.dot_general(
            qh[i],
            span_part(g, slice(0, HD)),
            (((1,), (1,)), ((), ())),
            preferred_element_type=jnp.float32,
        )
        parts = []
        row = lax.broadcasted_iota(jnp.int32, (TOK, TOK), 0)
        col = lax.broadcasted_iota(jnp.int32, (TOK, TOK), 1)
        for k in range(4):
            ahead = (4 * (4 * g + k) + y - 4 * own - i) * TOK
            parts.append(jnp.where(col + ahead <= row, 0.0, lowest_score))
        mask = jnp.concatenate(parts, axis=1)
        s = s + jnp.concatenate([mask] * HEADS, axis=0)
        sbuf[slot] = s
        mx[slot] = fold(jnp.maximum, s)

    def fold_in(i, slot, values):
        old = top[i]
        peak = jnp.max(mx[slot], axis=1, keepdims=True) * SCALE2
        new = jnp.maximum(old, jnp.broadcast_to(peak, (ROWS, HD)))
        factor = jnp.exp2(old - new)
        top[i] = new
        p = jnp.exp2(sbuf[slot] * SCALE2 - wide(new)).astype(jnp.bfloat16)
        both = jnp.dot(
            p,
            jnp.concatenate([values, jnp.ones_like(values)], axis=1),
            preferred_element_type=jnp.float32,
        )
        acc[i] = acc[i] * factor + both[:, 0:HD]
        den[i] = den[i] * factor + both[:, HD : 2 * HD]

    def second(i, j, slot):
        fold_in(i, slot, kvg[j, 0:CH, HD : 2 * HD])

    def second_span(i, g, slot):
        fold_in(i, slot, span_part(g, slice(HD, 2 * HD)))

    first(y, own, 0)

    oz = zo * 4 + x
    own2, far_m, far_p, far_2 = z * 4 + x2, zo * 4 + xm, zo * 4 + xp, zo * 4 + x2
    own_m, own_p = z * 4 + xm, z * 4 + xp
    def early(k):
        step = k % 3
        return (z + k // 3) % 2 * 4 + (x + step + step // 2) % 4

    def tile(d):
        return (y + d) % 4

    def early_tile(n):
        k = n % 4
        return tile(k + k // 2 - 2 * (k // 3))

    def piece(kind, c):
        src, dst, device = ((w_hbm, wh, pair), (w_hbm, wz, dz), (wh, wzh, dz))[kind]
        rows = pl.ds(pl.multiple_of(c * WP, WP), WP)
        return pltpu.make_async_remote_copy(
            src_ref=src.at[rows],
            dst_ref=dst.at[rows],
            send_sem=w_s.at[kind, c],
            recv_sem=w_r.at[kind, c],
            device_id=device,
            device_id_type=MESH,
        )

    def pass_first():
        wait("b_z", "b_xp", "b_xm", "a_xp", "a_xm", "a_z")
        kv_send("bz_xp", oz, b, dxp)
        kv_send("bz_xm", oz, b, dxm)
        kv_send("az_m", own_m, a, dz)
        kv_send("az_p", own_p, a, dz)
        kv_send("bf_xp", own_m, b0, dxp)
        kv_send("bf_xm", own_p, b1, dxm)
        kv_send("af_xp", own_m, a0, dxp)
        kv_send("af_xm", own_p, a1, dxm)
        wait("qf_yp", "qf_ym")

    def round_one():
        near_wait(0)
        near_signal(1)

    def round_two():
        near_wait(1)
        near_signal(2)

    def pass_b():
        wait("bz_xp")
        kv_send("bzf_xp", far_m, b0, dxp)
        wait("bz_xm")
        kv_send("bzf_xm", far_p, b1, dxm)

    def pass_a():
        wait("af_xp")
        kv_send("az_2a", own2, a0, dz)
        wait("af_xm")
        kv_send("az_2b", own2, a1, dz)

    oz = zo * 4 + x
    own2, far_m, far_p, far_2 = z * 4 + x2, zo * 4 + xm, zo * 4 + xp, zo * 4 + x2
    own_m, own_p = z * 4 + xm, z * 4 + xp
    wait("q_yp")
    start("qf_yp", (qh, ym, h0), (qh, ym, h0), dyp)
    wait("q_ym")
    start("qf_ym", (qh, yp, h1), (qh, yp, h1), dym)
    points = {
        1: pass_first,
        2: round_one,
        4: round_two,
        5: pass_b,
        6: pass_a,
    }

    @pl.loop(0, 7)
    def _(step):
        for at, action in points.items():
            pl.when(step == at)(action)
        for u in range(2):
            n = 2 * step + u
            first(early_tile(n + 1), early((n + 1) // 4), 1 - u)
            second(early_tile(n), early(n // 4), u)

    late = (own2, far_p, far_m, far_2)
    first(tile(2), early(3), 1)
    second(tile(3), early(3), 0)
    wait("bf_xp", "bf_xm", "az_m", "az_p")
    first(tile(1), late[0], 0)
    second(tile(2), early(3), 1)

    def wait_last():
        wait("bzf_xp", "bzf_xm", "az_2a", "az_2b")
        near_wait(2)

    def send_piece(t, k):
        n = 6 * t + k
        c = n % 8

        @pl.when(n // 8 == 0)
        def _():
            piece(0, c).start()

        @pl.when(n // 8 == 1)
        def _():
            piece(1, c).start()

        @pl.when(n // 8 == 2)
        def _():
            piece(0, c).wait_recv()
            piece(2, c).start()

    lane_t = lax.broadcasted_iota(jnp.int32, (TOK, HD), 1)
    t0 = pl.ds(0, HALF)
    t1 = pl.ds(HALF, HALF)

    def send_yp():
        start("to_p", (o4, 0), (part, 2), dyp)
        start("st_p", (st, 0), (stat, 2), dyp)

    def send_far():
        start("far_p", (o4, 1, t0), (fwd, 0), dyp)
        start("far_m", (o4, 1, t1), (fwd, 1), dym)
        start("st_2", (st, 1), (stat, 1), dy2)

    def send_ym():
        start("to_m", (o4, 2), (part, 0), dym)
        start("st_m", (st, 2), (stat, 0), dym)
        wait("far_p")
        start("fw_p", (fwd, 0), (part, 1, t0), dyp)
        wait("far_m")
        start("fw_m", (fwd, 1), (part, 1, t1), dym)

    @pl.loop(0, 4)
    def _(t):
        i = tile(t + 1)
        for k in range(3):
            send_piece(t, k)
            if k == 2:
                pl.when(t == 0)(wait_last)
            first(i, late[k + 1], (k + 1) % 2)
            second(i, late[k], k % 2)
        send_piece(t, 3)
        first_span(i, 0, 0)
        second(i, late[3], 1)
        send_piece(t, 4)
        first_span(i, 1, 1)
        second_span(i, 0, 0)
        send_piece(t, 5)
        first(tile(t + 2), late[0], 0)
        second_span(i, 1, 1)
        total = den[i]
        o = acc[i] / total
        lse = top[i] + jnp.log2(total)
        packed = jnp.zeros((TOK, HD), jnp.float32)
        for h in range(HEADS):
            rows = slice(h * TOK, (h + 1) * TOK)
            o4[t, :, h * HD : (h + 1) * HD] = o[rows].astype(jnp.bfloat16)
            packed = jnp.where(lane_t == h, lse[rows], packed)
        st[t] = packed.T[0:HEADS]
        pl.when(t == 0)(send_yp)
        pl.when(t == 1)(send_far)
        pl.when(t == 2)(send_ym)

    wait("st_p", "st_m", "st_2")
    s_own = st[3]
    s_p, s_m, s_2 = stat[0], stat[2], stat[1]
    best = jnp.maximum(jnp.maximum(s_own, s_p), jnp.maximum(s_m, s_2))
    e_own = jnp.exp2(s_own - best)
    e_p = jnp.exp2(s_p - best)
    e_m = jnp.exp2(s_m - best)
    e_2 = jnp.exp2(s_2 - best)
    norm = 1.0 / (e_own + e_p + e_m + e_2)
    table[...] = jnp.concatenate(
        [e_own * norm, e_p * norm, e_m * norm, e_2 * norm, jnp.zeros((96, TOK), jnp.float32)],
        axis=0,
    ).T
    wait("to_p", "to_m", "fw_p", "fw_m")
    slot_own = x * 4 + y

    def combined(begin, dest):
        rows = pl.ds(pl.multiple_of(begin, HALF), HALF)
        for h in range(HEADS):
            lanes = slice(h * HD, (h + 1) * HD)
            out = o4[3, rows, lanes].astype(jnp.float32) * table[rows, h : h + 1]
            out += part[0, rows, lanes].astype(jnp.float32) * table[rows, 8 + h : 9 + h]
            out += part[2, rows, lanes].astype(jnp.float32) * table[rows, 16 + h : 17 + h]
            out += part[1, rows, lanes].astype(jnp.float32) * table[rows, 24 + h : 25 + h]
            dest[:, lanes] = out.astype(jnp.bfloat16)

    combined(even * HALF, att.at[0, slot_own])
    lo, hi, full = pl.ds(0, HALF // 2), pl.ds(HALF // 2, HALF // 2), pl.ds(0, HALF)

    def send(name, k, slot, rows, device):
        start(name, (att, k, slot, rows), (att, k, slot, rows), device)

    def both_y(r, xs):
        send("ayp%d" % r, 0, xs * 4 + y, full, dyp)
        send("aym%d" % r, 0, xs * 4 + y, full, dym)

    def both_x(r, ys):
        send("bxp%d" % r, 1, x * 4 + ys, full, dxp)
        send("bxm%d" % r, 1, x * 4 + ys, full, dxm)

    send("axp", 0, slot_own, full, dxp)
    send("axm", 0, slot_own, full, dxm)
    both_y(0, x)
    combined((1 - even) * HALF, away)
    start("swap", away, (att, 1, slot_own), pair)
    wait("axp")
    send("axfp", 0, xm * 4 + y, lo, dxp)
    both_y(3, xm)
    wait("axm")
    send("axfm", 0, xp * 4 + y, hi, dxm)
    both_y(1, xp)
    wait("swap")
    send("byp", 1, slot_own, full, dyp)
    send("bym", 1, slot_own, full, dym)
    both_x(0, y)

    def relay_a(r):
        xs = (x + r) % 4
        wait("ayp%d" % r)
        send("lap%d" % r, 0, xs * 4 + ym, lo, dyp)
        wait("aym%d" % r)
        send("lam%d" % r, 0, xs * 4 + yp, hi, dym)

    def relay_b(r):
        ys = (y + r) % 4
        wait("bxp%d" % r)
        send("lbp%d" % r, 1, xm * 4 + ys, lo, dxp)
        wait("bxm%d" % r)
        send("lbm%d" % r, 1, xp * 4 + ys, hi, dxm)

    def core_copy(n):
        return pltpu.make_async_remote_copy(
            src_ref=give.at[n],
            dst_ref=got.at[n],
            send_sem=core_s.at[n],
            recv_sem=core_r.at[n],
            device_id=other,
            device_id_type=MESH,
        )

    def z_copy(row, n, far):
        return pltpu.make_async_remote_copy(
            src_ref=keep.at[n, far],
            dst_ref=box.at[high],
            send_sem=z_s.at[2 * n + far],
            recv_sem=z_r.at[high],
            device_id={
                "ctx": ctx_of(zo if far else z, x, y),
                "tp": (2 * z + row // 2) * 2 + core,
            },
            device_id_type=MESH,
        )

    def half_product(row, n, far):
        wa, wb = (wz, wzh) if far else (w_ref, wh)
        slots = pl.ds(4 * row, 4)
        rows_a = att[0, slots].reshape(BLK // 2, HEADS * HD)
        rows_b = att[1, slots].reshape(BLK // 2, HEADS * HD)
        prod[n % 2, far] = jnp.dot(rows_a, wa[...], preferred_element_type=jnp.float32) + jnp.dot(
            rows_b, wb[...], preferred_element_type=jnp.float32
        )

    def hand_over(row, n):
        keeps = row % 2 == core

        @pl.when(jnp.logical_not(keeps))
        def _():
            give[n] = prod[n % 2].astype(jnp.bfloat16)
            core_copy(n).start()

    def product(row, n):
        half_product(row, n, 0)
        half_product(row, n, 1)
        hand_over(row, n)

    def settle(row, n):
        keeps = row % 2 == core
        remote = 2 * z + row // 2 != high

        @pl.when(keeps)
        def _():
            core_copy(n).wait_recv()
            keep[n] = (prod[n % 2] + got[n].astype(jnp.float32)).astype(jnp.bfloat16)
            z_copy(row, n, 1).start()

            @pl.when(remote)
            def _():
                z_copy(row, n, 0).start()

            @pl.when(jnp.logical_not(remote))
            def _():
                box[high] = keep[n, 0]

    relay_a(0)
    wait("byp")
    send("byfp", 1, x * 4 + ym, lo, dyp)
    both_x(3, ym)
    wait("bym")
    send("byfm", 1, x * 4 + yp, hi, dym)
    both_x(1, yp)
    wait("axfp", "axfm")
    both_y(2, x2)
    relay_a(3)
    relay_b(0)
    wait("byfp", "byfm")
    both_x(2, y2)
    wait("lap0", "lam0")
    weights_here.wait()
    half_product(x, 0, 0)
    for c in range(8):
        piece(1, c).wait_recv()
        piece(2, c).wait_recv()
    half_product(x, 0, 1)
    hand_over(x, 0)
    relay_a(1)
    settle(x, 0)
    relay_b(3)
    relay_b(1)
    relay_a(2)
    relay_b(2)
    wait("lap3", "lam3")
    product(xm, 1)
    settle(xm, 1)
    wait("lap1", "lam1")
    product(xp, 2)
    settle(xp, 2)
    wait("lap2", "lam2")
    for r in range(4):
        wait("lbp%d" % r, "lbm%d" % r)
    product(x2, 3)
    settle(x2, 3)

    source_z = high // 2
    for s in range(4):
        arrives = jnp.logical_or(high != s, z != source_z)

        @pl.when(arrives)
        def _(s=s):
            pltpu.make_async_remote_copy(
                src_ref=keep.at[0, 0],
                dst_ref=box.at[s],
                send_sem=z_s.at[0],
                recv_sem=z_r.at[s],
                device_id=other,
                device_id_type=MESH,
            ).wait_recv()

    for e in range(2):
        total = box[e].astype(jnp.float32) + box[2 + e].astype(jnp.float32)
        total = total.astype(jnp.bfloat16)
        for g in range(4):
            begin = g * TOK + e * HALF
            out_ref[begin : begin + HALF] = total[g * HALF : (g + 1) * HALF]
    for n, row in enumerate((x, xm, xp, x2)):
        keeps = row % 2 == core
        remote = 2 * z + row // 2 != high

        @pl.when(keeps)
        def _(n=n, row=row, remote=remote):
            z_copy(row, n, 1).wait_send()

            @pl.when(remote)
            def _():
                z_copy(row, n, 0).wait_send()

        @pl.when(jnp.logical_not(keeps))
        def _(n=n):
            core_copy(n).wait_send()

    for make in makers.values():
        make().wait_send()
    for kind in range(3):
        for c in range(8):
            piece(kind, c).wait_send()


def fused(lengths, q, cache, span, cosine, sine, w):
    bf16, f32 = jnp.bfloat16, jnp.float32
    return pl.pallas_call(
        fused_kernel,
        name="attention_block",
        out_shape=jax.ShapeDtypeStruct((BLK, COLS), bf16),
        in_specs=[pl.BlockSpec(memory_space=pltpu.SMEM)]
        + [pl.BlockSpec(memory_space=pltpu.VMEM)] * 5
        + [pl.BlockSpec(memory_space=pltpu.HBM)],
        out_specs=pl.BlockSpec(memory_space=pltpu.VMEM),
        scratch_shapes=[
            pltpu.VMEM((HEADS * HD, COLS), bf16),
            pltpu.VMEM((4, ROWS, HD), bf16),
            pltpu.VMEM((8, KV_ROWS, 2 * HD), bf16),
            pltpu.VMEM((8, CH), f32),
            pltpu.VMEM((2, ROWS, CH), f32),
            pltpu.VMEM((2, ROWS, HD), f32),
            pltpu.VMEM((4, ROWS, HD), f32),
            pltpu.VMEM((4, ROWS, HD), f32),
            pltpu.VMEM((4, ROWS, HD), f32),
            pltpu.VMEM((4, TOK, HEADS * HD), bf16),
            pltpu.VMEM((4, HEADS, TOK), f32),
            pltpu.VMEM((3, TOK, HEADS * HD), bf16),
            pltpu.VMEM((3, HEADS, TOK), f32),
            pltpu.VMEM((TOK, TOK), f32),
            pltpu.VMEM((2, HALF, HEADS * HD), bf16),
            pltpu.VMEM((HALF, HEADS * HD), bf16),
            pltpu.VMEM((HEADS * HD, COLS), bf16),
            pltpu.VMEM((HEADS * HD, COLS), bf16),
            pltpu.VMEM((HEADS * HD, COLS), bf16),
            pltpu.VMEM((2, 16, HALF, HEADS * HD), bf16),
            pltpu.VMEM((2, 2, BLK // 2, COLS), f32),
            pltpu.VMEM((4, 2, BLK // 2, COLS), bf16),
            pltpu.VMEM((4, 2, BLK // 2, COLS), bf16),
            pltpu.VMEM((4, 2, BLK // 2, COLS), bf16),
            pltpu.VMEM((4, BLK // 2, COLS), bf16),
            pltpu.SemaphoreType.DMA((COPIES,)),
            pltpu.SemaphoreType.DMA((COPIES,)),
            pltpu.SemaphoreType.DMA((3, 8)),
            pltpu.SemaphoreType.DMA((3, 8)),
            pltpu.SemaphoreType.DMA,
            pltpu.SemaphoreType.REGULAR((3,)),
            pltpu.SemaphoreType.DMA((4,)),
            pltpu.SemaphoreType.DMA((4,)),
            pltpu.SemaphoreType.DMA((8,)),
            pltpu.SemaphoreType.DMA((4,)),
        ],
        compiler_params=pltpu.CompilerParams(
            collective_id=0, has_side_effects=True, vmem_limit_bytes=48 << 20
        ),
    )(lengths, q, cache, span, cosine, sine, w)


def body(queries, span_kv, cache_kv, out_weight, offset, lengths):
    first_token = lax.axis_index("ctx") * TOK
    positions = offset[0] + first_token + jnp.arange(TOK, dtype=jnp.int32)
    cosine, sine = rotary_tables(positions)
    cache = cache_kv.reshape(CH, 2 * HD)
    span = span_kv.reshape(TOK, 2 * HD)
    return fused(lengths, queries, cache, span, cosine, sine, out_weight)


def solution(mesh):
    return jax.shard_map(
        body,
        mesh=mesh,
        in_specs=(
            P("ctx", "tp"),
            P("ctx", "tp", None, None),
            P("ctx", "tp", None, None),
            P("tp", "ctx"),
            P(),
            P(),
        ),
        out_specs=P("tp", "ctx"),
        check_vma=False,
    )
```
